512 devices in a mesh: dom: 64 (over z_hi, x, y, core), lag: 8 (over z_lo).
Axes of the slice: x: 4, y: 4, z: 16 (z_hi: 2, z_lo: 8; z = z_hi * 8 + z_lo), core: 2. Of those that a mesh axis runs over, the one named last changes fastest.
Arguments:
- delayed_crowd_history: bfloat16 [8, 64, 2048, 128], P('lag', None, 'dom'), may hold values from -6 to 6
- predicted_crowd_array: bfloat16 [64, 2048, 128], P('lag', 'dom'), may hold values from -40 to 40
- probe_target_spot: int32 [1024, 256], P('dom'), may hold values from 0 to 255
- alive_probe_places: int32 [1024], P('dom'), may hold values from 64 to 256, as said below
- probed_heat_levels: float32 [1024, 256], P('dom'), may hold values from -6 to 6
- probe_reciprocal_spread: float32 [1024, 256], P('dom'), may hold values from 0.1 to 1.6
- decay_extent_squares: int32 [1024], P('dom'), may hold values from 16 to 32
Outputs:
- smoothed: bfloat16 [8, 64, 2048, 128], P('lag', None, 'dom')
The draws below stay inside these ranges and needn't reach their ends.
Inputs may be any that keep to these rules, and one draw needn't show every extreme that they name: `alive_probe_places`: live observations of a patch occupy its first slots.
All inputs are finite; a program needn't handle non-finite values.
Results may differ from the reference program's by a relative error of at most 0.0062.
Values may be sent and summed in bfloat16 or wider, within the bound.
A program may use at most 64 MiB of HBM per device.

```python
import math
import jax
import jax.numpy as jnp
from jax import lax

MEM = 64
PATCH = 16
COLS = 128
SENSOR_LIMIT = 256
RADIUS = 32
NS_STEPS = 4
REACH = 2
NROWS = 2048
SUBDOMAINS = 1024
LAGS = 8


def draw_predicted_crowd_array(key, part):
    key_member, key_cell, key_base, key_noise = jax.random.split(jax.random.fold_in(key, 11), 4)
    log_low = math.log(0.4)
    log_high = math.log(3.0)
    member_scale = jnp.exp(jax.random.uniform(key_member, (MEM, 1, 1), jnp.float32, log_low, log_high))
    cell_scale = jnp.exp(jax.random.uniform(key_cell, (1, NROWS, COLS), jnp.float32, math.log(0.5), math.log(2.0)))
    background = jax.random.normal(key_base, (1, NROWS, COLS), jnp.float32)
    noise_field = jax.random.normal(key_noise, (MEM, NROWS, COLS), jnp.float32)
    values = jnp.clip(background + member_scale * cell_scale * noise_field, -40.0, 40.0)
    return values.astype(jnp.bfloat16)


def draw_alive_probe_places(key, part):
    key_count, key_place = jax.random.split(jax.random.fold_in(key, 23))
    counts = jax.random.randint(key_count, (SUBDOMAINS,), SENSOR_LIMIT // 4, SENSOR_LIMIT + 1, jnp.int32)
    chosen = jax.random.permutation(key_place, SUBDOMAINS)
    counts = counts.at[chosen[0]].set(SENSOR_LIMIT)
    return counts.at[chosen[1]].set(SENSOR_LIMIT // 4)


def draw_decay_extent_squares(key, part):
    key_value, key_place = jax.random.split(jax.random.fold_in(key, 37))
    radii = jax.random.randint(key_value, (SUBDOMAINS,), RADIUS // 2, RADIUS + 1, jnp.int32)
    chosen = jax.random.permutation(key_place, SUBDOMAINS)
    radii = radii.at[chosen[0]].set(RADIUS)
    return radii.at[chosen[1]].set(RADIUS // 2)


def place_ends(drawn, rng, least, largest):
    longest = drawn.shape.index(max(drawn.shape))
    spots = []
    for shift in (0, 1):
        where = [jax.random.randint(jax.random.fold_in(rng, axis), (), 0, length) for axis, length in enumerate(drawn.shape)]
        where[longest] = (where[longest] + shift) % drawn.shape[longest]
        spots.append(tuple(where))
    return drawn.at[spots[0]].set(least).at[spots[1]].set(largest)


def block_levels(own_key, shape, cuts, least, top_value):
    def one(position, blocks):
        heights = jax.random.uniform(jax.random.fold_in(jax.random.fold_in(own_key, 6), position), (blocks,), jnp.float32, least / len(cuts), top_value / len(cuts))
        return jnp.repeat(jnp.exp(heights), shape[position] // blocks).reshape((-1,) + (1,) * (len(shape) - position - 1))

    gain = one(*cuts[0])
    for cut in cuts[1:]:
        gain = gain * one(*cut)
    return gain


def noise(own_key, shape, width, limit, cuts=(), kind=jnp.bfloat16):
    level = block_levels(own_key, shape, cuts, -0.22, 0.18) if cuts else 1.0
    drawn = jax.random.normal(own_key, shape, jnp.float32) * width * level
    return jnp.minimum(jnp.maximum(drawn, -limit), limit).astype(kind)


def setup_inputs(seed: int = 0) -> dict:
    arg_keys = jax.random.split(jax.random.key(seed), 8)
    return {
        "delayed_crowd_history": noise(arg_keys[0], (LAGS, MEM, NROWS, COLS), 1.0, 6.0, ((0, 8), (2, 64))),
        "predicted_crowd_array": draw_predicted_crowd_array(jax.random.fold_in(arg_keys[7], 71), 0),
        "probe_target_spot": place_ends(jax.random.randint(arg_keys[2], (SUBDOMAINS, SENSOR_LIMIT), 0, PATCH * PATCH), jax.random.fold_in(arg_keys[2], 1), 0, (PATCH * PATCH) - 1).astype(jnp.int32),
        "alive_probe_places": draw_alive_probe_places(jax.random.fold_in(arg_keys[7], 71), 0),
        "probed_heat_levels": noise(arg_keys[4], (SUBDOMAINS, SENSOR_LIMIT), 1.0, 6.0, ((0, 64),), jnp.float32),
        "probe_reciprocal_spread": jnp.clip(jnp.exp(math.log(1.6) - 2.7725887 * jax.random.uniform(arg_keys[5], (SUBDOMAINS, SENSOR_LIMIT), jnp.float32) ** block_levels(arg_keys[5], (SUBDOMAINS, SENSOR_LIMIT), ((0, 64),), -0.2, 0.2)), 0.1, 1.6),
        "decay_extent_squares": draw_decay_extent_squares(jax.random.fold_in(arg_keys[7], 71), 0),
    }


def inverse_root(gram_part, right_side):
    crowd_members_number = gram_part.shape[-1]
    identity = jnp.eye(crowd_members_number, dtype=jnp.float32)
    frobenius = jnp.sqrt(lax.optimization_barrier(jnp.sum(gram_part * gram_part, axis=(1, 2))))
    bound_value = crowd_members_number - 1.0 + frobenius
    iterate = (gram_part + (crowd_members_number - 1.0) * identity) / bound_value[:, None, None]
    root_iter = jnp.broadcast_to(identity, gram_part.shape)
    for sweep_index in range(NS_STEPS):
        correction = 1.5 * identity - 0.5 * jnp.matmul(root_iter, iterate, precision=lax.Precision.HIGHEST)
        iterate = jnp.matmul(iterate, correction, precision=lax.Precision.HIGHEST)
        root_iter = jnp.matmul(correction, root_iter, precision=lax.Precision.HIGHEST)
    inner_prod = jnp.matmul(root_iter, right_side[:, :, None], precision=lax.Precision.HIGHEST)
    mean_weights = jnp.matmul(root_iter, inner_prod, precision=lax.Precision.HIGHEST)[:, :, 0] / bound_value[:, None]
    spread = jnp.sqrt(crowd_members_number - 1.0) / jnp.sqrt(bound_value)
    return (spread[:, None, None] * root_iter + mean_weights[:, :, None]).astype(jnp.bfloat16)

def reference(delayed_crowd_history, predicted_crowd_array, probe_target_spot, alive_probe_places, probed_heat_levels, probe_reciprocal_spread, decay_extent_squares):
    crowd_members_number, tile_vertical_extent, tile_lateral_extent = predicted_crowd_array.shape
    patch_rows = tile_vertical_extent // PATCH
    patch_cols = tile_lateral_extent // PATCH
    patch_total = patch_rows * patch_cols
    slot_count = probe_target_spot.shape[1]
    index_patch = jnp.arange(patch_total, dtype=jnp.int32)
    row_in = probe_target_spot // PATCH
    col_in = probe_target_spot % PATCH
    lattice_node_place = (((index_patch // patch_cols)[:, None] * PATCH + row_in) * tile_lateral_extent + (index_patch % patch_cols)[:, None] * PATCH + col_in).astype(jnp.int32)
    probed_markers = jnp.take(predicted_crowd_array.reshape(crowd_members_number, tile_vertical_extent * tile_lateral_extent), lattice_node_place.reshape(-1), axis=1)
    probed_markers = probed_markers.reshape(crowd_members_number, patch_total, slot_count)
    average_reading = lax.optimization_barrier(jnp.sum(probed_markers, axis=0, dtype=jnp.float32)) / crowd_members_number
    obs_anomaly = lax.optimization_barrier((probed_markers.astype(jnp.float32) - average_reading).astype(jnp.bfloat16))
    usable_entry = jnp.arange(slot_count, dtype=jnp.int32)[None, :] < alive_probe_places[:, None]
    obs_weight = lax.optimization_barrier(jnp.where(usable_entry, probe_reciprocal_spread, 0.0).astype(jnp.bfloat16))
    departure_vector = lax.optimization_barrier(jnp.where(usable_entry, probe_reciprocal_spread * (probed_heat_levels - average_reading), 0.0).astype(jnp.bfloat16))
    pad_plan = ((REACH, REACH), (REACH, REACH), (0, 0))
    anomaly_pad = jnp.pad(obs_anomaly.reshape(crowd_members_number, patch_rows, patch_cols, slot_count), ((0, 0),) + pad_plan)
    weight_pad = jnp.pad(obs_weight.reshape(patch_rows, patch_cols, slot_count), pad_plan)
    innov_pad = jnp.pad(departure_vector.reshape(patch_rows, patch_cols, slot_count), pad_plan)
    rowin_pad = jnp.pad(row_in.reshape(patch_rows, patch_cols, slot_count).astype(jnp.float32), pad_plan)
    colin_pad = jnp.pad(col_in.reshape(patch_rows, patch_cols, slot_count).astype(jnp.float32), pad_plan)
    radius = decay_extent_squares.reshape(patch_rows, patch_cols, 1).astype(jnp.float32)
    gram_sum = jnp.zeros((patch_rows, patch_cols, crowd_members_number, crowd_members_number), jnp.float32)
    right_side = jnp.zeros((patch_rows, patch_cols, crowd_members_number), jnp.float32)
    reach_width = 2 * REACH + 1
    for shift_row in range(reach_width):
        for shift_col in range(reach_width):
            anomaly_near = anomaly_pad[:, shift_row:shift_row + patch_rows, shift_col:shift_col + patch_cols, :]
            weight_near = weight_pad[shift_row:shift_row + patch_rows, shift_col:shift_col + patch_cols, :]
            innov_near = innov_pad[shift_row:shift_row + patch_rows, shift_col:shift_col + patch_cols, :]
            rowin_near = rowin_pad[shift_row:shift_row + patch_rows, shift_col:shift_col + patch_cols, :]
            colin_near = colin_pad[shift_row:shift_row + patch_rows, shift_col:shift_col + patch_cols, :]
            row_offset = (shift_row - REACH) * PATCH + rowin_near - 7.5
            col_offset = (shift_col - REACH) * PATCH + colin_near - 7.5
            taper_weight = jnp.square(jnp.maximum(0.0, 1.0 - (jnp.square(row_offset) + jnp.square(col_offset)) / jnp.square(radius)))
            scaled = lax.optimization_barrier((taper_weight * weight_near.astype(jnp.float32) * anomaly_near.astype(jnp.float32)).astype(jnp.bfloat16))
            weighted = lax.optimization_barrier((taper_weight * innov_near.astype(jnp.float32)).astype(jnp.bfloat16))
            gram_sum = gram_sum + jnp.einsum('mxyo,nxyo->xymn', scaled.astype(jnp.float32), anomaly_near.astype(jnp.float32))
            right_side = right_side + jnp.einsum('mxyo,xyo->xym', anomaly_near.astype(jnp.float32), weighted.astype(jnp.float32))
    transform = inverse_root(gram_sum.reshape(patch_total, crowd_members_number, crowd_members_number), right_side.reshape(patch_total, crowd_members_number))
    transform = lax.optimization_barrier(transform)
    mixing = transform.reshape(patch_rows, patch_cols, crowd_members_number, crowd_members_number).astype(jnp.float32)

    def smooth(lag_state):
        lag_mean = lax.optimization_barrier(jnp.sum(lag_state, axis=0, dtype=jnp.float32)) / crowd_members_number
        lag_anomaly = lax.optimization_barrier((lag_state.astype(jnp.float32) - lag_mean).astype(jnp.bfloat16))
        patch_grid = lag_anomaly.astype(jnp.float32).reshape(crowd_members_number, patch_rows, PATCH, patch_cols, PATCH)
        updated = jnp.einsum('maibj,abmn->naibj', patch_grid, mixing)
        return (updated.reshape(crowd_members_number, tile_vertical_extent, tile_lateral_extent) + lag_mean).astype(jnp.bfloat16)
    return lax.map(smooth, delayed_crowd_history)
```

```python
import functools

import jax
import jax.numpy as jnp
from jax import lax
from jax.experimental import pallas as pl
from jax.experimental.pallas import tpu as pltpu
from jax.sharding import PartitionSpec as P

PATCH = 16
NS_STEPS = 4
HALO = 3
MESH = pl.DeviceIdType.MESH
NT = (((1,), (1,)), ((), ()))


def split2(x):
    high = x.astype(jnp.bfloat16)
    return high, (x - high.astype(jnp.float32)).astype(jnp.bfloat16)


def product(x, y):
    xh, xl = split2(x)
    yh, yl = split2(y)
    dot = functools.partial(jnp.dot, preferred_element_type=jnp.float32)
    return dot(xh, yh) + (dot(xh, yl) + dot(xl, yh))


def kernel(
    tiles,
    lags,
    fore_ref,
    spot_ref,
    heat_ref,
    spread_ref,
    alive_ref,
    radius_ref,
    hist_hbm,
    out_ref,
    hist_ref,
    lift_ref,
    mean_ref,
    turned_ref,
    fore32_ref,
    send_ref,
    cells_ref,
    field_ref,
    wsend_ref,
    wcells_ref,
    acc_ref,
    gsend_ref,
    gram_ref,
    rsend_ref,
    rhs_ref,
    tsend_ref,
    trans_ref,
    hist_sem,
    send_sem,
    recv_sem,
    wsend_sem,
    wrecv_sem,
    gsend_sem,
    grecv_sem,
    rsend_sem,
    rrecv_sem,
    tsend_sem,
    trecv_sem,
):
    tile = lax.axis_index("dom")
    lag = lax.axis_index("lag")
    share, rows, cols = fore_ref.shape
    members = share * lags
    groups = rows // lags
    patch_cols = cols // PATCH
    slots = spot_ref.shape[1]
    f32, bf16 = jnp.float32, jnp.bfloat16

    def place(target_tile, target_lag):
        return {"dom": target_tile, "lag": target_lag}

    def peer(step):
        return lax.rem(lag + step, lags)

    load = pltpu.make_async_copy(hist_hbm.at[0], hist_ref, hist_sem)
    load.start()

    barrier = pltpu.get_barrier_semaphore()

    def greet(target_tile, target_lag):
        pl.semaphore_signal(
            barrier, inc=1, device_id=place(target_tile, target_lag), device_id_type=MESH
        )

    @pl.loop(1, lags)
    def _(step):
        greet(tile, peer(step))

    @pl.when(tile > 0)
    def _():
        @pl.loop(0, lags)
        def _(step):
            greet(tile - 1, step)

    @pl.when(tile < tiles - 1)
    def _():
        @pl.loop(0, lags)
        def _(step):
            greet(tile + 1, step)

    for m in range(share):
        fore32_ref[m * rows : (m + 1) * rows, :] = fore_ref[m].astype(f32)
    for target in range(lags):
        for k in range(groups):
            row = k * lags + target
            send_ref[target, k] = fore32_ref[pl.ds(row, share, stride=rows), :].astype(bf16)

    field_ref[...] = jnp.zeros_like(field_ref)
    slot_index = lax.broadcasted_iota(jnp.int32, (1, slots), 1)
    row_iota = lax.broadcasted_iota(jnp.int32, (PATCH, slots), 0)
    col_iota = lax.broadcasted_iota(jnp.int32, (cols, slots), 0)

    @pl.loop(0, rows // PATCH)
    def _(a):
        @pl.loop(0, patch_cols)
        def _(b):
            p = a * patch_cols + b
            spot = spot_ref[pl.ds(p, 1), :]
            live = slot_index < alive_ref[p]
            spread = jnp.where(live, spread_ref[pl.ds(p, 1), :], 0.0)
            weight = spread.astype(bf16).astype(f32)
            level = spread * heat_ref[pl.ds(p, 1), :]
            parts = [weight]
            for value in (level, spread):
                for _ in range(3):
                    part = value.astype(bf16).astype(f32)
                    parts.append(part)
                    value = value - part
            in_row = row_iota == lax.shift_right_logical(spot, 4)
            in_col = col_iota == (spot & (PATCH - 1)) + b * PATCH
            left = jnp.concatenate([jnp.where(in_row, part, 0.0) for part in parts], axis=0)
            right = jnp.where(in_col, 1.0, 0.0).astype(bf16)
            sums = lax.dot_general(left.astype(bf16), right, NT, preferred_element_type=f32)
            base = pl.multiple_of(a * PATCH, PATCH)
            for q, chosen in enumerate(((0,), (3, 2, 1), (6, 5, 4))):
                total = field_ref[pl.ds(q * rows + base, PATCH), :]
                for c in chosen:
                    total = total + sums[c * PATCH : (c + 1) * PATCH]
                field_ref[pl.ds(q * rows + base, PATCH), :] = total

    for k in range(groups):
        mine = field_ref[pl.ds(k * lags + lag, 8, stride=rows), :]
        wsend_ref[k] = mine
        wcells_ref[HALO + k] = mine

    for k in range(groups):
        cells_ref[HALO + k, lag] = send_ref[lag, k]

    @pl.when(tile == 0)
    def _():
        cells_ref[0:HALO] = jnp.zeros((HALO, lags, share, cols), bf16)
        wcells_ref[0:HALO] = jnp.zeros((HALO, 8, cols), f32)

    @pl.when(tile == tiles - 1)
    def _():
        cells_ref[HALO + groups :] = jnp.zeros((HALO, lags, share, cols), bf16)
        wcells_ref[HALO + groups :] = jnp.zeros((HALO, 8, cols), f32)

    neighbours = (
        lags - 1 + jnp.where(tile > 0, lags, 0) + jnp.where(tile < tiles - 1, lags, 0)
    )
    pl.semaphore_wait(barrier, neighbours)

    def cell_copy(kind, target_lag, source_lag):
        first = 1 if kind == 1 else 0
        count = groups if kind == 0 else HALO
        start = (HALO, 0, HALO + groups)[kind]
        return pltpu.make_async_remote_copy(
            src_ref=send_ref.at[target_lag, pl.ds(first, count)],
            dst_ref=cells_ref.at[pl.ds(start, count), source_lag],
            send_sem=send_sem.at[kind, target_lag],
            recv_sem=recv_sem.at[kind, source_lag],
            device_id=place(tile + (0, 1, -1)[kind], target_lag),
            device_id_type=MESH,
        )

    def weight_copy(kind):
        first = 1 if kind == 1 else 0
        start = (HALO, 0, HALO + groups)[kind]
        return pltpu.make_async_remote_copy(
            src_ref=wsend_ref.at[pl.ds(first, HALO)],
            dst_ref=wcells_ref.at[pl.ds(start, HALO)],
            send_sem=wsend_sem.at[kind - 1],
            recv_sem=wrecv_sem.at[kind - 1],
            device_id=place(tile + (0, 1, -1)[kind], lag),
            device_id_type=MESH,
        )

    has_below = tile < tiles - 1
    has_above = tile > 0

    @pl.when(has_below)
    def _():
        @pl.loop(0, lags)
        def _(step):
            cell_copy(1, peer(step), lag).start()

        weight_copy(1).start()

    @pl.when(has_above)
    def _():
        @pl.loop(0, lags)
        def _(step):
            cell_copy(2, peer(step), lag).start()

        weight_copy(2).start()

    @pl.loop(1, lags)
    def _(step):
        cell_copy(0, peer(step), lag).start()

    load.wait()

    def lift(m, total):
        state = hist_ref[m].astype(f32)
        lift_ref[pl.ds(pl.multiple_of(m * rows, rows), rows), :] = state
        return total + state

    mean = lax.fori_loop(0, members, lift, jnp.zeros((rows, cols), f32)) / members
    mean_ref[...] = mean

    @pl.loop(0, rows)
    def _(r):
        state = lift_ref[pl.ds(r, members, stride=rows), :]
        turned_ref[r] = (state - mean_ref[pl.ds(r, 1), :]).astype(bf16)

    sub = lax.broadcasted_iota(jnp.int32, (patch_cols, cols), 0)
    lane = lax.broadcasted_iota(jnp.int32, (patch_cols, cols), 1)
    col_offset = (lane - PATCH * sub).astype(f32) - 7.5
    col_square = col_offset * col_offset
    squares = []
    for a in range(2):
        radius = jnp.zeros((patch_cols, cols), f32)
        for b in range(patch_cols):
            value = radius_ref[a * patch_cols + b].astype(f32)
            radius = jnp.where(sub == b, value, radius)
        squares.append(radius * radius)

    acc_ref[...] = jnp.zeros_like(acc_ref)

    for step in range(1, lags):
        cell_copy(0, lag, peer(step)).wait_recv()

    @pl.when(has_above)
    def _():
        @pl.loop(0, lags)
        def _(step):
            cell_copy(1, lag, step).wait_recv()

        weight_copy(1).wait_recv()

    @pl.when(has_below)
    def _():
        @pl.loop(0, lags)
        def _(step):
            cell_copy(2, lag, step).wait_recv()

        weight_copy(2).wait_recv()

    @pl.loop(0, groups + 2 * HALO - 2)
    def _(i):
        row_offset = (lags * i + lag).astype(f32) - 31.5
        lefts, rights = [], []
        for a in range(2):
            values = cells_ref[i + 2 * a].astype(f32).reshape(members, cols)
            average = jnp.sum(values, axis=0, keepdims=True) / members
            anomaly = (values - average).astype(bf16)
            wide = anomaly.astype(f32)
            table = wcells_ref[i + 2 * a]
            innovation = table[1:2] - table[2:3] * average
            taper = jnp.maximum(0.0, 1.0 - (row_offset * row_offset + col_square) / squares[a])
            taper = taper * taper
            scale = taper * table[0:1]
            pieces = [(wide * scale[b : b + 1]).astype(bf16) for b in range(patch_cols)]
            extra = jnp.concatenate([taper * innovation, jnp.zeros_like(taper)], axis=0)
            lefts.append(jnp.concatenate(pieces + [extra.astype(bf16)], axis=0))
            empty = jnp.zeros_like(anomaly)
            pair = [anomaly, empty] if a == 0 else [empty, anomaly]
            rights.append(jnp.concatenate(pair, axis=0))
        left = jnp.concatenate(lefts, axis=1)
        right = jnp.concatenate(rights, axis=1)
        acc_ref[...] += lax.dot_general(left, right, NT, preferred_element_type=f32)

    for b in range(lags):
        gsend_ref[b] = acc_ref[b * members : (b + 1) * members].astype(bf16)
        rsend_ref[b] = acc_ref[patch_cols * members + b : patch_cols * members + b + 1]

    def gram_copies(target_lag, source_lag):
        where = place(tile, target_lag)
        return (
            pltpu.make_async_remote_copy(
                src_ref=gsend_ref.at[target_lag],
                dst_ref=gram_ref.at[source_lag],
                send_sem=gsend_sem.at[target_lag],
                recv_sem=grecv_sem.at[source_lag],
                device_id=where,
                device_id_type=MESH,
            ),
            pltpu.make_async_remote_copy(
                src_ref=rsend_ref.at[target_lag],
                dst_ref=rhs_ref.at[source_lag],
                send_sem=rsend_sem.at[target_lag],
                recv_sem=rrecv_sem.at[source_lag],
                device_id=where,
                device_id_type=MESH,
            ),
        )

    @pl.loop(1, lags)
    def _(step):
        for copy in gram_copies(peer(step), lag):
            copy.start()

    gram_ref[lag] = gsend_ref[lag]
    rhs_ref[lag] = rsend_ref[lag]

    @pl.loop(1, lags)
    def _(step):
        for copy in gram_copies(lag, peer(step)):
            copy.wait_recv()

    gram = gram_ref[0].astype(f32)
    rhs = rhs_ref[0]
    for source in range(1, lags):
        gram = gram + gram_ref[source].astype(f32)
        rhs = rhs + rhs_ref[source]

    identity = (
        lax.broadcasted_iota(jnp.int32, (members, members), 0)
        == lax.broadcasted_iota(jnp.int32, (members, members), 1)
    ).astype(f32)
    halves = [gram[:, :members], gram[:, members:]]
    sides = [rhs[:, :members], rhs[:, members:]]
    bounds = [
        members - 1.0
        + jnp.sqrt(jnp.sum(jnp.sum(half * half, axis=1, keepdims=True), axis=0, keepdims=True))
        for half in halves
    ]
    iterates = [
        (half + (members - 1.0) * identity) / bound for half, bound in zip(halves, bounds)
    ]
    roots = [1.5 * identity - 0.5 * iterate for iterate in iterates]
    iterates = [product(iterate, root) for iterate, root in zip(iterates, roots)]
    for sweep in range(1, NS_STEPS):
        corrections = [
            1.5 * identity - 0.5 * product(root, iterate)
            for root, iterate in zip(roots, iterates)
        ]
        if sweep < NS_STEPS - 1:
            iterates = [product(y, c) for y, c in zip(iterates, corrections)]
        roots = [product(c, root) for c, root in zip(corrections, roots)]
    transforms = []
    for root, side, bound in zip(roots, sides, bounds):
        inner = jnp.sum(root * side, axis=1, keepdims=True)
        weights = jnp.sum(root * inner, axis=0, keepdims=True) / bound
        factor = jnp.sqrt(jnp.full_like(bound, members - 1.0)) / jnp.sqrt(bound)
        transforms.append(factor * root + weights)
    tsend_ref[...] = jnp.concatenate(transforms, axis=1).astype(bf16)

    def transform_copy(target_lag, source_lag):
        return pltpu.make_async_remote_copy(
            src_ref=tsend_ref,
            dst_ref=trans_ref.at[source_lag],
            send_sem=tsend_sem.at[target_lag],
            recv_sem=trecv_sem.at[source_lag],
            device_id=place(tile, target_lag),
            device_id_type=MESH,
        )

    @pl.loop(1, lags)
    def _(step):
        transform_copy(peer(step), lag).start()

    trans_ref[lag] = tsend_ref[...]

    @pl.loop(1, lags)
    def _(step):
        cell_copy(0, peer(step), lag).wait_send()
        for copy in gram_copies(peer(step), lag):
            copy.wait_send()

    @pl.when(has_below)
    def _():
        @pl.loop(0, lags)
        def _(step):
            cell_copy(1, step, lag).wait_send()

        weight_copy(1).wait_send()

    @pl.when(has_above)
    def _():
        @pl.loop(0, lags)
        def _(step):
            cell_copy(2, step, lag).wait_send()

        weight_copy(2).wait_send()

    @pl.loop(1, lags)
    def _(step):
        transform_copy(lag, peer(step)).wait_recv()

    transforms = trans_ref[...].reshape(lags * members, 2 * members)
    lane_patch = lax.broadcasted_iota(jnp.int32, (members, cols), 1) // PATCH
    half_rows = rows // 2

    @pl.loop(0, half_rows)
    def _(i):
        first, second = turned_ref[i], turned_ref[i + half_rows]
        empty = jnp.zeros_like(first)
        right = jnp.concatenate(
            [
                jnp.concatenate([first, empty], axis=1),
                jnp.concatenate([empty, second], axis=1),
            ],
            axis=0,
        )
        mixed = jnp.dot(transforms, right, preferred_element_type=f32)
        for a in range(2):
            value = mixed[:members, a * cols : (a + 1) * cols]
            for b in range(1, patch_cols):
                piece = mixed[b * members : (b + 1) * members, a * cols : (a + 1) * cols]
                value = jnp.where(lane_patch == b, piece, value)
            r = i + a * half_rows
            lift_ref[pl.ds(r, members, stride=rows), :] = value + mean_ref[pl.ds(r, 1), :]

    @pl.loop(0, members)
    def _(m):
        state = lift_ref[pl.ds(pl.multiple_of(m * rows, rows), rows), :]
        out_ref[0, m] = state.astype(bf16)

    @pl.loop(1, lags)
    def _(step):
        transform_copy(peer(step), lag).wait_send()


def solution(mesh):
    tiles, lags = mesh.shape["dom"], mesh.shape["lag"]

    def shards(history, forecast, spot, alive, heat, spread, radius):
        share, rows, cols = forecast.shape
        members = share * lags
        groups = rows // lags
        patch_cols = cols // PATCH
        window = groups + 2 * HALO
        f32, bf16, dma = jnp.float32, jnp.bfloat16, pltpu.SemaphoreType.DMA
        vmem = pl.BlockSpec(memory_space=pltpu.VMEM)
        smem = pl.BlockSpec(memory_space=pltpu.SMEM)
        return pl.pallas_call(
            functools.partial(kernel, tiles, lags),
            out_shape=jax.ShapeDtypeStruct(history.shape, history.dtype),
            in_specs=[vmem, vmem, vmem, vmem, smem, smem, pl.BlockSpec(memory_space=pl.ANY)],
            out_specs=vmem,
            scratch_shapes=[
                pltpu.VMEM((members, rows, cols), bf16),
                pltpu.VMEM((members * rows, cols), f32),
                pltpu.VMEM((rows, cols), f32),
                pltpu.VMEM((rows, members, cols), bf16),
                pltpu.VMEM((share * rows, cols), f32),
                pltpu.VMEM((lags, groups, share, cols), bf16),
                pltpu.VMEM((window, lags, share, cols), bf16),
                pltpu.VMEM((8 * rows, cols), f32),
                pltpu.VMEM((groups, 8, cols), f32),
                pltpu.VMEM((window, 8, cols), f32),
                pltpu.VMEM((patch_cols * members + 16, 2 * members), f32),
                pltpu.VMEM((lags, members, 2 * members), bf16),
                pltpu.VMEM((lags, members, 2 * members), bf16),
                pltpu.VMEM((lags, 1, 2 * members), f32),
                pltpu.VMEM((lags, 1, 2 * members), f32),
                pltpu.VMEM((members, 2 * members), bf16),
                pltpu.VMEM((lags, members, 2 * members), bf16),
                dma,
                dma((3, lags)),
                dma((3, lags)),
                dma((2,)),
                dma((2,)),
                dma((lags,)),
                dma((lags,)),
                dma((lags,)),
                dma((lags,)),
                dma((lags,)),
                dma((lags,)),
            ],
            compiler_params=pltpu.CompilerParams(collective_id=0, has_side_effects=True),
            name="smoother",
        )(forecast, spot, heat, spread, alive, radius, history)

    in_specs = (
        P("lag", None, "dom", None),
        P("lag", "dom", None),
        P("dom", None),
        P("dom"),
        P("dom", None),
        P("dom", None),
        P("dom"),
    )
    out_specs = P("lag", None, "dom", None)
    return jax.shard_map(shards, mesh=mesh, in_specs=in_specs, out_specs=out_specs, check_vma=False)
```

```python
import functools

import jax
import jax.numpy as jnp
from jax import lax
from jax.experimental import pallas as pl
from jax.experimental.pallas import tpu as pltpu
from jax.sharding import PartitionSpec as P

PATCH = 16
NS_STEPS = 4
WORKERS = 4
HALO = 24 // WORKERS
MESH = pl.DeviceIdType.MESH
NT = (((1,), (1,)), ((), ()))


def split2(x):
    high = x.astype(jnp.bfloat16)
    return high, (x - high.astype(jnp.float32)).astype(jnp.bfloat16)


def product(x, y):
    xh, xl = split2(x)
    yh, yl = split2(y)
    dot = functools.partial(jnp.dot, preferred_element_type=jnp.float32)
    return dot(xh, yh) + (dot(xh, yl) + dot(xl, yh))


def kernel(
    tiles,
    lags,
    fore_hbm,
    spot_hbm,
    heat_hbm,
    spread_hbm,
    alive_hbm,
    radius_hbm,
    hist_hbm,
    out_ref,
    fore_ref,
    spot_ref,
    heat_ref,
    spread_ref,
    alive_ref,
    radius_ref,
    hist_ref,
    mixed_ref,
    turn_ref,
    mean_ref,
    turned_ref,
    fore32_ref,
    send_ref,
    cells_ref,
    field_ref,
    wsend_ref,
    wcells_ref,
    acc_ref,
    gsend_ref,
    gram_ref,
    rsend_ref,
    rhs_ref,
    tsend_ref,
    trans_ref,
    load_sem,
    send_sem,
    recv_sem,
    wsend_sem,
    wrecv_sem,
    gsend_sem,
    grecv_sem,
    rsend_sem,
    rrecv_sem,
    tsend_sem,
    trecv_sem,
):
    tile = lax.axis_index("dom")
    lag = lax.axis_index("lag")
    share, rows, cols = fore_ref.shape
    members = share * lags
    groups = rows // WORKERS
    patch_cols = cols // PATCH
    slots = spot_ref.shape[1]
    block_rows = members + 16
    first = lags // 2 - WORKERS // 2
    f32, bf16 = jnp.float32, jnp.bfloat16
    has_below = tile < tiles - 1
    has_above = tile > 0
    mine = lag - first
    is_worker = jnp.logical_and(mine >= 0, mine < WORKERS)

    def place(target_tile, target_lag):
        return {"dom": target_tile, "lag": target_lag}

    loads = [
        pltpu.make_async_copy(source, target, load_sem.at[n])
        for n, (source, target) in enumerate(
            (
                (fore_hbm, fore_ref),
                (alive_hbm, alive_ref),
                (radius_hbm, radius_ref),
                (spot_hbm, spot_ref),
                (spread_hbm, spread_ref),
                (heat_hbm, heat_ref),
                (hist_hbm.at[0], hist_ref),
            )
        )
    ]

    barrier = pltpu.get_barrier_semaphore()

    def greet(target_tile, target_lag):
        pl.semaphore_signal(
            barrier, inc=1, device_id=place(target_tile, target_lag), device_id_type=MESH
        )

    @pl.when(is_worker)
    def _():
        @pl.when(has_above)
        def _():
            for target in range(lags):
                greet(tile - 1, target)

        @pl.when(has_below)
        def _():
            for target in range(lags):
                greet(tile + 1, target)

        for step in range(1, lags):
            greet(tile, lax.rem(lag + step, lags))

    for load in loads:
        load.start()

    loads[0].wait()
    for m in range(share):
        fore32_ref[m * rows : (m + 1) * rows, :] = fore_ref[m].astype(f32)
    for target in range(WORKERS):
        for k in range(groups):
            row = k * WORKERS + target
            send_ref[target, k] = fore32_ref[pl.ds(row, share, stride=rows), :].astype(bf16)

    pl.semaphore_wait(
        barrier,
        WORKERS
        - jnp.where(is_worker, 1, 0)
        + jnp.where(has_above, WORKERS, 0)
        + jnp.where(has_below, WORKERS, 0),
    )

    def cell_copy(kind, worker, source_lag):
        begin = groups - HALO if kind == 1 else 0
        count = groups if kind == 0 else HALO
        start = (HALO, 0, HALO + groups)[kind]
        return pltpu.make_async_remote_copy(
            src_ref=send_ref.at[worker, pl.ds(begin, count)],
            dst_ref=cells_ref.at[pl.ds(start, count), source_lag],
            send_sem=send_sem.at[kind, worker],
            recv_sem=recv_sem.at[kind, source_lag],
            device_id=place(tile + (0, 1, -1)[kind], first + worker),
            device_id_type=MESH,
        )

    def weight_copy(kind):
        begin = groups - HALO if kind == 1 else 0
        start = (HALO, 0, HALO + groups)[kind]
        return pltpu.make_async_remote_copy(
            src_ref=wsend_ref.at[pl.ds(begin, HALO)],
            dst_ref=wcells_ref.at[pl.ds(start, HALO)],
            send_sem=wsend_sem.at[kind - 1],
            recv_sem=wrecv_sem.at[kind - 1],
            device_id=place(tile + (0, 1, -1)[kind], lag),
            device_id_type=MESH,
        )

    def order(step):
        return jnp.where(lag < lags // 2, WORKERS - 1 - step, step)

    @pl.when(has_below)
    def _():
        for step in range(WORKERS):
            cell_copy(1, order(step), lag).start()

    @pl.when(has_above)
    def _():
        for step in range(WORKERS):
            cell_copy(2, order(step), lag).start()

    for step in range(WORKERS):
        worker = order(step)

        @pl.when(worker != mine)
        def _():
            cell_copy(0, worker, lag).start()

    for load in loads[1:6]:
        load.wait()

    def sides(kind, source_lag):
        return cell_copy(kind, 0, source_lag)

    def gram_copies(worker, source):
        where = place(tile, first + worker)
        return (
            pltpu.make_async_remote_copy(
                src_ref=gsend_ref.at[worker],
                dst_ref=gram_ref.at[source],
                send_sem=gsend_sem.at[worker],
                recv_sem=grecv_sem.at[source],
                device_id=where,
                device_id_type=MESH,
            ),
            pltpu.make_async_remote_copy(
                src_ref=rsend_ref.at[worker],
                dst_ref=rhs_ref.at[source],
                send_sem=rsend_sem.at[worker],
                recv_sem=rrecv_sem.at[source],
                device_id=where,
                device_id_type=MESH,
            ),
        )

    @pl.when(is_worker)
    def _():
        field_ref[...] = jnp.zeros_like(field_ref)
        slot_index = lax.broadcasted_iota(jnp.int32, (1, slots), 1)
        row_iota = lax.broadcasted_iota(jnp.int32, (PATCH, slots), 0)
        col_iota = lax.broadcasted_iota(jnp.int32, (cols, slots), 0)

        @pl.loop(0, rows // PATCH)
        def _(a):
            @pl.loop(0, patch_cols)
            def _(b):
                p = a * patch_cols + b
                spot = spot_ref[pl.ds(p, 1), :]
                live = slot_index < alive_ref[p]
                spread = jnp.where(live, spread_ref[pl.ds(p, 1), :], 0.0)
                weight = spread.astype(bf16).astype(f32)
                level = spread * heat_ref[pl.ds(p, 1), :]
                parts = [weight]
                for value in (level, spread):
                    for _ in range(3):
                        part = value.astype(bf16).astype(f32)
                        parts.append(part)
                        value = value - part
                in_row = row_iota == lax.shift_right_logical(spot, 4)
                in_col = col_iota == (spot & (PATCH - 1)) + b * PATCH
                left = jnp.concatenate([jnp.where(in_row, part, 0.0) for part in parts], axis=0)
                right = jnp.where(in_col, 1.0, 0.0).astype(bf16)
                sums = lax.dot_general(left.astype(bf16), right, NT, preferred_element_type=f32)
                base = pl.multiple_of(a * PATCH, PATCH)
                for q, chosen in enumerate(((0,), (3, 2, 1), (6, 5, 4))):
                    total = field_ref[pl.ds(q * rows + base, PATCH), :]
                    for c in chosen:
                        total = total + sums[c * PATCH : (c + 1) * PATCH]
                    field_ref[pl.ds(q * rows + base, PATCH), :] = total

        for k in range(groups):
            table = field_ref[pl.ds(k * WORKERS + mine, 8, stride=rows), :]
            wsend_ref[k] = table
            wcells_ref[HALO + k] = table

        @pl.when(has_below)
        def _():
            weight_copy(1).start()

        @pl.when(has_above)
        def _():
            weight_copy(2).start()

        for k in range(groups):
            cells_ref[HALO + k, lag] = send_ref[mine, k]

        @pl.when(tile == 0)
        def _():
            cells_ref[0:HALO] = jnp.zeros((HALO, lags, share, cols), bf16)
            wcells_ref[0:HALO] = jnp.zeros((HALO, 8, cols), f32)

        @pl.when(tile == tiles - 1)
        def _():
            cells_ref[HALO + groups :] = jnp.zeros((HALO, lags, share, cols), bf16)
            wcells_ref[HALO + groups :] = jnp.zeros((HALO, 8, cols), f32)

        sub = lax.broadcasted_iota(jnp.int32, (patch_cols, cols), 0)
        lane = lax.broadcasted_iota(jnp.int32, (patch_cols, cols), 1)
        col_offset = (lane - PATCH * sub).astype(f32) - 7.5
        col_square = col_offset * col_offset
        squares = []
        for a in range(2):
            radius = jnp.zeros((patch_cols, cols), f32)
            for b in range(patch_cols):
                value = radius_ref[a * patch_cols + b].astype(f32)
                radius = jnp.where(sub == b, value, radius)
            squares.append(radius * radius)

        acc_ref[...] = jnp.zeros_like(acc_ref)
        half = patch_cols // 2

        def accumulate(jj):
            wides, anomalies, scales, weighteds = [], [], [], []
            for n in range(2):
                j = 2 * jj + n
                values = cells_ref[j].astype(f32).reshape(members, cols)
                average = jnp.sum(values, axis=0, keepdims=True) / members
                anomaly = (values - average).astype(bf16)
                anomalies.append(anomaly)
                wides.append(anomaly.astype(f32))
                table = wcells_ref[j]
                innovation = table[1:2] - table[2:3] * average
                for a in range(2):
                    row_offset = (WORKERS * j - PATCH * a - 24 + mine).astype(f32) - 7.5
                    taper = 1.0 - (row_offset * row_offset + col_square) / squares[a]
                    taper = jnp.maximum(0.0, taper)
                    taper = taper * taper
                    both = taper[:half] + taper[half:]
                    scales.append(both * table[0:1])
                    weighteds.append(both * innovation)
            for b in range(half):
                lefts, rights = [], []
                for n in range(2):
                    column = []
                    for a in range(2):
                        scale, weighted = scales[2 * n + a], weighteds[2 * n + a]
                        column.append((wides[n] * scale[b : b + 1]).astype(bf16))
                        extra = jnp.where(sub == 0, weighted[b : b + 1], 0.0)
                        extra = jnp.concatenate([extra, jnp.zeros_like(extra)], axis=0)
                        column.append(extra.astype(bf16))
                    lefts.append(jnp.concatenate(column, axis=0))
                    near = lane[:1] < PATCH * b + 40
                    near, far = (
                        jnp.where(near, 1.0, 0.0).astype(bf16),
                        jnp.where(near, 0.0, 1.0).astype(bf16),
                    )
                    rights.append(
                        jnp.concatenate([anomalies[n] * near, anomalies[n] * far], axis=0)
                    )
                left = jnp.concatenate(lefts, axis=1)
                right = jnp.concatenate(rights, axis=1)
                acc_ref[b] += lax.dot_general(left, right, NT, preferred_element_type=f32)

        for source in range(lags):

            @pl.when(source != lag)
            def _():
                sides(0, source).wait_recv()

        @pl.loop(HALO // 2, (HALO + groups) // 2)
        def _(jj):
            accumulate(jj)

        @pl.loop(0, 2)
        def _(turn):
            side = jnp.where(tile < tiles // 2, turn, 1 - turn)

            @pl.when(jnp.logical_and(side == 0, has_above))
            def _():
                for source in range(lags):
                    sides(1, source).wait_recv()
                weight_copy(1).wait_recv()

            @pl.when(jnp.logical_and(side == 1, has_below))
            def _():
                for source in range(lags):
                    sides(2, source).wait_recv()
                weight_copy(2).wait_recv()

            @pl.loop(0, HALO // 2)
            def _(n):
                accumulate(n + side * ((HALO + groups) // 2))

        for worker in range(WORKERS):
            for a in range(2):
                base = a * block_rows
                gsend_ref[worker, a] = acc_ref[worker, base : base + members].astype(bf16)
                rsend_ref[worker, a : a + 1] = acc_ref[
                    worker, base + members : base + members + 1
                ]

        for worker in range(WORKERS):

            @pl.when(worker != mine)
            def _():
                for copy in gram_copies(worker, mine):
                    copy.start()

        gram_ref[mine] = gsend_ref[mine]
        rhs_ref[mine] = rsend_ref[mine]

    row_major = lax.broadcasted_iota(jnp.int32, (share * rows, share * rows), 0)
    member_major = lax.broadcasted_iota(jnp.int32, (share * rows, share * rows), 1)
    wanted = lax.rem(row_major, share) * rows + row_major // share
    turn_ref[...] = jnp.where(member_major == wanted, 1.0, 0.0).astype(bf16)

    loads[6].wait()

    def lift(m, total):
        for n in range(8):
            total = total + hist_ref[8 * m + n].astype(f32)
        return total

    mean = lax.fori_loop(0, members // 8, lift, jnp.zeros((rows, cols), f32)) / members
    mean_ref[...] = mean

    @pl.loop(0, members // 8)
    def _(m):
        for n in range(8):
            hist_ref[8 * m + n] = (hist_ref[8 * m + n].astype(f32) - mean).astype(bf16)

    @pl.loop(0, members // (2 * share))
    def _(g):
        first = hist_ref[pl.ds(2 * share * g, share)].reshape(share * rows, cols)
        second = hist_ref[pl.ds(2 * share * g + share, share)].reshape(share * rows, cols)
        pair = jnp.concatenate([first, second], axis=1)
        turned = jnp.dot(turn_ref[...], pair, preferred_element_type=f32)
        turned = turned.reshape(rows, share, 2 * cols)
        turned = jnp.concatenate([turned[:, :, :cols], turned[:, :, cols:]], axis=1)
        start = pl.multiple_of(2 * share * g, 2 * share)
        turned_ref[:, pl.ds(start, 2 * share), :] = turned.astype(bf16)


    def transform_copy(target_lag, worker):
        return pltpu.make_async_remote_copy(
            src_ref=tsend_ref,
            dst_ref=trans_ref.at[worker],
            send_sem=tsend_sem.at[target_lag],
            recv_sem=trecv_sem.at[worker],
            device_id=place(tile, target_lag),
            device_id_type=MESH,
        )

    @pl.when(is_worker)
    def _():
        for source in range(WORKERS):

            @pl.when(source != mine)
            def _():
                for copy in gram_copies(0, source):
                    copy.wait_recv()

        identity = (
            lax.broadcasted_iota(jnp.int32, (members, members), 0)
            == lax.broadcasted_iota(jnp.int32, (members, members), 1)
        ).astype(f32)
        halves, sides_ = [], []
        for a in range(2):
            gram = gram_ref[0, a].astype(f32)
            rhs = rhs_ref[0, a : a + 1]
            for source in range(1, WORKERS):
                gram = gram + gram_ref[source, a].astype(f32)
                rhs = rhs + rhs_ref[source, a : a + 1]
            halves += [gram[:, :members], gram[:, members:]]
            sides_ += [rhs[:, :members], rhs[:, members:]]
        bounds = [
            members
            - 1.0
            + jnp.sqrt(jnp.sum(jnp.sum(x * x, axis=1, keepdims=True), axis=0, keepdims=True))
            for x in halves
        ]
        iterates = [(x + (members - 1.0) * identity) / bound for x, bound in zip(halves, bounds)]
        roots = [1.5 * identity - 0.5 * iterate for iterate in iterates]
        iterates = [product(iterate, root) for iterate, root in zip(iterates, roots)]
        for sweep in range(1, NS_STEPS):
            corrections = [
                1.5 * identity - 0.5 * product(root, iterate)
                for root, iterate in zip(roots, iterates)
            ]
            if sweep < NS_STEPS - 1:
                iterates = [product(y, c) for y, c in zip(iterates, corrections)]
            roots = [product(c, root) for c, root in zip(corrections, roots)]
        transforms = []
        for root, side, bound in zip(roots, sides_, bounds):
            inner = jnp.sum(root * side, axis=1, keepdims=True)
            weights = jnp.sum(root * inner, axis=0, keepdims=True) / bound
            factor = jnp.sqrt(jnp.full_like(bound, members - 1.0)) / jnp.sqrt(bound)
            transforms.append(factor * root + weights)
        for a in range(2):
            tsend_ref[a] = jnp.concatenate(transforms[2 * a : 2 * a + 2], axis=1).astype(bf16)

        for target in (0, lags - 1, 1, lags - 2, 2, lags - 3, 3, lags - 4):

            @pl.when(target != lag)
            def _():
                transform_copy(target, mine).start()

        trans_ref[mine] = tsend_ref[...]

    lane_patch = lax.broadcasted_iota(jnp.int32, (members, cols), 1) // PATCH
    half_rows = rows // 2

    @pl.loop(0, WORKERS)
    def _(step):
        near = jnp.where(is_worker, mine, jnp.where(lag < first, 0, WORKERS - 1))
        worker = jnp.where(
            is_worker, lax.rem(near + step, WORKERS), jnp.where(lag < first, step, near - step)
        )

        @pl.when(worker != mine)
        def _():
            transform_copy(lag, worker).wait_recv()

        mine_low = lane_patch == worker
        mine_high = lane_patch == worker + WORKERS
        mask = jnp.logical_or(mine_low, mine_high)
        low = jnp.where(mine_low[:1], 1.0, 0.0).astype(bf16)
        high = jnp.where(mine_high[:1], 1.0, 0.0).astype(bf16)
        for a in range(2):
            block = trans_ref[worker, a]

            @pl.loop(0, half_rows // 2, unroll=8)
            def _(i):
                rights = []
                for n in range(2):
                    state = turned_ref[a * half_rows + 2 * i + n]
                    rights.append(jnp.concatenate([state * low, state * high], axis=0))
                right = jnp.concatenate(rights, axis=1)
                mixed = jnp.dot(block, right, preferred_element_type=f32)
                for n in range(2):
                    r = a * half_rows + 2 * i + n
                    value = mixed[:, n * cols : (n + 1) * cols] + mean_ref[pl.ds(r, 1), :]
                    pltpu.store(mixed_ref.at[r], value, mask=mask)

    @pl.loop(0, rows, unroll=4)
    def _(r):
        out_ref[r] = mixed_ref[r].astype(bf16)

    @pl.when(has_below)
    def _():
        for worker in range(WORKERS):
            cell_copy(1, worker, lag).wait_send()

    @pl.when(has_above)
    def _():
        for worker in range(WORKERS):
            cell_copy(2, worker, lag).wait_send()

    for worker in range(WORKERS):

        @pl.when(worker != mine)
        def _():
            cell_copy(0, worker, lag).wait_send()

    @pl.when(is_worker)
    def _():
        @pl.when(has_below)
        def _():
            weight_copy(1).wait_send()

        @pl.when(has_above)
        def _():
            weight_copy(2).wait_send()

        for worker in range(WORKERS):

            @pl.when(worker != mine)
            def _():
                for copy in gram_copies(worker, mine):
                    copy.wait_send()

        for target in range(lags):

            @pl.when(target != lag)
            def _():
                transform_copy(target, mine).wait_send()


def solution(mesh):
    tiles, lags = mesh.shape["dom"], mesh.shape["lag"]

    def shards(history, forecast, spot, alive, heat, spread, radius):
        share, rows, cols = forecast.shape
        members = share * lags
        groups = rows // WORKERS
        window = groups + 2 * HALO
        f32, bf16, dma = jnp.float32, jnp.bfloat16, pltpu.SemaphoreType.DMA
        result = pl.pallas_call(
            functools.partial(kernel, tiles, lags),
            out_shape=jax.ShapeDtypeStruct((rows, members, cols), history.dtype),
            in_specs=[pl.BlockSpec(memory_space=pl.ANY)] * 7,
            out_specs=pl.BlockSpec(memory_space=pltpu.VMEM),
            scratch_shapes=[
                pltpu.VMEM(forecast.shape, bf16),
                pltpu.VMEM(spot.shape, jnp.int32),
                pltpu.VMEM(heat.shape, f32),
                pltpu.VMEM(spread.shape, f32),
                pltpu.SMEM(alive.shape, jnp.int32),
                pltpu.SMEM(radius.shape, jnp.int32),
                pltpu.VMEM((members, rows, cols), bf16),
                pltpu.VMEM((rows, members, cols), f32),
                pltpu.VMEM((share * rows, share * rows), bf16),
                pltpu.VMEM((rows, cols), f32),
                pltpu.VMEM((rows, members, cols), bf16),
                pltpu.VMEM((share * rows, cols), f32),
                pltpu.VMEM((WORKERS, groups, share, cols), bf16),
                pltpu.VMEM((window, lags, share, cols), bf16),
                pltpu.VMEM((8 * rows, cols), f32),
                pltpu.VMEM((groups, 8, cols), f32),
                pltpu.VMEM((window, 8, cols), f32),
                pltpu.VMEM((WORKERS, 2 * (members + 16), 2 * members), f32),
                pltpu.VMEM((WORKERS, 2, members, 2 * members), bf16),
                pltpu.VMEM((WORKERS, 2, members, 2 * members), bf16),
                pltpu.VMEM((WORKERS, 2, 2 * members), f32),
                pltpu.VMEM((WORKERS, 2, 2 * members), f32),
                pltpu.VMEM((2, members, 2 * members), bf16),
                pltpu.VMEM((WORKERS, 2, members, 2 * members), bf16),
                dma((7,)),
                dma((3, lags)),
                dma((3, lags)),
                dma((2,)),
                dma((2,)),
                dma((lags,)),
                dma((lags,)),
                dma((lags,)),
                dma((lags,)),
                dma((lags,)),
                dma((lags,)),
            ],
            compiler_params=pltpu.CompilerParams(collective_id=0, has_side_effects=True),
            name="smoother",
        )(forecast, spot, heat, spread, alive, radius, history)
        return jnp.transpose(result, (1, 0, 2))[None]

    in_specs = (
        P("lag", None, "dom", None),
        P("lag", "dom", None),
        P("dom", None),
        P("dom"),
        P("dom", None),
        P("dom", None),
        P("dom"),
    )
    out_specs = P("lag", None, "dom", None)
    return jax.shard_map(shards, mesh=mesh, in_specs=in_specs, out_specs=out_specs, check_vma=False)
```

```python
import functools

import jax
import jax.numpy as jnp
from jax import lax
from jax.experimental import pallas as pl
from jax.experimental.pallas import tpu as pltpu
from jax.sharding import PartitionSpec as P

PATCH = 16
NS_STEPS = 4
WORKERS = 4
HALO = 24 // WORKERS
MESH = pl.DeviceIdType.MESH
NT = (((1,), (1,)), ((), ()))


def split2(x):
    high = x.astype(jnp.bfloat16)
    return high, (x - high.astype(jnp.float32)).astype(jnp.bfloat16)


def product(x, y, low, high):
    xh, xl = split2(x)
    yh, yl = split2(y)
    yh = jnp.concatenate([yh * low, yh * high], axis=0)
    yl = jnp.concatenate([yl * low, yl * high], axis=0)
    dot = functools.partial(jnp.dot, preferred_element_type=jnp.float32)
    wide = dot(jnp.concatenate([xh, xl], axis=1), jnp.concatenate([yh, yh], axis=0))
    return wide + dot(xh, yl)


def kernel(
    tiles,
    lags,
    fore_hbm,
    spot_hbm,
    heat_hbm,
    spread_hbm,
    alive_hbm,
    radius_hbm,
    hist_hbm,
    out_ref,
    fore_ref,
    spot_ref,
    heat_ref,
    spread_ref,
    alive_ref,
    radius_ref,
    hist_ref,
    mixed_ref,
    turn_ref,
    mean_ref,
    turned_ref,
    fore32_ref,
    send_ref,
    cells_ref,
    field_ref,
    wsend_ref,
    wcells_ref,
    acc_ref,
    gsend_ref,
    gram_ref,
    rsend_ref,
    rhs_ref,
    tsend_ref,
    trans_ref,
    load_sem,
    send_sem,
    recv_sem,
    wsend_sem,
    wrecv_sem,
    gsend_sem,
    grecv_sem,
    rsend_sem,
    rrecv_sem,
    tsend_sem,
    trecv_sem,
):
    tile = lax.axis_index("dom")
    lag = lax.axis_index("lag")
    share, rows, cols = fore_ref.shape
    members = share * lags
    groups = rows // WORKERS
    patch_cols = cols // PATCH
    slots = spot_ref.shape[1]
    block_rows = members + 16
    first = lags // 2 - WORKERS // 2
    f32, bf16 = jnp.float32, jnp.bfloat16
    has_below = tile < tiles - 1
    has_above = tile > 0
    mine = lag - first
    is_worker = jnp.logical_and(mine >= 0, mine < WORKERS)

    def place(target_tile, target_lag):
        return {"dom": target_tile, "lag": target_lag}

    loads = [
        pltpu.make_async_copy(source, target, load_sem.at[n])
        for n, (source, target) in enumerate(
            (
                (fore_hbm, fore_ref),
                (alive_hbm, alive_ref),
                (radius_hbm, radius_ref),
                (spot_hbm, spot_ref),
                (spread_hbm, spread_ref),
                (heat_hbm, heat_ref),
                (hist_hbm.at[0], hist_ref),
            )
        )
    ]

    barrier = pltpu.get_barrier_semaphore()

    def greet(target_tile, target_lag):
        pl.semaphore_signal(
            barrier, inc=1, device_id=place(target_tile, target_lag), device_id_type=MESH
        )

    @pl.when(is_worker)
    def _():
        @pl.when(has_above)
        def _():
            for target in range(lags):
                greet(tile - 1, target)

        @pl.when(has_below)
        def _():
            for target in range(lags):
                greet(tile + 1, target)

        for step in range(1, lags):
            greet(tile, lax.rem(lag + step, lags))

    for load in loads:
        load.start()

    loads[0].wait()
    for m in range(share):
        fore32_ref[m * rows : (m + 1) * rows, :] = fore_ref[m].astype(f32)
    for target in range(WORKERS):
        for k in range(groups):
            row = k * WORKERS + target
            send_ref[target, k] = fore32_ref[pl.ds(row, share, stride=rows), :].astype(bf16)

    pl.semaphore_wait(
        barrier,
        WORKERS
        - jnp.where(is_worker, 1, 0)
        + jnp.where(has_above, WORKERS, 0)
        + jnp.where(has_below, WORKERS, 0),
    )

    def cell_copy(kind, worker, source_lag):
        begin = groups - HALO if kind == 1 else 0
        count = groups if kind == 0 else HALO
        start = (HALO, 0, HALO + groups)[kind]
        return pltpu.make_async_remote_copy(
            src_ref=send_ref.at[worker, pl.ds(begin, count)],
            dst_ref=cells_ref.at[pl.ds(start, count), source_lag],
            send_sem=send_sem.at[kind, worker],
            recv_sem=recv_sem.at[kind, source_lag],
            device_id=place(tile + (0, 1, -1)[kind], first + worker),
            device_id_type=MESH,
        )

    def weight_copy(kind):
        begin = groups - HALO if kind == 1 else 0
        start = (HALO, 0, HALO + groups)[kind]
        return pltpu.make_async_remote_copy(
            src_ref=wsend_ref.at[pl.ds(begin, HALO)],
            dst_ref=wcells_ref.at[pl.ds(start, HALO)],
            send_sem=wsend_sem.at[kind - 1],
            recv_sem=wrecv_sem.at[kind - 1],
            device_id=place(tile + (0, 1, -1)[kind], lag),
            device_id_type=MESH,
        )

    def order(step):
        return jnp.where(lag < lags // 2, WORKERS - 1 - step, step)

    @pl.when(has_below)
    def _():
        for step in range(WORKERS):
            cell_copy(1, order(step), lag).start()

    @pl.when(has_above)
    def _():
        for step in range(WORKERS):
            cell_copy(2, order(step), lag).start()

    for step in range(WORKERS):
        worker = order(step)

        @pl.when(worker != mine)
        def _():
            cell_copy(0, worker, lag).start()

    for load in loads[1:6]:
        load.wait()

    def sides(kind, source_lag):
        return cell_copy(kind, 0, source_lag)

    def gram_copies(worker, source):
        where = place(tile, first + worker)
        return (
            pltpu.make_async_remote_copy(
                src_ref=gsend_ref.at[worker],
                dst_ref=gram_ref.at[source],
                send_sem=gsend_sem.at[worker],
                recv_sem=grecv_sem.at[source],
                device_id=where,
                device_id_type=MESH,
            ),
            pltpu.make_async_remote_copy(
                src_ref=rsend_ref.at[worker],
                dst_ref=rhs_ref.at[source],
                send_sem=rsend_sem.at[worker],
                recv_sem=rrecv_sem.at[source],
                device_id=where,
                device_id_type=MESH,
            ),
        )

    @pl.when(is_worker)
    def _():
        field_ref[...] = jnp.zeros_like(field_ref)
        slot_index = lax.broadcasted_iota(jnp.int32, (1, slots), 1)
        row_iota = lax.broadcasted_iota(jnp.int32, (PATCH, slots), 0)
        col_iota = lax.broadcasted_iota(jnp.int32, (cols, slots), 0)

        @pl.loop(0, rows // PATCH)
        def _(a):
            @pl.loop(0, patch_cols)
            def _(b):
                p = a * patch_cols + b
                spot = spot_ref[pl.ds(p, 1), :]
                live = slot_index < alive_ref[p]
                spread = jnp.where(live, spread_ref[pl.ds(p, 1), :], 0.0)
                weight = spread.astype(bf16).astype(f32)
                level = spread * heat_ref[pl.ds(p, 1), :]
                parts = [weight]
                for value in (level, spread):
                    for _ in range(3):
                        part = value.astype(bf16).astype(f32)
                        parts.append(part)
                        value = value - part
                in_row = row_iota == lax.shift_right_logical(spot, 4)
                in_col = col_iota == (spot & (PATCH - 1)) + b * PATCH
                left = jnp.concatenate([jnp.where(in_row, part, 0.0) for part in parts], axis=0)
                right = jnp.where(in_col, 1.0, 0.0).astype(bf16)
                sums = lax.dot_general(left.astype(bf16), right, NT, preferred_element_type=f32)
                base = pl.multiple_of(a * PATCH, PATCH)
                for q, chosen in enumerate(((0,), (3, 2, 1), (6, 5, 4))):
                    total = field_ref[pl.ds(q * rows + base, PATCH), :]
                    for c in chosen:
                        total = total + sums[c * PATCH : (c + 1) * PATCH]
                    field_ref[pl.ds(q * rows + base, PATCH), :] = total

        for k in range(groups):
            table = field_ref[pl.ds(k * WORKERS + mine, 8, stride=rows), :]
            wsend_ref[k] = table
            wcells_ref[HALO + k] = table

        @pl.when(has_below)
        def _():
            weight_copy(1).start()

        @pl.when(has_above)
        def _():
            weight_copy(2).start()

        for k in range(groups):
            cells_ref[HALO + k, lag] = send_ref[mine, k]

        @pl.when(tile == 0)
        def _():
            cells_ref[0:HALO] = jnp.zeros((HALO, lags, share, cols), bf16)
            wcells_ref[0:HALO] = jnp.zeros((HALO, 8, cols), f32)

        @pl.when(tile == tiles - 1)
        def _():
            cells_ref[HALO + groups :] = jnp.zeros((HALO, lags, share, cols), bf16)
            wcells_ref[HALO + groups :] = jnp.zeros((HALO, 8, cols), f32)

    row_major = lax.broadcasted_iota(jnp.int32, (share * rows, share * rows), 0)
    member_major = lax.broadcasted_iota(jnp.int32, (share * rows, share * rows), 1)
    wanted = lax.rem(row_major, share) * rows + row_major // share
    turn_ref[...] = jnp.where(member_major == wanted, 1.0, 0.0).astype(bf16)

    loads[6].wait()

    def lift(m, total):
        for n in range(8):
            total = total + hist_ref[8 * m + n].astype(f32)
        return total

    mean = lax.fori_loop(0, members // 8, lift, jnp.zeros((rows, cols), f32)) / members
    mean_ref[...] = mean

    @pl.loop(0, members // 8)
    def _(m):
        for n in range(8):
            hist_ref[8 * m + n] = (hist_ref[8 * m + n].astype(f32) - mean).astype(bf16)

    @pl.loop(0, members // (2 * share))
    def _(g):
        first = hist_ref[pl.ds(2 * share * g, share)].reshape(share * rows, cols)
        second = hist_ref[pl.ds(2 * share * g + share, share)].reshape(share * rows, cols)
        pair = jnp.concatenate([first, second], axis=1)
        turned = jnp.dot(turn_ref[...], pair, preferred_element_type=f32)
        turned = turned.reshape(rows, share, 2 * cols)
        turned = jnp.concatenate([turned[:, :, :cols], turned[:, :, cols:]], axis=1)
        start = pl.multiple_of(2 * share * g, 2 * share)
        turned_ref[:, pl.ds(start, 2 * share), :] = turned.astype(bf16)


    @pl.when(is_worker)
    def _():
        sub = lax.broadcasted_iota(jnp.int32, (patch_cols, cols), 0)
        lane = lax.broadcasted_iota(jnp.int32, (patch_cols, cols), 1)
        col_offset = (lane - PATCH * sub).astype(f32) - 7.5
        col_square = col_offset * col_offset
        squares = []
        for a in range(2):
            radius = jnp.zeros((patch_cols, cols), f32)
            for b in range(patch_cols):
                value = radius_ref[a * patch_cols + b].astype(f32)
                radius = jnp.where(sub == b, value, radius)
            squares.append(radius * radius)

        acc_ref[...] = jnp.zeros_like(acc_ref)
        half = patch_cols // 2

        def accumulate(begin, count):
            wides, anomalies, scales, weighteds = [], [], [], []
            for n in range(count):
                j = begin + n
                values = cells_ref[j].astype(f32).reshape(members, cols)
                average = jnp.sum(values, axis=0, keepdims=True) / members
                anomaly = (values - average).astype(bf16)
                anomalies.append(anomaly)
                wides.append(anomaly.astype(f32))
                table = wcells_ref[j]
                innovation = table[1:2] - table[2:3] * average
                for a in range(2):
                    row_offset = (WORKERS * j - PATCH * a - 24 + mine).astype(f32) - 7.5
                    taper = 1.0 - (row_offset * row_offset + col_square) / squares[a]
                    taper = jnp.maximum(0.0, taper)
                    taper = taper * taper
                    both = taper[:half] + taper[half:]
                    scales.append(both * table[0:1])
                    weighteds.append(both * innovation)
            for b in range(half):
                near = lane[:1] < PATCH * b + 40
                near, far = (
                    jnp.where(near, 1.0, 0.0).astype(bf16),
                    jnp.where(near, 0.0, 1.0).astype(bf16),
                )
                lefts, rights = [], []
                for n in range(count):
                    column = []
                    for a in range(2):
                        scale, weighted = scales[2 * n + a], weighteds[2 * n + a]
                        column.append((wides[n] * scale[b : b + 1]).astype(bf16))
                        extra = jnp.where(sub == 0, weighted[b : b + 1], 0.0)
                        extra = jnp.concatenate([extra, jnp.zeros_like(extra)], axis=0)
                        column.append(extra.astype(bf16))
                    lefts.append(jnp.concatenate(column, axis=0))
                    rights.append(
                        jnp.concatenate([anomalies[n] * near, anomalies[n] * far], axis=0)
                    )
                left = jnp.concatenate(lefts, axis=1)
                right = jnp.concatenate(rights, axis=1)
                acc_ref[b] += lax.dot_general(left, right, NT, preferred_element_type=f32)

        for source in range(lags):

            @pl.when(source != lag)
            def _():
                sides(0, source).wait_recv()

        @pl.loop(0, 2)
        def _(n):
            accumulate(HALO + n * (groups // 2), groups // 2)

        @pl.loop(0, 2)
        def _(turn):
            side = jnp.where(tile < tiles // 2, turn, 1 - turn)

            @pl.when(jnp.logical_and(side == 0, has_above))
            def _():
                for source in range(lags):
                    sides(1, source).wait_recv()
                weight_copy(1).wait_recv()

            @pl.when(jnp.logical_and(side == 1, has_below))
            def _():
                for source in range(lags):
                    sides(2, source).wait_recv()
                weight_copy(2).wait_recv()

            accumulate(side * (HALO + groups), HALO)

        for worker in range(WORKERS):
            for a in range(2):
                base = a * block_rows
                gsend_ref[worker, a] = acc_ref[worker, base : base + members].astype(bf16)
                rsend_ref[worker, a : a + 1] = acc_ref[
                    worker, base + members : base + members + 1
                ]

        for worker in range(WORKERS):

            @pl.when(worker != mine)
            def _():
                for copy in gram_copies(worker, mine):
                    copy.start()

        gram_ref[mine] = gsend_ref[mine]
        rhs_ref[mine] = rsend_ref[mine]

    def transform_copy(target_lag, worker):
        return pltpu.make_async_remote_copy(
            src_ref=tsend_ref,
            dst_ref=trans_ref.at[worker],
            send_sem=tsend_sem.at[target_lag],
            recv_sem=trecv_sem.at[worker],
            device_id=place(tile, target_lag),
            device_id_type=MESH,
        )

    @pl.when(is_worker)
    def _():
        for source in range(WORKERS):

            @pl.when(source != mine)
            def _():
                for copy in gram_copies(0, source):
                    copy.wait_recv()

        row = lax.broadcasted_iota(jnp.int32, (members, 2 * members), 0)
        column = lax.broadcasted_iota(jnp.int32, (members, 2 * members), 1)
        identity = (row == lax.rem(column, members)).astype(f32)
        is_low = column[:1] < members
        low = jnp.where(is_low, 1.0, 0.0).astype(bf16)
        high = jnp.where(is_low, 0.0, 1.0).astype(bf16)

        def pick(values):
            return jnp.where(is_low, values[0], values[1])

        def lane_sums(x):
            return [
                jnp.sum(x[:, n * members : (n + 1) * members], axis=1, keepdims=True)
                for n in range(2)
            ]

        iterates, roots, bounds, rights_ = [], [], [], []
        for a in range(2):
            gram = gram_ref[0, a].astype(f32)
            rhs = rhs_ref[0, a : a + 1]
            for source in range(1, WORKERS):
                gram = gram + gram_ref[source, a].astype(f32)
                rhs = rhs + rhs_ref[source, a : a + 1]
            squares_ = lane_sums(jnp.sum(gram * gram, axis=0, keepdims=True))
            bound = members - 1.0 + jnp.sqrt(pick(squares_))
            bounds.append(bound)
            rights_.append(rhs)
            iterates.append((gram + (members - 1.0) * identity) / bound)
        roots = [1.5 * identity - 0.5 * iterate for iterate in iterates]
        iterates = [product(y, root, low, high) for y, root in zip(iterates, roots)]
        for sweep in range(1, NS_STEPS):
            corrections = [
                1.5 * identity - 0.5 * product(root, y, low, high)
                for root, y in zip(roots, iterates)
            ]
            if sweep < NS_STEPS - 1:
                iterates = [product(y, c, low, high) for y, c in zip(iterates, corrections)]
            roots = [product(c, root, low, high) for c, root in zip(corrections, roots)]
        for a in range(2):
            root, bound = roots[a], bounds[a]
            inner = pick(lane_sums(root * rights_[a]))
            weights = jnp.sum(root * inner, axis=0, keepdims=True) / bound
            factor = jnp.sqrt(jnp.full_like(bound, members - 1.0)) / jnp.sqrt(bound)
            tsend_ref[a] = (factor * root + weights).astype(bf16)

        for target in (0, lags - 1, 1, lags - 2, 2, lags - 3, 3, lags - 4):

            @pl.when(target != lag)
            def _():
                transform_copy(target, mine).start()

        trans_ref[mine] = tsend_ref[...]

    lane_patch = lax.broadcasted_iota(jnp.int32, (members, cols), 1) // PATCH
    half_rows = rows // 2

    @pl.loop(0, WORKERS)
    def _(step):
        near = jnp.where(is_worker, mine, jnp.where(lag < first, 0, WORKERS - 1))
        worker = jnp.where(
            is_worker, lax.rem(near + step, WORKERS), jnp.where(lag < first, step, near - step)
        )

        @pl.when(worker != mine)
        def _():
            transform_copy(lag, worker).wait_recv()

        mine_low = lane_patch == worker
        mine_high = lane_patch == worker + WORKERS
        mask = jnp.logical_or(mine_low, mine_high)
        low = jnp.where(mine_low[:1], 1.0, 0.0).astype(bf16)
        high = jnp.where(mine_high[:1], 1.0, 0.0).astype(bf16)
        for a in range(2):
            block = trans_ref[worker, a]

            @pl.loop(0, half_rows // 2, unroll=8)
            def _(i):
                rights = []
                for n in range(2):
                    state = turned_ref[a * half_rows + 2 * i + n]
                    rights.append(jnp.concatenate([state * low, state * high], axis=0))
                right = jnp.concatenate(rights, axis=1)
                mixed = jnp.dot(block, right, preferred_element_type=f32)
                for n in range(2):
                    r = a * half_rows + 2 * i + n
                    value = mixed[:, n * cols : (n + 1) * cols] + mean_ref[pl.ds(r, 1), :]
                    pltpu.store(mixed_ref.at[r], value, mask=mask)

    @pl.loop(0, rows, unroll=4)
    def _(r):
        out_ref[r] = mixed_ref[r].astype(bf16)

    @pl.when(has_below)
    def _():
        for worker in range(WORKERS):
            cell_copy(1, worker, lag).wait_send()

    @pl.when(has_above)
    def _():
        for worker in range(WORKERS):
            cell_copy(2, worker, lag).wait_send()

    for worker in range(WORKERS):

        @pl.when(worker != mine)
        def _():
            cell_copy(0, worker, lag).wait_send()

    @pl.when(is_worker)
    def _():
        @pl.when(has_below)
        def _():
            weight_copy(1).wait_send()

        @pl.when(has_above)
        def _():
            weight_copy(2).wait_send()

        for worker in range(WORKERS):

            @pl.when(worker != mine)
            def _():
                for copy in gram_copies(worker, mine):
                    copy.wait_send()

        for target in range(lags):

            @pl.when(target != lag)
            def _():
                transform_copy(target, mine).wait_send()


def solution(mesh):
    tiles, lags = mesh.shape["dom"], mesh.shape["lag"]

    def shards(history, forecast, spot, alive, heat, spread, radius):
        share, rows, cols = forecast.shape
        members = share * lags
        groups = rows // WORKERS
        window = groups + 2 * HALO
        f32, bf16, dma = jnp.float32, jnp.bfloat16, pltpu.SemaphoreType.DMA
        result = pl.pallas_call(
            functools.partial(kernel, tiles, lags),
            out_shape=jax.ShapeDtypeStruct((rows, members, cols), history.dtype),
            in_specs=[pl.BlockSpec(memory_space=pltpu.HBM)] * 7,
            out_specs=pl.BlockSpec(memory_space=pltpu.VMEM),
            scratch_shapes=[
                pltpu.VMEM(forecast.shape, bf16),
                pltpu.VMEM(spot.shape, jnp.int32),
                pltpu.VMEM(heat.shape, f32),
                pltpu.VMEM(spread.shape, f32),
                pltpu.SMEM(alive.shape, jnp.int32),
                pltpu.SMEM(radius.shape, jnp.int32),
                pltpu.VMEM((members, rows, cols), bf16),
                pltpu.VMEM((rows, members, cols), f32),
                pltpu.VMEM((share * rows, share * rows), bf16),
                pltpu.VMEM((rows, cols), f32),
                pltpu.VMEM((rows, members, cols), bf16),
                pltpu.VMEM((share * rows, cols), f32),
                pltpu.VMEM((WORKERS, groups, share, cols), bf16),
                pltpu.VMEM((window, lags, share, cols), bf16),
                pltpu.VMEM((8 * rows, cols), f32),
                pltpu.VMEM((groups, 8, cols), f32),
                pltpu.VMEM((window, 8, cols), f32),
                pltpu.VMEM((WORKERS, 2 * (members + 16), 2 * members), f32),
                pltpu.VMEM((WORKERS, 2, members, 2 * members), bf16),
                pltpu.VMEM((WORKERS, 2, members, 2 * members), bf16),
                pltpu.VMEM((WORKERS, 2, 2 * members), f32),
                pltpu.VMEM((WORKERS, 2, 2 * members), f32),
                pltpu.VMEM((2, members, 2 * members), bf16),
                pltpu.VMEM((WORKERS, 2, members, 2 * members), bf16),
                dma((7,)),
                dma((3, lags)),
                dma((3, lags)),
                dma((2,)),
                dma((2,)),
                dma((lags,)),
                dma((lags,)),
                dma((lags,)),
                dma((lags,)),
                dma((lags,)),
                dma((lags,)),
            ],
            compiler_params=pltpu.CompilerParams(
                collective_id=0, has_side_effects=True, vmem_limit_bytes=16 << 20
            ),
            name="smoother",
        )(
            *(
                pltpu.with_memory_space_constraint(x, pltpu.HBM)
                for x in (forecast, spot, heat, spread, alive, radius, history)
            )
        )
        return jnp.transpose(result, (1, 0, 2))[None]

    in_specs = (
        P("lag", None, "dom", None),
        P("lag", "dom", None),
        P("dom", None),
        P("dom"),
        P("dom", None),
        P("dom", None),
        P("dom"),
    )
    out_specs = P("lag", None, "dom", None)
    return jax.shard_map(shards, mesh=mesh, in_specs=in_specs, out_specs=out_specs, check_vma=False)
```

```python
import functools

import jax
import jax.numpy as jnp
from jax import lax
from jax.experimental import pallas as pl
from jax.experimental.pallas import tpu as pltpu
from jax.sharding import PartitionSpec as P

PATCH = 16
NS_STEPS = 4
WORKERS = 4
HALO = 24 // WORKERS
MESH = pl.DeviceIdType.MESH
NT = (((1,), (1,)), ((), ()))


def split2(x):
    high = x.astype(jnp.bfloat16)
    return high, (x - high.astype(jnp.float32)).astype(jnp.bfloat16)


def product(x, y, low, high):
    xh, xl = split2(x)
    yh, yl = split2(y)
    yh = jnp.concatenate([yh * low, yh * high], axis=0)
    yl = jnp.concatenate([yl * low, yl * high], axis=0)
    dot = functools.partial(jnp.dot, preferred_element_type=jnp.float32)
    wide = dot(jnp.concatenate([xh, xl], axis=1), jnp.concatenate([yh, yh], axis=0))
    return wide + dot(xh, yl)


def kernel(
    tiles,
    lags,
    fore_hbm,
    spot_hbm,
    heat_hbm,
    spread_hbm,
    alive_hbm,
    radius_hbm,
    hist_hbm,
    out_ref,
    fore_ref,
    spot_ref,
    heat_ref,
    spread_ref,
    alive_ref,
    radius_ref,
    hist_ref,
    mixed_ref,
    turn_ref,
    mean_ref,
    turned_ref,
    fore32_ref,
    send_ref,
    cells_ref,
    field_ref,
    wsend_ref,
    wcells_ref,
    acc_ref,
    gsend_ref,
    gram_ref,
    rsend_ref,
    rhs_ref,
    tsend_ref,
    trans_ref,
    relay_ref,
    wrelay_ref,
    load_sem,
    send_sem,
    recv_sem,
    wsend_sem,
    wrecv_sem,
    gsend_sem,
    grecv_sem,
    rsend_sem,
    rrecv_sem,
    tsend_sem,
    trecv_sem,
    hsend_sem,
    hrecv_sem,
    relay_sem,
    forward_sem,
):
    tile = lax.axis_index("dom")
    lag = lax.axis_index("lag")
    share, rows, cols = fore_ref.shape
    members = share * lags
    groups = rows // WORKERS
    patch_cols = cols // PATCH
    slots = spot_ref.shape[1]
    block_rows = members + 16
    first = lags // 2 - WORKERS // 2
    f32, bf16 = jnp.float32, jnp.bfloat16
    has_below = tile < tiles - 1
    has_above = tile > 0
    seam = tiles // 2
    is_lower = tile == seam - 1
    is_upper = tile == seam
    is_relay = tile == tiles - 1
    near_below = jnp.logical_and(has_below, tile != seam - 1)
    near_above = jnp.logical_and(has_above, tile != seam)
    mine = lag - first
    is_worker = jnp.logical_and(mine >= 0, mine < WORKERS)

    def place(target_tile, target_lag):
        return {"dom": target_tile, "lag": target_lag}

    loads = [
        pltpu.make_async_copy(source, target, load_sem.at[n])
        for n, (source, target) in enumerate(
            (
                (fore_hbm, fore_ref),
                (alive_hbm, alive_ref),
                (radius_hbm, radius_ref),
                (spot_hbm, spot_ref),
                (spread_hbm, spread_ref),
                (heat_hbm, heat_ref),
                (hist_hbm.at[0], hist_ref),
            )
        )
    ]

    barrier = pltpu.get_barrier_semaphore()

    def greet(target_tile, target_lag):
        pl.semaphore_signal(
            barrier, inc=1, device_id=place(target_tile, target_lag), device_id_type=MESH
        )

    @pl.when(is_worker)
    def _():
        @pl.when(is_lower)
        def _():
            for target in range(lags):
                greet(tiles - 1, target)

        @pl.when(is_upper)
        def _():
            for target in range(lags):
                greet(tile - 1, target)

        for step in range(1, lags):
            greet(tile, lax.rem(lag + step, lags))

        @pl.when(near_above)
        def _():
            greet(tile - 1, lag)

        @pl.when(near_below)
        def _():
            greet(tile + 1, lag)

    @pl.when(is_relay)
    def _():
        greet(seam, lag)

    for load in loads:
        load.start()

    loads[0].wait()
    for m in range(share):
        fore32_ref[m * rows : (m + 1) * rows, :] = fore_ref[m].astype(f32)
    for target in range(WORKERS):
        for k in range(groups):
            row = k * WORKERS + target
            send_ref[target, k] = fore32_ref[pl.ds(row, share, stride=rows), :].astype(bf16)

    pl.semaphore_wait(
        barrier,
        WORKERS
        - jnp.where(is_worker, 1, 0)
        + jnp.where(jnp.logical_and(is_worker, near_above), 1, 0)
        + jnp.where(jnp.logical_and(is_worker, near_below), 1, 0)
        + jnp.where(is_lower, WORKERS, 0)
        + jnp.where(is_upper, 1, 0)
        + jnp.where(is_relay, WORKERS, 0),
    )

    def cell_copy(kind, worker, source_lag):
        begin = groups - HALO if kind == 1 else 0
        count = groups if kind == 0 else HALO
        start = (HALO, 0, HALO + groups)[kind]
        return pltpu.make_async_remote_copy(
            src_ref=send_ref.at[worker, pl.ds(begin, count)],
            dst_ref=cells_ref.at[pl.ds(start, count), source_lag],
            send_sem=send_sem.at[kind, worker],
            recv_sem=recv_sem.at[kind, source_lag],
            device_id=place(tile + (0, 1, -1)[kind], first + worker),
            device_id_type=MESH,
        )

    def weight_copy(kind):
        begin = groups - HALO if kind == 1 else 0
        start = (HALO, 0, HALO + groups)[kind]
        return pltpu.make_async_remote_copy(
            src_ref=wsend_ref.at[pl.ds(begin, HALO)],
            dst_ref=wcells_ref.at[pl.ds(start, HALO)],
            send_sem=wsend_sem.at[kind - 1],
            recv_sem=wrecv_sem.at[kind - 1],
            device_id=place(tile + (0, 1, -1)[kind], lag),
            device_id_type=MESH,
        )

    def order(step):
        return jnp.where(lag < lags // 2, WORKERS - 1 - step, step)

    def halo_copy(kind):
        return pltpu.make_async_remote_copy(
            src_ref=cells_ref.at[pl.ds(groups if kind == 1 else HALO, HALO)],
            dst_ref=cells_ref.at[pl.ds(0 if kind == 1 else HALO + groups, HALO)],
            send_sem=hsend_sem.at[kind - 1],
            recv_sem=hrecv_sem.at[kind - 1],
            device_id=place(tile + (0, 1, -1)[kind], lag),
            device_id_type=MESH,
        )

    def relay_copy():
        return pltpu.make_async_remote_copy(
            src_ref=send_ref.at[:, pl.ds(0, HALO)],
            dst_ref=relay_ref,
            send_sem=relay_sem.at[0],
            recv_sem=relay_sem.at[1],
            device_id=place(tiles - 1, lag),
            device_id_type=MESH,
        )

    def relay_weights():
        return pltpu.make_async_remote_copy(
            src_ref=wsend_ref.at[pl.ds(0, HALO)],
            dst_ref=wrelay_ref,
            send_sem=relay_sem.at[2],
            recv_sem=relay_sem.at[3],
            device_id=place(tiles - 1, lag),
            device_id_type=MESH,
        )

    def forward_copy(worker):
        return pltpu.make_async_remote_copy(
            src_ref=relay_ref.at[worker],
            dst_ref=cells_ref.at[pl.ds(HALO + groups, HALO), lag],
            send_sem=forward_sem.at[worker],
            recv_sem=recv_sem.at[2, lag],
            device_id=place(seam - 1, first + worker),
            device_id_type=MESH,
        )

    def forward_weights():
        return pltpu.make_async_remote_copy(
            src_ref=wrelay_ref,
            dst_ref=wcells_ref.at[pl.ds(HALO + groups, HALO)],
            send_sem=forward_sem.at[WORKERS],
            recv_sem=wrecv_sem.at[1],
            device_id=place(seam - 1, lag),
            device_id_type=MESH,
        )

    @pl.when(is_lower)
    def _():
        for step in range(WORKERS):
            cell_copy(1, order(step), lag).start()

    @pl.when(is_upper)
    def _():
        relay_copy().start()

    for step in range(WORKERS):
        worker = order(step)

        @pl.when(worker != mine)
        def _():
            cell_copy(0, worker, lag).start()

    @pl.when(is_relay)
    def _():
        relay_copy().wait_recv()
        for step in range(WORKERS):
            forward_copy(order(step)).start()

    for load in loads[1:6]:
        load.wait()

    def sides(kind, source_lag):
        return cell_copy(kind, 0, source_lag)

    def gram_copies(worker, source):
        where = place(tile, first + worker)
        return (
            pltpu.make_async_remote_copy(
                src_ref=gsend_ref.at[worker],
                dst_ref=gram_ref.at[source],
                send_sem=gsend_sem.at[worker],
                recv_sem=grecv_sem.at[source],
                device_id=where,
                device_id_type=MESH,
            ),
            pltpu.make_async_remote_copy(
                src_ref=rsend_ref.at[worker],
                dst_ref=rhs_ref.at[source],
                send_sem=rsend_sem.at[worker],
                recv_sem=rrecv_sem.at[source],
                device_id=where,
                device_id_type=MESH,
            ),
        )

    @pl.when(is_worker)
    def _():
        field_ref[...] = jnp.zeros_like(field_ref)
        slot_index = lax.broadcasted_iota(jnp.int32, (1, slots), 1)
        row_iota = lax.broadcasted_iota(jnp.int32, (PATCH, slots), 0)
        col_iota = lax.broadcasted_iota(jnp.int32, (cols, slots), 0)

        @pl.loop(0, rows // PATCH)
        def _(a):
            @pl.loop(0, patch_cols)
            def _(b):
                p = a * patch_cols + b
                spot = spot_ref[pl.ds(p, 1), :]
                live = slot_index < alive_ref[p]
                spread = jnp.where(live, spread_ref[pl.ds(p, 1), :], 0.0)
                weight = spread.astype(bf16).astype(f32)
                level = spread * heat_ref[pl.ds(p, 1), :]
                parts = [weight]
                for value in (level, spread):
                    for _ in range(3):
                        part = value.astype(bf16).astype(f32)
                        parts.append(part)
                        value = value - part
                in_row = row_iota == lax.shift_right_logical(spot, 4)
                in_col = col_iota == (spot & (PATCH - 1)) + b * PATCH
                left = jnp.concatenate([jnp.where(in_row, part, 0.0) for part in parts], axis=0)
                right = jnp.where(in_col, 1.0, 0.0).astype(bf16)
                sums = lax.dot_general(left.astype(bf16), right, NT, preferred_element_type=f32)
                base = pl.multiple_of(a * PATCH, PATCH)
                for q, chosen in enumerate(((0,), (3, 2, 1), (6, 5, 4))):
                    total = field_ref[pl.ds(q * rows + base, PATCH), :]
                    for c in chosen:
                        total = total + sums[c * PATCH : (c + 1) * PATCH]
                    field_ref[pl.ds(q * rows + base, PATCH), :] = total

        for k in range(groups):
            table = field_ref[pl.ds(k * WORKERS + mine, 8, stride=rows), :]
            wsend_ref[k] = table
            wcells_ref[HALO + k] = table

        @pl.when(has_below)
        def _():
            weight_copy(1).start()

        @pl.when(near_above)
        def _():
            weight_copy(2).start()

        @pl.when(is_upper)
        def _():
            relay_weights().start()

        @pl.when(is_relay)
        def _():
            relay_weights().wait_recv()
            forward_weights().start()

        for k in range(groups):
            cells_ref[HALO + k, lag] = send_ref[mine, k]

        @pl.when(tile == 0)
        def _():
            cells_ref[0:HALO] = jnp.zeros((HALO, lags, share, cols), bf16)
            wcells_ref[0:HALO] = jnp.zeros((HALO, 8, cols), f32)

        @pl.when(tile == tiles - 1)
        def _():
            cells_ref[HALO + groups :] = jnp.zeros((HALO, lags, share, cols), bf16)
            wcells_ref[HALO + groups :] = jnp.zeros((HALO, 8, cols), f32)

    row_major = lax.broadcasted_iota(jnp.int32, (share * rows, share * rows), 0)
    member_major = lax.broadcasted_iota(jnp.int32, (share * rows, share * rows), 1)
    wanted = lax.rem(row_major, share) * rows + row_major // share
    turn_ref[...] = jnp.where(member_major == wanted, 1.0, 0.0).astype(bf16)

    loads[6].wait()

    def lift(m, total):
        for n in range(8):
            total = total + hist_ref[8 * m + n].astype(f32)
        return total

    mean = lax.fori_loop(0, members // 8, lift, jnp.zeros((rows, cols), f32)) / members
    mean_ref[...] = mean

    @pl.loop(0, members // 8)
    def _(m):
        for n in range(8):
            hist_ref[8 * m + n] = (hist_ref[8 * m + n].astype(f32) - mean).astype(bf16)

    @pl.loop(0, members // (2 * share))
    def _(g):
        first = hist_ref[pl.ds(2 * share * g, share)].reshape(share * rows, cols)
        second = hist_ref[pl.ds(2 * share * g + share, share)].reshape(share * rows, cols)
        pair = jnp.concatenate([first, second], axis=1)
        turned = jnp.dot(turn_ref[...], pair, preferred_element_type=f32)
        turned = turned.reshape(rows, share, 2 * cols)
        turned = jnp.concatenate([turned[:, :, :cols], turned[:, :, cols:]], axis=1)
        start = pl.multiple_of(2 * share * g, 2 * share)
        turned_ref[:, pl.ds(start, 2 * share), :] = turned.astype(bf16)


    @pl.when(is_worker)
    def _():
        sub = lax.broadcasted_iota(jnp.int32, (patch_cols, cols), 0)
        lane = lax.broadcasted_iota(jnp.int32, (patch_cols, cols), 1)
        col_offset = (lane - PATCH * sub).astype(f32) - 7.5
        col_square = col_offset * col_offset
        squares = []
        for a in range(2):
            radius = jnp.zeros((patch_cols, cols), f32)
            for b in range(patch_cols):
                value = radius_ref[a * patch_cols + b].astype(f32)
                radius = jnp.where(sub == b, value, radius)
            squares.append(radius * radius)

        acc_ref[...] = jnp.zeros_like(acc_ref)
        half = patch_cols // 2

        def accumulate(begin, count):
            wides, anomalies, scales, weighteds = [], [], [], []
            for n in range(count):
                j = begin + n
                values = cells_ref[j].astype(f32).reshape(members, cols)
                average = jnp.sum(values, axis=0, keepdims=True) / members
                anomaly = (values - average).astype(bf16)
                anomalies.append(anomaly)
                wides.append(anomaly.astype(f32))
                table = wcells_ref[j]
                innovation = table[1:2] - table[2:3] * average
                for a in range(2):
                    row_offset = (WORKERS * j - PATCH * a - 24 + mine).astype(f32) - 7.5
                    taper = 1.0 - (row_offset * row_offset + col_square) / squares[a]
                    taper = jnp.maximum(0.0, taper)
                    taper = taper * taper
                    both = taper[:half] + taper[half:]
                    scales.append(both * table[0:1])
                    weighteds.append(both * innovation)
            for b in range(half):
                near = lane[:1] < PATCH * b + 40
                near, far = (
                    jnp.where(near, 1.0, 0.0).astype(bf16),
                    jnp.where(near, 0.0, 1.0).astype(bf16),
                )
                lefts, rights = [], []
                for n in range(count):
                    column = []
                    for a in range(2):
                        scale, weighted = scales[2 * n + a], weighteds[2 * n + a]
                        column.append((wides[n] * scale[b : b + 1]).astype(bf16))
                        extra = jnp.where(sub == 0, weighted[b : b + 1], 0.0)
                        extra = jnp.concatenate([extra, jnp.zeros_like(extra)], axis=0)
                        column.append(extra.astype(bf16))
                    lefts.append(jnp.concatenate(column, axis=0))
                    rights.append(
                        jnp.concatenate([anomalies[n] * near, anomalies[n] * far], axis=0)
                    )
                left = jnp.concatenate(lefts, axis=1)
                right = jnp.concatenate(rights, axis=1)
                acc_ref[b] += lax.dot_general(left, right, NT, preferred_element_type=f32)

        for source in range(lags):

            @pl.when(source != lag)
            def _():
                sides(0, source).wait_recv()

        @pl.when(near_below)
        def _():
            halo_copy(1).start()

        @pl.when(near_above)
        def _():
            halo_copy(2).start()

        @pl.loop(0, 2)
        def _(n):
            accumulate(HALO + n * (groups // 2), groups // 2)

        @pl.loop(0, 2)
        def _(turn):
            side = jnp.where(tile < tiles // 2, turn, 1 - turn)

            @pl.when(jnp.logical_and(side == 0, near_above))
            def _():
                halo_copy(1).wait_recv()

            @pl.when(jnp.logical_and(side == 0, is_upper))
            def _():
                for source in range(lags):
                    sides(1, source).wait_recv()

            @pl.when(jnp.logical_and(side == 0, has_above))
            def _():
                weight_copy(1).wait_recv()

            @pl.when(jnp.logical_and(side == 1, near_below))
            def _():
                halo_copy(2).wait_recv()

            @pl.when(jnp.logical_and(side == 1, is_lower))
            def _():
                for source in range(lags):
                    sides(2, source).wait_recv()

            @pl.when(jnp.logical_and(side == 1, has_below))
            def _():
                weight_copy(2).wait_recv()

            accumulate(side * (HALO + groups), HALO)

        for worker in range(WORKERS):
            for a in range(2):
                base = a * block_rows
                gsend_ref[worker, a] = acc_ref[worker, base : base + members].astype(bf16)
                rsend_ref[worker, a : a + 1] = acc_ref[
                    worker, base + members : base + members + 1
                ]

        for worker in range(WORKERS):

            @pl.when(worker != mine)
            def _():
                for copy in gram_copies(worker, mine):
                    copy.start()

        gram_ref[mine] = gsend_ref[mine]
        rhs_ref[mine] = rsend_ref[mine]

    def transform_copy(target_lag, worker):
        return pltpu.make_async_remote_copy(
            src_ref=tsend_ref,
            dst_ref=trans_ref.at[worker],
            send_sem=tsend_sem.at[target_lag],
            recv_sem=trecv_sem.at[worker],
            device_id=place(tile, target_lag),
            device_id_type=MESH,
        )

    @pl.when(is_worker)
    def _():
        for source in range(WORKERS):

            @pl.when(source != mine)
            def _():
                for copy in gram_copies(0, source):
                    copy.wait_recv()

        row = lax.broadcasted_iota(jnp.int32, (members, 2 * members), 0)
        column = lax.broadcasted_iota(jnp.int32, (members, 2 * members), 1)
        identity = (row == lax.rem(column, members)).astype(f32)
        is_low = column[:1] < members
        low = jnp.where(is_low, 1.0, 0.0).astype(bf16)
        high = jnp.where(is_low, 0.0, 1.0).astype(bf16)

        def pick(values):
            return jnp.where(is_low, values[0], values[1])

        def lane_sums(x):
            return [
                jnp.sum(x[:, n * members : (n + 1) * members], axis=1, keepdims=True)
                for n in range(2)
            ]

        iterates, roots, bounds, rights_ = [], [], [], []
        for a in range(2):
            gram = gram_ref[0, a].astype(f32)
            rhs = rhs_ref[0, a : a + 1]
            for source in range(1, WORKERS):
                gram = gram + gram_ref[source, a].astype(f32)
                rhs = rhs + rhs_ref[source, a : a + 1]
            squares_ = lane_sums(jnp.sum(gram * gram, axis=0, keepdims=True))
            bound = members - 1.0 + jnp.sqrt(pick(squares_))
            bounds.append(bound)
            rights_.append(rhs)
            iterates.append((gram + (members - 1.0) * identity) / bound)
        roots = [1.5 * identity - 0.5 * iterate for iterate in iterates]
        iterates = [product(y, root, low, high) for y, root in zip(iterates, roots)]
        for sweep in range(1, NS_STEPS):
            corrections = [
                1.5 * identity - 0.5 * product(root, y, low, high)
                for root, y in zip(roots, iterates)
            ]
            if sweep < NS_STEPS - 1:
                iterates = [product(y, c, low, high) for y, c in zip(iterates, corrections)]
            roots = [product(c, root, low, high) for c, root in zip(corrections, roots)]
        for a in range(2):
            root, bound = roots[a], bounds[a]
            inner = pick(lane_sums(root * rights_[a]))
            weights = jnp.sum(root * inner, axis=0, keepdims=True) / bound
            factor = jnp.sqrt(jnp.full_like(bound, members - 1.0)) / jnp.sqrt(bound)
            tsend_ref[a] = (factor * root + weights).astype(bf16)

        for target in (0, lags - 1, 1, lags - 2, 2, lags - 3, 3, lags - 4):

            @pl.when(target != lag)
            def _():
                transform_copy(target, mine).start()

        trans_ref[mine] = tsend_ref[...]

    lane_patch = lax.broadcasted_iota(jnp.int32, (members, cols), 1) // PATCH
    half_rows = rows // 2

    @pl.loop(0, WORKERS)
    def _(step):
        near = jnp.where(is_worker, mine, jnp.where(lag < first, 0, WORKERS - 1))
        worker = jnp.where(
            is_worker, lax.rem(near + step, WORKERS), jnp.where(lag < first, step, near - step)
        )

        @pl.when(worker != mine)
        def _():
            transform_copy(lag, worker).wait_recv()

        mine_low = lane_patch == worker
        mine_high = lane_patch == worker + WORKERS
        mask = jnp.logical_or(mine_low, mine_high)
        low = jnp.where(mine_low[:1], 1.0, 0.0).astype(bf16)
        high = jnp.where(mine_high[:1], 1.0, 0.0).astype(bf16)
        for a in range(2):
            block = trans_ref[worker, a]

            @pl.loop(0, half_rows // 2, unroll=8)
            def _(i):
                rights = []
                for n in range(2):
                    state = turned_ref[a * half_rows + 2 * i + n]
                    rights.append(jnp.concatenate([state * low, state * high], axis=0))
                right = jnp.concatenate(rights, axis=1)
                mixed = jnp.dot(block, right, preferred_element_type=f32)
                for n in range(2):
                    r = a * half_rows + 2 * i + n
                    value = mixed[:, n * cols : (n + 1) * cols] + mean_ref[pl.ds(r, 1), :]
                    pltpu.store(mixed_ref.at[r], value, mask=mask)

    @pl.loop(0, rows, unroll=4)
    def _(r):
        out_ref[r] = mixed_ref[r].astype(bf16)

    @pl.when(is_lower)
    def _():
        for worker in range(WORKERS):
            cell_copy(1, worker, lag).wait_send()

    @pl.when(is_upper)
    def _():
        relay_copy().wait_send()

    @pl.when(is_relay)
    def _():
        for worker in range(WORKERS):
            forward_copy(worker).wait_send()

    for worker in range(WORKERS):

        @pl.when(worker != mine)
        def _():
            cell_copy(0, worker, lag).wait_send()

    @pl.when(is_worker)
    def _():
        @pl.when(has_below)
        def _():
            weight_copy(1).wait_send()

        @pl.when(near_above)
        def _():
            weight_copy(2).wait_send()
            halo_copy(2).wait_send()

        @pl.when(near_below)
        def _():
            halo_copy(1).wait_send()

        @pl.when(is_upper)
        def _():
            relay_weights().wait_send()

        @pl.when(is_relay)
        def _():
            forward_weights().wait_send()

        for worker in range(WORKERS):

            @pl.when(worker != mine)
            def _():
                for copy in gram_copies(worker, mine):
                    copy.wait_send()

        for target in range(lags):

            @pl.when(target != lag)
            def _():
                transform_copy(target, mine).wait_send()


def solution(mesh):
    tiles, lags = mesh.shape["dom"], mesh.shape["lag"]

    def shards(history, forecast, spot, alive, heat, spread, radius):
        share, rows, cols = forecast.shape
        members = share * lags
        groups = rows // WORKERS
        window = groups + 2 * HALO
        f32, bf16, dma = jnp.float32, jnp.bfloat16, pltpu.SemaphoreType.DMA
        result = pl.pallas_call(
            functools.partial(kernel, tiles, lags),
            out_shape=jax.ShapeDtypeStruct((rows, members, cols), history.dtype),
            in_specs=[pl.BlockSpec(memory_space=pltpu.HBM)] * 7,
            out_specs=pl.BlockSpec(memory_space=pltpu.VMEM),
            scratch_shapes=[
                pltpu.VMEM(forecast.shape, bf16),
                pltpu.VMEM(spot.shape, jnp.int32),
                pltpu.VMEM(heat.shape, f32),
                pltpu.VMEM(spread.shape, f32),
                pltpu.SMEM(alive.shape, jnp.int32),
                pltpu.SMEM(radius.shape, jnp.int32),
                pltpu.VMEM((members, rows, cols), bf16),
                pltpu.VMEM((rows, members, cols), f32),
                pltpu.VMEM((share * rows, share * rows), bf16),
                pltpu.VMEM((rows, cols), f32),
                pltpu.VMEM((rows, members, cols), bf16),
                pltpu.VMEM((share * rows, cols), f32),
                pltpu.VMEM((WORKERS, groups, share, cols), bf16),
                pltpu.VMEM((window, lags, share, cols), bf16),
                pltpu.VMEM((8 * rows, cols), f32),
                pltpu.VMEM((groups, 8, cols), f32),
                pltpu.VMEM((window, 8, cols), f32),
                pltpu.VMEM((WORKERS, 2 * (members + 16), 2 * members), f32),
                pltpu.VMEM((WORKERS, 2, members, 2 * members), bf16),
                pltpu.VMEM((WORKERS, 2, members, 2 * members), bf16),
                pltpu.VMEM((WORKERS, 2, 2 * members), f32),
                pltpu.VMEM((WORKERS, 2, 2 * members), f32),
                pltpu.VMEM((2, members, 2 * members), bf16),
                pltpu.VMEM((WORKERS, 2, members, 2 * members), bf16),
                pltpu.VMEM((WORKERS, HALO, share, cols), bf16),
                pltpu.VMEM((HALO, 8, cols), f32),
                dma((7,)),
                dma((3, lags)),
                dma((3, lags)),
                dma((2,)),
                dma((2,)),
                dma((lags,)),
                dma((lags,)),
                dma((lags,)),
                dma((lags,)),
                dma((lags,)),
                dma((lags,)),
                dma((2,)),
                dma((2,)),
                dma((4,)),
                dma((WORKERS + 1,)),
            ],
            compiler_params=pltpu.CompilerParams(
                collective_id=0, has_side_effects=True, vmem_limit_bytes=16 << 20
            ),
            name="smoother",
        )(
            *(
                pltpu.with_memory_space_constraint(x, pltpu.HBM)
                for x in (forecast, spot, heat, spread, alive, radius, history)
            )
        )
        return jnp.transpose(result, (1, 0, 2))[None]

    in_specs = (
        P("lag", None, "dom", None),
        P("lag", "dom", None),
        P("dom", None),
        P("dom"),
        P("dom", None),
        P("dom", None),
        P("dom"),
    )
    out_specs = P("lag", None, "dom", None)
    return jax.shard_map(shards, mesh=mesh, in_specs=in_specs, out_specs=out_specs, check_vma=False)
```

```python
import functools

import jax
import jax.numpy as jnp
from jax import lax
from jax.experimental import pallas as pl
from jax.experimental.pallas import tpu as pltpu
from jax.sharding import PartitionSpec as P

PATCH = 16
NS_STEPS = 4
WORKERS = 4
HALO = 24 // WORKERS
MESH = pl.DeviceIdType.MESH
NT = (((1,), (1,)), ((), ()))


def split2(x):
    high = x.astype(jnp.bfloat16)
    return high, (x - high.astype(jnp.float32)).astype(jnp.bfloat16)


def product(x, y, low, high):
    xh, xl = split2(x)
    yh, yl = split2(y)
    yh = jnp.concatenate([yh * low, yh * high], axis=0)
    yl = jnp.concatenate([yl * low, yl * high], axis=0)
    dot = functools.partial(jnp.dot, preferred_element_type=jnp.float32)
    wide = dot(jnp.concatenate([xh, xl], axis=1), jnp.concatenate([yh, yh], axis=0))
    return wide + dot(xh, yl)


def kernel(
    tiles,
    lags,
    fore_hbm,
    spot_hbm,
    heat_hbm,
    spread_hbm,
    alive_hbm,
    radius_hbm,
    hist_hbm,
    out_ref,
    fore_ref,
    spot_ref,
    heat_ref,
    spread_ref,
    alive_ref,
    radius_ref,
    hist_ref,
    turn_ref,
    mean_ref,
    turned_ref,
    fore32_ref,
    send_ref,
    cells_ref,
    field_ref,
    wsend_ref,
    wcells_ref,
    acc_ref,
    gsend_ref,
    gram_ref,
    rsend_ref,
    rhs_ref,
    tsend_ref,
    trans_ref,
    relay_ref,
    wrelay_ref,
    down_ref,
    wdown_ref,
    load_sem,
    send_sem,
    recv_sem,
    wsend_sem,
    wrecv_sem,
    gsend_sem,
    grecv_sem,
    rsend_sem,
    rrecv_sem,
    tsend_sem,
    trecv_sem,
    hsend_sem,
    hrecv_sem,
    relay_sem,
    forward_sem,
    down_sem,
    onward_sem,
):
    tile = lax.axis_index("dom")
    lag = lax.axis_index("lag")
    share, rows, cols = fore_ref.shape
    members = share * lags
    groups = rows // WORKERS
    patch_cols = cols // PATCH
    slots = spot_ref.shape[1]
    block_rows = members + 16
    first = lags // 2 - WORKERS // 2
    f32, bf16 = jnp.float32, jnp.bfloat16
    has_below = tile < tiles - 1
    has_above = tile > 0
    seam = tiles // 2
    is_lower = tile == seam - 1
    is_upper = tile == seam
    is_last = tile == tiles - 1
    at_seam = jnp.logical_or(is_lower, is_upper)
    middle = lags // 2
    is_end = jnp.logical_and(is_last, jnp.logical_or(lag == 0, lag == lags - 1))
    end_lag = jnp.where(lag < middle, lags - 1, 0)
    end_base = jnp.where(lag == 0, middle, 0)
    near_below = jnp.logical_and(has_below, tile != seam - 1)
    near_above = jnp.logical_and(has_above, tile != seam)
    mine = lag - first
    is_worker = jnp.logical_and(mine >= 0, mine < WORKERS)

    def place(target_tile, target_lag):
        return {"dom": target_tile, "lag": target_lag}

    loads = [
        pltpu.make_async_copy(source, target, load_sem.at[n])
        for n, (source, target) in enumerate(
            (
                (fore_hbm, fore_ref),
                (alive_hbm, alive_ref),
                (radius_hbm, radius_ref),
                (spot_hbm, spot_ref),
                (spread_hbm, spread_ref),
                (heat_hbm, heat_ref),
                (hist_hbm.at[0], hist_ref),
            )
        )
    ]

    barrier = pltpu.get_barrier_semaphore()

    def greet(target_tile, target_lag):
        pl.semaphore_signal(
            barrier, inc=1, device_id=place(target_tile, target_lag), device_id_type=MESH
        )

    @pl.when(is_worker)
    def _():
        @pl.when(is_lower)
        def _():
            for target in range(lags):
                greet(tiles - 1, target)

        @pl.when(is_upper)
        def _():
            greet(tiles - 1, 0)
            greet(tiles - 1, lags - 1)

        for step in range(1, lags):
            greet(tile, lax.rem(lag + step, lags))

        @pl.when(near_above)
        def _():
            greet(tile - 1, lag)

        @pl.when(near_below)
        def _():
            greet(tile + 1, lag)

    @pl.when(is_last)
    def _():
        greet(seam, lag)

    @pl.when(is_end)
    def _():
        for n in range(middle):
            greet(seam - 1, end_base + n)

    for load in loads:
        load.start()

    loads[0].wait()
    for m in range(share):
        fore32_ref[m * rows : (m + 1) * rows, :] = fore_ref[m].astype(f32)
    for target in range(WORKERS):
        for k in range(groups):
            row = k * WORKERS + target
            send_ref[target, k] = fore32_ref[pl.ds(row, share, stride=rows), :].astype(bf16)

    def weight_sums():
        for load in loads[1:6]:
            load.wait()

        field_ref[...] = jnp.zeros_like(field_ref)
        slot_index = lax.broadcasted_iota(jnp.int32, (1, slots), 1)
        row_iota = lax.broadcasted_iota(jnp.int32, (PATCH, slots), 0)
        col_iota = lax.broadcasted_iota(jnp.int32, (cols, slots), 0)

        @pl.loop(0, rows // PATCH)
        def _(a):
            @pl.loop(0, patch_cols)
            def _(b):
                p = a * patch_cols + b
                spot = spot_ref[pl.ds(p, 1), :]
                live = slot_index < alive_ref[p]
                spread = jnp.where(live, spread_ref[pl.ds(p, 1), :], 0.0)
                weight = spread.astype(bf16).astype(f32)
                level = spread * heat_ref[pl.ds(p, 1), :]
                parts = [weight]
                for value in (level, spread):
                    for _ in range(3):
                        part = value.astype(bf16).astype(f32)
                        parts.append(part)
                        value = value - part
                in_row = row_iota == lax.shift_right_logical(spot, 4)
                in_col = col_iota == (spot & (PATCH - 1)) + b * PATCH
                left = jnp.concatenate([jnp.where(in_row, part, 0.0) for part in parts], axis=0)
                right = jnp.where(in_col, 1.0, 0.0).astype(bf16)
                sums = lax.dot_general(left.astype(bf16), right, NT, preferred_element_type=f32)
                base = pl.multiple_of(a * PATCH, PATCH)
                for q, chosen in enumerate(((0,), (3, 2, 1), (6, 5, 4))):
                    total = field_ref[pl.ds(q * rows + base, PATCH), :]
                    for c in chosen:
                        total = total + sums[c * PATCH : (c + 1) * PATCH]
                    field_ref[pl.ds(q * rows + base, PATCH), :] = total

        for k in range(groups):
            table = field_ref[pl.ds(k * WORKERS + mine, 8, stride=rows), :]
            wsend_ref[k] = table
            wcells_ref[HALO + k] = table

    @pl.when(jnp.logical_and(is_worker, at_seam))
    def _():
        weight_sums()

    pl.semaphore_wait(
        barrier,
        WORKERS
        - jnp.where(is_worker, 1, 0)
        + jnp.where(jnp.logical_and(is_worker, near_above), 1, 0)
        + jnp.where(jnp.logical_and(is_worker, near_below), 1, 0)
        + jnp.where(at_seam, 1, 0)
        + jnp.where(is_last, WORKERS, 0)
        + jnp.where(is_end, WORKERS, 0),
    )

    def cell_copy(kind, worker, source_lag):
        begin = groups - HALO if kind == 1 else 0
        count = groups if kind == 0 else HALO
        start = (HALO, 0, HALO + groups)[kind]
        return pltpu.make_async_remote_copy(
            src_ref=send_ref.at[worker, pl.ds(begin, count)],
            dst_ref=cells_ref.at[pl.ds(start, count), source_lag],
            send_sem=send_sem.at[kind, worker],
            recv_sem=recv_sem.at[kind, source_lag],
            device_id=place(tile + (0, 1, -1)[kind], first + worker),
            device_id_type=MESH,
        )

    def weight_copy(kind):
        begin = groups - HALO if kind == 1 else 0
        start = (HALO, 0, HALO + groups)[kind]
        return pltpu.make_async_remote_copy(
            src_ref=wsend_ref.at[pl.ds(begin, HALO)],
            dst_ref=wcells_ref.at[pl.ds(start, HALO)],
            send_sem=wsend_sem.at[kind - 1],
            recv_sem=wrecv_sem.at[kind - 1],
            device_id=place(tile + (0, 1, -1)[kind], lag),
            device_id_type=MESH,
        )

    def order(step):
        return jnp.where(lag < lags // 2, WORKERS - 1 - step, step)

    def halo_copy(kind):
        return pltpu.make_async_remote_copy(
            src_ref=cells_ref.at[pl.ds(groups if kind == 1 else HALO, HALO)],
            dst_ref=cells_ref.at[pl.ds(0 if kind == 1 else HALO + groups, HALO)],
            send_sem=hsend_sem.at[kind - 1],
            recv_sem=hrecv_sem.at[kind - 1],
            device_id=place(tile + (0, 1, -1)[kind], lag),
            device_id_type=MESH,
        )

    def up_copy():
        return pltpu.make_async_remote_copy(
            src_ref=send_ref.at[:, pl.ds(0, HALO)],
            dst_ref=relay_ref,
            send_sem=relay_sem.at[0],
            recv_sem=relay_sem.at[1],
            device_id=place(tiles - 1, lag),
            device_id_type=MESH,
        )

    def up_weights():
        return pltpu.make_async_remote_copy(
            src_ref=wsend_ref.at[pl.ds(0, HALO)],
            dst_ref=wrelay_ref,
            send_sem=relay_sem.at[2],
            recv_sem=relay_sem.at[3],
            device_id=place(tiles - 1, lag),
            device_id_type=MESH,
        )

    def up_forward(worker):
        return pltpu.make_async_remote_copy(
            src_ref=relay_ref.at[worker],
            dst_ref=cells_ref.at[pl.ds(HALO + groups, HALO), lag],
            send_sem=forward_sem.at[worker],
            recv_sem=recv_sem.at[2, lag],
            device_id=place(seam - 1, first + worker),
            device_id_type=MESH,
        )

    def up_forward_weights():
        return pltpu.make_async_remote_copy(
            src_ref=wrelay_ref,
            dst_ref=wcells_ref.at[pl.ds(HALO + groups, HALO)],
            send_sem=forward_sem.at[WORKERS],
            recv_sem=wrecv_sem.at[1],
            device_id=place(seam - 1, lag),
            device_id_type=MESH,
        )

    def down_copy(source):
        return pltpu.make_async_remote_copy(
            src_ref=send_ref.at[:, pl.ds(groups - HALO, HALO)],
            dst_ref=down_ref.at[source],
            send_sem=relay_sem.at[0],
            recv_sem=down_sem.at[0, source],
            device_id=place(tiles - 1, end_lag),
            device_id_type=MESH,
        )

    def down_weights(source):
        return pltpu.make_async_remote_copy(
            src_ref=wsend_ref.at[pl.ds(groups - HALO, HALO)],
            dst_ref=wdown_ref.at[source],
            send_sem=relay_sem.at[2],
            recv_sem=down_sem.at[1, source],
            device_id=place(tiles - 1, end_lag),
            device_id_type=MESH,
        )

    def down_forward(source, worker):
        return pltpu.make_async_remote_copy(
            src_ref=down_ref.at[source, worker],
            dst_ref=cells_ref.at[pl.ds(0, HALO), source],
            send_sem=onward_sem.at[source, worker],
            recv_sem=recv_sem.at[1, source],
            device_id=place(seam, first + worker),
            device_id_type=MESH,
        )

    def down_forward_weights(source):
        return pltpu.make_async_remote_copy(
            src_ref=wdown_ref.at[source],
            dst_ref=wcells_ref.at[pl.ds(0, HALO)],
            send_sem=onward_sem.at[source, WORKERS],
            recv_sem=wrecv_sem.at[0],
            device_id=place(seam, source),
            device_id_type=MESH,
        )

    @pl.when(is_lower)
    def _():
        down_copy(lag).start()

    @pl.when(is_upper)
    def _():
        up_copy().start()

    for step in range(WORKERS):
        worker = order(step)

        @pl.when(worker != mine)
        def _():
            cell_copy(0, worker, lag).start()

    def sides(kind, source_lag):
        return cell_copy(kind, 0, source_lag)

    def gram_copies(worker, source):
        where = place(tile, first + worker)
        return (
            pltpu.make_async_remote_copy(
                src_ref=gsend_ref.at[worker],
                dst_ref=gram_ref.at[source],
                send_sem=gsend_sem.at[worker],
                recv_sem=grecv_sem.at[source],
                device_id=where,
                device_id_type=MESH,
            ),
            pltpu.make_async_remote_copy(
                src_ref=rsend_ref.at[worker],
                dst_ref=rhs_ref.at[source],
                send_sem=rsend_sem.at[worker],
                recv_sem=rrecv_sem.at[source],
                device_id=where,
                device_id_type=MESH,
            ),
        )

    @pl.when(jnp.logical_and(is_worker, jnp.logical_not(at_seam)))
    def _():
        weight_sums()

    @pl.when(jnp.logical_not(is_worker))
    def _():
        for load in loads[1:6]:
            load.wait()

    @pl.when(is_worker)
    def _():
        @pl.when(near_below)
        def _():
            weight_copy(1).start()

        @pl.when(near_above)
        def _():
            weight_copy(2).start()

        @pl.when(is_lower)
        def _():
            down_weights(lag).start()

        @pl.when(is_upper)
        def _():
            up_weights().start()

        for k in range(groups):
            cells_ref[HALO + k, lag] = send_ref[mine, k]

        @pl.when(tile == 0)
        def _():
            cells_ref[0:HALO] = jnp.zeros((HALO, lags, share, cols), bf16)
            wcells_ref[0:HALO] = jnp.zeros((HALO, 8, cols), f32)

        @pl.when(tile == tiles - 1)
        def _():
            cells_ref[HALO + groups :] = jnp.zeros((HALO, lags, share, cols), bf16)
            wcells_ref[HALO + groups :] = jnp.zeros((HALO, 8, cols), f32)

    @pl.when(is_last)
    def _():
        up_copy().wait_recv()
        for step in range(WORKERS):
            up_forward(order(step)).start()

        @pl.when(is_worker)
        def _():
            up_weights().wait_recv()
            up_forward_weights().start()

    def sends_weights(source):
        return jnp.logical_and(source >= first, source < first + WORKERS)

    @pl.when(is_end)
    def _():
        @pl.loop(0, middle)
        def _(n):
            source = end_base + n
            down_copy(source).wait_recv()
            for worker in range(WORKERS):
                down_forward(source, worker).start()

            @pl.when(sends_weights(source))
            def _():
                down_weights(source).wait_recv()
                down_forward_weights(source).start()

    row_major = lax.broadcasted_iota(jnp.int32, (share * rows, share * rows), 0)
    member_major = lax.broadcasted_iota(jnp.int32, (share * rows, share * rows), 1)
    wanted = lax.rem(row_major, share) * rows + row_major // share
    turn_ref[...] = jnp.where(member_major == wanted, 1.0, 0.0).astype(bf16)

    @pl.loop(0, rows)
    def _(r):
        out_ref[r] = jnp.zeros((members, cols), bf16)

    loads[6].wait()

    def lift(m, total):
        for n in range(8):
            total = total + hist_ref[8 * m + n].astype(f32)
        return total

    mean = lax.fori_loop(0, members // 8, lift, jnp.zeros((rows, cols), f32)) / members
    mean_ref[...] = mean

    @pl.loop(0, members // 8)
    def _(m):
        for n in range(8):
            hist_ref[8 * m + n] = (hist_ref[8 * m + n].astype(f32) - mean).astype(bf16)

    @pl.loop(0, members // (2 * share))
    def _(g):
        first = hist_ref[pl.ds(2 * share * g, share)].reshape(share * rows, cols)
        second = hist_ref[pl.ds(2 * share * g + share, share)].reshape(share * rows, cols)
        pair = jnp.concatenate([first, second], axis=1)
        turned = jnp.dot(turn_ref[...], pair, preferred_element_type=f32)
        turned = turned.reshape(rows, share, 2 * cols)
        turned = jnp.concatenate([turned[:, :, :cols], turned[:, :, cols:]], axis=1)
        start = pl.multiple_of(2 * share * g, 2 * share)
        turned_ref[:, pl.ds(start, 2 * share), :] = turned.astype(bf16)


    @pl.when(is_worker)
    def _():
        sub = lax.broadcasted_iota(jnp.int32, (patch_cols, cols), 0)
        lane = lax.broadcasted_iota(jnp.int32, (patch_cols, cols), 1)
        col_offset = (lane - PATCH * sub).astype(f32) - 7.5
        col_square = col_offset * col_offset
        squares = []
        for a in range(2):
            radius = jnp.zeros((patch_cols, cols), f32)
            for b in range(patch_cols):
                value = radius_ref[a * patch_cols + b].astype(f32)
                radius = jnp.where(sub == b, value, radius)
            squares.append(radius * radius)

        acc_ref[...] = jnp.zeros_like(acc_ref)
        half = patch_cols // 2

        def accumulate(begin, count):
            wides, anomalies, scales, weighteds = [], [], [], []
            for n in range(count):
                j = begin + n
                values = cells_ref[j].astype(f32).reshape(members, cols)
                average = jnp.sum(values, axis=0, keepdims=True) / members
                anomaly = (values - average).astype(bf16)
                anomalies.append(anomaly)
                wides.append(anomaly.astype(f32))
                table = wcells_ref[j]
                innovation = table[1:2] - table[2:3] * average
                for a in range(2):
                    row_offset = (WORKERS * j - PATCH * a - 24 + mine).astype(f32) - 7.5
                    taper = 1.0 - (row_offset * row_offset + col_square) / squares[a]
                    taper = jnp.maximum(0.0, taper)
                    taper = taper * taper
                    both = taper[:half] + taper[half:]
                    scales.append(both * table[0:1])
                    weighteds.append(both * innovation)
            for b in range(half):
                near = lane[:1] < PATCH * b + 40
                near, far = (
                    jnp.where(near, 1.0, 0.0).astype(bf16),
                    jnp.where(near, 0.0, 1.0).astype(bf16),
                )
                lefts, rights = [], []
                for n in range(count):
                    column = []
                    for a in range(2):
                        scale, weighted = scales[2 * n + a], weighteds[2 * n + a]
                        column.append((wides[n] * scale[b : b + 1]).astype(bf16))
                        extra = jnp.where(sub == 0, weighted[b : b + 1], 0.0)
                        extra = jnp.concatenate([extra, jnp.zeros_like(extra)], axis=0)
                        column.append(extra.astype(bf16))
                    lefts.append(jnp.concatenate(column, axis=0))
                    rights.append(
                        jnp.concatenate([anomalies[n] * near, anomalies[n] * far], axis=0)
                    )
                left = jnp.concatenate(lefts, axis=1)
                right = jnp.concatenate(rights, axis=1)
                acc_ref[b] += lax.dot_general(left, right, NT, preferred_element_type=f32)

        for source in range(lags):

            @pl.when(source != lag)
            def _():
                sides(0, source).wait_recv()

        @pl.when(near_below)
        def _():
            halo_copy(1).start()

        @pl.when(near_above)
        def _():
            halo_copy(2).start()

        @pl.loop(0, 2)
        def _(n):
            accumulate(HALO + n * (groups // 2), groups // 2)

        @pl.loop(0, 2)
        def _(turn):
            side = jnp.where(tile < tiles // 2, turn, 1 - turn)

            @pl.when(jnp.logical_and(side == 0, near_above))
            def _():
                halo_copy(1).wait_recv()

            @pl.when(jnp.logical_and(side == 0, is_upper))
            def _():
                for source in range(lags):
                    sides(1, source).wait_recv()

            @pl.when(jnp.logical_and(side == 0, has_above))
            def _():
                weight_copy(1).wait_recv()

            @pl.when(jnp.logical_and(side == 1, near_below))
            def _():
                halo_copy(2).wait_recv()

            @pl.when(jnp.logical_and(side == 1, is_lower))
            def _():
                for source in range(lags):
                    sides(2, source).wait_recv()

            @pl.when(jnp.logical_and(side == 1, has_below))
            def _():
                weight_copy(2).wait_recv()

            accumulate(side * (HALO + groups), HALO)

        for worker in range(WORKERS):
            for a in range(2):
                base = a * block_rows
                gsend_ref[worker, a] = acc_ref[worker, base : base + members].astype(bf16)
                rsend_ref[worker, a : a + 1] = acc_ref[
                    worker, base + members : base + members + 1
                ]

        for worker in range(WORKERS):

            @pl.when(worker != mine)
            def _():
                for copy in gram_copies(worker, mine):
                    copy.start()

        gram_ref[mine] = gsend_ref[mine]
        rhs_ref[mine] = rsend_ref[mine]

    def transform_copy(target_lag, worker):
        return pltpu.make_async_remote_copy(
            src_ref=tsend_ref,
            dst_ref=trans_ref.at[worker],
            send_sem=tsend_sem.at[target_lag],
            recv_sem=trecv_sem.at[worker],
            device_id=place(tile, target_lag),
            device_id_type=MESH,
        )

    @pl.when(is_worker)
    def _():
        for source in range(WORKERS):

            @pl.when(source != mine)
            def _():
                for copy in gram_copies(0, source):
                    copy.wait_recv()

        row = lax.broadcasted_iota(jnp.int32, (members, 2 * members), 0)
        column = lax.broadcasted_iota(jnp.int32, (members, 2 * members), 1)
        identity = (row == lax.rem(column, members)).astype(f32)
        is_low = column[:1] < members
        low = jnp.where(is_low, 1.0, 0.0).astype(bf16)
        high = jnp.where(is_low, 0.0, 1.0).astype(bf16)

        def pick(values):
            return jnp.where(is_low, values[0], values[1])

        def lane_sums(x):
            return [
                jnp.sum(x[:, n * members : (n + 1) * members], axis=1, keepdims=True)
                for n in range(2)
            ]

        iterates, roots, bounds, rights_ = [], [], [], []
        for a in range(2):
            gram = gram_ref[0, a].astype(f32)
            rhs = rhs_ref[0, a : a + 1]
            for source in range(1, WORKERS):
                gram = gram + gram_ref[source, a].astype(f32)
                rhs = rhs + rhs_ref[source, a : a + 1]
            squares_ = lane_sums(jnp.sum(gram * gram, axis=0, keepdims=True))
            bound = members - 1.0 + jnp.sqrt(pick(squares_))
            bounds.append(bound)
            rights_.append(rhs)
            iterates.append((gram + (members - 1.0) * identity) / bound)
        roots = [1.5 * identity - 0.5 * iterate for iterate in iterates]
        iterates = [product(y, root, low, high) for y, root in zip(iterates, roots)]
        for sweep in range(1, NS_STEPS):
            corrections = [
                1.5 * identity - 0.5 * product(root, y, low, high)
                for root, y in zip(roots, iterates)
            ]
            if sweep < NS_STEPS - 1:
                iterates = [product(y, c, low, high) for y, c in zip(iterates, corrections)]
            roots = [product(c, root, low, high) for c, root in zip(corrections, roots)]
        for a in range(2):
            root, bound = roots[a], bounds[a]
            inner = pick(lane_sums(root * rights_[a]))
            weights = jnp.sum(root * inner, axis=0, keepdims=True) / bound
            factor = jnp.sqrt(jnp.full_like(bound, members - 1.0)) / jnp.sqrt(bound)
            tsend_ref[a] = (factor * root + weights).astype(bf16)

        for target in (0, lags - 1, 1, lags - 2, 2, lags - 3, 3, lags - 4):

            @pl.when(target != lag)
            def _():
                transform_copy(target, mine).start()

        trans_ref[mine] = tsend_ref[...]

    lane_patch = lax.broadcasted_iota(jnp.int32, (members, cols), 1) // PATCH
    half_rows = rows // 2

    @pl.loop(0, WORKERS)
    def _(step):
        near = jnp.where(is_worker, mine, jnp.where(lag < first, 0, WORKERS - 1))
        worker = jnp.where(
            is_worker, lax.rem(near + step, WORKERS), jnp.where(lag < first, step, near - step)
        )

        @pl.when(worker != mine)
        def _():
            transform_copy(lag, worker).wait_recv()

        mine_low = lane_patch == worker
        mine_high = lane_patch == worker + WORKERS
        mask = jnp.logical_or(mine_low, mine_high)
        low = jnp.where(mine_low[:1], 1.0, 0.0).astype(bf16)
        high = jnp.where(mine_high[:1], 1.0, 0.0).astype(bf16)
        for a in range(2):
            block = trans_ref[worker, a]

            @pl.loop(0, half_rows // 2, unroll=8)
            def _(i):
                rights = []
                for n in range(2):
                    state = turned_ref[a * half_rows + 2 * i + n]
                    rights.append(jnp.concatenate([state * low, state * high], axis=0))
                right = jnp.concatenate(rights, axis=1)
                mixed = jnp.dot(block, right, preferred_element_type=f32)
                for n in range(2):
                    r = a * half_rows + 2 * i + n
                    value = mixed[:, n * cols : (n + 1) * cols] + mean_ref[pl.ds(r, 1), :]
                    out_ref[r] = jnp.where(mask, value.astype(bf16), out_ref[r])

    @pl.when(is_lower)
    def _():
        down_copy(lag).wait_send()

        @pl.when(is_worker)
        def _():
            down_weights(lag).wait_send()

    @pl.when(is_upper)
    def _():
        up_copy().wait_send()

        @pl.when(is_worker)
        def _():
            up_weights().wait_send()

    @pl.when(is_last)
    def _():
        for worker in range(WORKERS):
            up_forward(worker).wait_send()

        @pl.when(is_worker)
        def _():
            up_forward_weights().wait_send()

    @pl.when(is_end)
    def _():
        @pl.loop(0, middle)
        def _(n):
            source = end_base + n
            for worker in range(WORKERS):
                down_forward(source, worker).wait_send()

            @pl.when(sends_weights(source))
            def _():
                down_forward_weights(source).wait_send()

    for worker in range(WORKERS):

        @pl.when(worker != mine)
        def _():
            cell_copy(0, worker, lag).wait_send()

    @pl.when(is_worker)
    def _():
        @pl.when(near_above)
        def _():
            weight_copy(2).wait_send()
            halo_copy(2).wait_send()

        @pl.when(near_below)
        def _():
            weight_copy(1).wait_send()
            halo_copy(1).wait_send()

        for worker in range(WORKERS):

            @pl.when(worker != mine)
            def _():
                for copy in gram_copies(worker, mine):
                    copy.wait_send()

        for target in range(lags):

            @pl.when(target != lag)
            def _():
                transform_copy(target, mine).wait_send()


def solution(mesh):
    tiles, lags = mesh.shape["dom"], mesh.shape["lag"]

    def shards(history, forecast, spot, alive, heat, spread, radius):
        share, rows, cols = forecast.shape
        members = share * lags
        groups = rows // WORKERS
        window = groups + 2 * HALO
        f32, bf16, dma = jnp.float32, jnp.bfloat16, pltpu.SemaphoreType.DMA
        result = pl.pallas_call(
            functools.partial(kernel, tiles, lags),
            out_shape=jax.ShapeDtypeStruct((rows, members, cols), history.dtype),
            in_specs=[pl.BlockSpec(memory_space=pltpu.HBM)] * 7,
            out_specs=pl.BlockSpec(memory_space=pltpu.VMEM),
            scratch_shapes=[
                pltpu.VMEM(forecast.shape, bf16),
                pltpu.VMEM(spot.shape, jnp.int32),
                pltpu.VMEM(heat.shape, f32),
                pltpu.VMEM(spread.shape, f32),
                pltpu.SMEM(alive.shape, jnp.int32),
                pltpu.SMEM(radius.shape, jnp.int32),
                pltpu.VMEM((members, rows, cols), bf16),
                pltpu.VMEM((share * rows, share * rows), bf16),
                pltpu.VMEM((rows, cols), f32),
                pltpu.VMEM((rows, members, cols), bf16),
                pltpu.VMEM((share * rows, cols), f32),
                pltpu.VMEM((WORKERS, groups, share, cols), bf16),
                pltpu.VMEM((window, lags, share, cols), bf16),
                pltpu.VMEM((8 * rows, cols), f32),
                pltpu.VMEM((groups, 8, cols), f32),
                pltpu.VMEM((window, 8, cols), f32),
                pltpu.VMEM((WORKERS, 2 * (members + 16), 2 * members), f32),
                pltpu.VMEM((WORKERS, 2, members, 2 * members), bf16),
                pltpu.VMEM((WORKERS, 2, members, 2 * members), bf16),
                pltpu.VMEM((WORKERS, 2, 2 * members), f32),
                pltpu.VMEM((WORKERS, 2, 2 * members), f32),
                pltpu.VMEM((2, members, 2 * members), bf16),
                pltpu.VMEM((WORKERS, 2, members, 2 * members), bf16),
                pltpu.VMEM((WORKERS, HALO, share, cols), bf16),
                pltpu.VMEM((HALO, 8, cols), f32),
                pltpu.VMEM((lags, WORKERS, HALO, share, cols), bf16),
                pltpu.VMEM((lags, HALO, 8, cols), f32),
                dma((7,)),
                dma((3, lags)),
                dma((3, lags)),
                dma((2,)),
                dma((2,)),
                dma((lags,)),
                dma((lags,)),
                dma((lags,)),
                dma((lags,)),
                dma((lags,)),
                dma((lags,)),
                dma((2,)),
                dma((2,)),
                dma((4,)),
                dma((WORKERS + 1,)),
                dma((2, lags)),
                dma((lags, WORKERS + 1)),
            ],
            compiler_params=pltpu.CompilerParams(
                collective_id=0, has_side_effects=True, vmem_limit_bytes=16 << 20
            ),
            name="smoother",
        )(
            *(
                pltpu.with_memory_space_constraint(x, pltpu.HBM)
                for x in (forecast, spot, heat, spread, alive, radius, history)
            )
        )
        return jnp.transpose(result, (1, 0, 2))[None]

    in_specs = (
        P("lag", None, "dom", None),
        P("lag", "dom", None),
        P("dom", None),
        P("dom"),
        P("dom", None),
        P("dom", None),
        P("dom"),
    )
    out_specs = P("lag", None, "dom", None)
    return jax.shard_map(shards, mesh=mesh, in_specs=in_specs, out_specs=out_specs, check_vma=False)
```

```python
import functools

import jax
import jax.numpy as jnp
from jax import lax
from jax.experimental import pallas as pl
from jax.experimental.pallas import tpu as pltpu
from jax.sharding import PartitionSpec as P

PATCH = 16
NS_STEPS = 4
WORKERS = 4
HALO = 24 // WORKERS
MESH = pl.DeviceIdType.MESH
NT = (((1,), (1,)), ((), ()))


def split2(x):
    high = x.astype(jnp.bfloat16)
    return high, (x - high.astype(jnp.float32)).astype(jnp.bfloat16)


def product(x, y, low, high):
    xh, xl = split2(x)
    yh, yl = split2(y)
    yh = jnp.concatenate([yh * low, yh * high], axis=0)
    yl = jnp.concatenate([yl * low, yl * high], axis=0)
    dot = functools.partial(jnp.dot, preferred_element_type=jnp.float32)
    wide = dot(jnp.concatenate([xh, xl], axis=1), jnp.concatenate([yh, yh], axis=0))
    return wide + dot(xh, yl)


def kernel(
    tiles,
    lags,
    fore_hbm,
    spot_hbm,
    heat_hbm,
    spread_hbm,
    alive_hbm,
    radius_hbm,
    hist_hbm,
    out_ref,
    fore_ref,
    spot_ref,
    heat_ref,
    spread_ref,
    alive_ref,
    radius_ref,
    hist_ref,
    turn_ref,
    mean_ref,
    turned_ref,
    fore32_ref,
    send_ref,
    cells_ref,
    field_ref,
    wsend_ref,
    wcells_ref,
    acc_ref,
    accw_ref,
    gsend_ref,
    gram_ref,
    rsend_ref,
    rhs_ref,
    tsend_ref,
    trans_ref,
    relay_ref,
    wrelay_ref,
    down_ref,
    wdown_ref,
    load_sem,
    send_sem,
    recv_sem,
    wsend_sem,
    wrecv_sem,
    gsend_sem,
    grecv_sem,
    rsend_sem,
    rrecv_sem,
    tsend_sem,
    trecv_sem,
    hsend_sem,
    hrecv_sem,
    relay_sem,
    forward_sem,
    down_sem,
    onward_sem,
):
    tile = lax.axis_index("dom")
    lag = lax.axis_index("lag")
    share, rows, cols = fore_ref.shape
    members = share * lags
    groups = rows // WORKERS
    patch_cols = cols // PATCH
    slots = spot_ref.shape[1]
    first = lags // 2 - WORKERS // 2
    f32, bf16 = jnp.float32, jnp.bfloat16
    has_below = tile < tiles - 1
    has_above = tile > 0
    seam = tiles // 2
    is_lower = tile == seam - 1
    is_upper = tile == seam
    is_last = tile == tiles - 1
    at_seam = jnp.logical_or(is_lower, is_upper)
    middle = lags // 2
    is_end = jnp.logical_and(is_last, jnp.logical_or(lag == 0, lag == lags - 1))
    end_lag = jnp.where(lag < middle, lags - 1, 0)
    end_base = jnp.where(lag == 0, middle, 0)
    near_below = jnp.logical_and(has_below, tile != seam - 1)
    near_above = jnp.logical_and(has_above, tile != seam)
    mine = lag - first
    is_worker = jnp.logical_and(mine >= 0, mine < WORKERS)

    def place(target_tile, target_lag):
        return {"dom": target_tile, "lag": target_lag}

    loads = [
        pltpu.make_async_copy(source, target, load_sem.at[n])
        for n, (source, target) in enumerate(
            (
                (fore_hbm, fore_ref),
                (alive_hbm, alive_ref),
                (radius_hbm, radius_ref),
                (spot_hbm, spot_ref),
                (spread_hbm, spread_ref),
                (heat_hbm, heat_ref),
                (hist_hbm.at[0], hist_ref),
            )
        )
    ]

    barrier = pltpu.get_barrier_semaphore()

    def greet(target_tile, target_lag):
        pl.semaphore_signal(
            barrier, inc=1, device_id=place(target_tile, target_lag), device_id_type=MESH
        )

    @pl.when(is_worker)
    def _():
        @pl.when(is_lower)
        def _():
            for target in range(lags):
                greet(tiles - 1, target)

        @pl.when(is_upper)
        def _():
            greet(tiles - 1, 0)
            greet(tiles - 1, lags - 1)

        for step in range(1, lags):
            greet(tile, lax.rem(lag + step, lags))

        @pl.when(near_above)
        def _():
            greet(tile - 1, lag)

        @pl.when(near_below)
        def _():
            greet(tile + 1, lag)

    @pl.when(is_last)
    def _():
        greet(seam, lag)

    @pl.when(is_end)
    def _():
        for n in range(middle):
            greet(seam - 1, end_base + n)

    for load in loads:
        load.start()

    loads[0].wait()
    for m in range(share):
        fore32_ref[m * rows : (m + 1) * rows, :] = fore_ref[m].astype(f32)
    for target in range(WORKERS):
        for k in range(groups):
            row = k * WORKERS + target
            send_ref[target, k] = fore32_ref[pl.ds(row, share, stride=rows), :].astype(bf16)

    def weight_sums():
        for load in loads[1:6]:
            load.wait()

        field_ref[...] = jnp.zeros_like(field_ref)
        slot_index = lax.broadcasted_iota(jnp.int32, (1, slots), 1)
        row_iota = lax.broadcasted_iota(jnp.int32, (PATCH, slots), 0)
        col_iota = lax.broadcasted_iota(jnp.int32, (cols, slots), 0)

        @pl.loop(0, rows // PATCH)
        def _(a):
            @pl.loop(0, patch_cols)
            def _(b):
                p = a * patch_cols + b
                spot = spot_ref[pl.ds(p, 1), :]
                live = slot_index < alive_ref[p]
                spread = jnp.where(live, spread_ref[pl.ds(p, 1), :], 0.0)
                weight = spread.astype(bf16).astype(f32)
                level = spread * heat_ref[pl.ds(p, 1), :]
                parts = [weight]
                for value in (level, spread):
                    for _ in range(3):
                        part = value.astype(bf16).astype(f32)
                        parts.append(part)
                        value = value - part
                in_row = row_iota == lax.shift_right_logical(spot, 4)
                in_col = col_iota == (spot & (PATCH - 1)) + b * PATCH
                left = jnp.concatenate([jnp.where(in_row, part, 0.0) for part in parts], axis=0)
                right = jnp.where(in_col, 1.0, 0.0).astype(bf16)
                sums = lax.dot_general(left.astype(bf16), right, NT, preferred_element_type=f32)
                base = pl.multiple_of(a * PATCH, PATCH)
                for q, chosen in enumerate(((0,), (3, 2, 1), (6, 5, 4))):
                    total = field_ref[pl.ds(q * rows + base, PATCH), :]
                    for c in chosen:
                        total = total + sums[c * PATCH : (c + 1) * PATCH]
                    field_ref[pl.ds(q * rows + base, PATCH), :] = total

        for k in range(groups):
            table = field_ref[pl.ds(k * WORKERS + mine, 8, stride=rows), :]
            wsend_ref[k] = table
            wcells_ref[HALO + k] = table

    @pl.when(jnp.logical_and(is_worker, at_seam))
    def _():
        weight_sums()

    pl.semaphore_wait(
        barrier,
        WORKERS
        - jnp.where(is_worker, 1, 0)
        + jnp.where(jnp.logical_and(is_worker, near_above), 1, 0)
        + jnp.where(jnp.logical_and(is_worker, near_below), 1, 0)
        + jnp.where(at_seam, 1, 0)
        + jnp.where(is_last, WORKERS, 0)
        + jnp.where(is_end, WORKERS, 0),
    )

    def cell_copy(kind, worker, source_lag):
        begin = groups - HALO if kind == 1 else 0
        count = groups if kind == 0 else HALO
        start = (HALO, 0, HALO + groups)[kind]
        return pltpu.make_async_remote_copy(
            src_ref=send_ref.at[worker, pl.ds(begin, count)],
            dst_ref=cells_ref.at[pl.ds(start, count), source_lag],
            send_sem=send_sem.at[worker],
            recv_sem=recv_sem.at[min(kind, 1)],
            device_id=place(tile + (0, 1, -1)[kind], first + worker),
            device_id_type=MESH,
        )

    def weight_copy(kind):
        begin = groups - HALO if kind == 1 else 0
        start = (HALO, 0, HALO + groups)[kind]
        return pltpu.make_async_remote_copy(
            src_ref=wsend_ref.at[pl.ds(begin, HALO)],
            dst_ref=wcells_ref.at[pl.ds(start, HALO)],
            send_sem=wsend_sem.at[kind - 1],
            recv_sem=wrecv_sem.at[kind - 1],
            device_id=place(tile + (0, 1, -1)[kind], lag),
            device_id_type=MESH,
        )

    def order(step):
        return jnp.where(lag < lags // 2, WORKERS - 1 - step, step)

    def halo_copy(kind):
        return pltpu.make_async_remote_copy(
            src_ref=cells_ref.at[pl.ds(groups if kind == 1 else HALO, HALO)],
            dst_ref=cells_ref.at[pl.ds(0 if kind == 1 else HALO + groups, HALO)],
            send_sem=hsend_sem.at[kind - 1],
            recv_sem=hrecv_sem.at[kind - 1],
            device_id=place(tile + (0, 1, -1)[kind], lag),
            device_id_type=MESH,
        )

    def up_copy():
        return pltpu.make_async_remote_copy(
            src_ref=send_ref.at[:, pl.ds(0, HALO)],
            dst_ref=relay_ref,
            send_sem=relay_sem.at[0],
            recv_sem=relay_sem.at[1],
            device_id=place(tiles - 1, lag),
            device_id_type=MESH,
        )

    def up_weights():
        return pltpu.make_async_remote_copy(
            src_ref=wsend_ref.at[pl.ds(0, HALO)],
            dst_ref=wrelay_ref,
            send_sem=relay_sem.at[2],
            recv_sem=relay_sem.at[3],
            device_id=place(tiles - 1, lag),
            device_id_type=MESH,
        )

    def up_forward(worker):
        return pltpu.make_async_remote_copy(
            src_ref=relay_ref.at[worker],
            dst_ref=cells_ref.at[pl.ds(HALO + groups, HALO), lag],
            send_sem=forward_sem.at[0],
            recv_sem=recv_sem.at[1],
            device_id=place(seam - 1, first + worker),
            device_id_type=MESH,
        )

    def up_forward_weights():
        return pltpu.make_async_remote_copy(
            src_ref=wrelay_ref,
            dst_ref=wcells_ref.at[pl.ds(HALO + groups, HALO)],
            send_sem=forward_sem.at[1],
            recv_sem=wrecv_sem.at[1],
            device_id=place(seam - 1, lag),
            device_id_type=MESH,
        )

    def down_copy(source):
        return pltpu.make_async_remote_copy(
            src_ref=send_ref.at[:, pl.ds(groups - HALO, HALO)],
            dst_ref=down_ref.at[source],
            send_sem=relay_sem.at[0],
            recv_sem=down_sem.at[0, lax.rem(source, lags // 2)],
            device_id=place(tiles - 1, end_lag),
            device_id_type=MESH,
        )

    def down_weights(source):
        return pltpu.make_async_remote_copy(
            src_ref=wsend_ref.at[pl.ds(groups - HALO, HALO)],
            dst_ref=wdown_ref.at[source],
            send_sem=relay_sem.at[2],
            recv_sem=down_sem.at[1, lax.rem(source, lags // 2)],
            device_id=place(tiles - 1, end_lag),
            device_id_type=MESH,
        )

    def down_forward(source, worker):
        return pltpu.make_async_remote_copy(
            src_ref=down_ref.at[source, worker],
            dst_ref=cells_ref.at[pl.ds(0, HALO), source],
            send_sem=onward_sem.at[0, lax.rem(source, lags // 2)],
            recv_sem=recv_sem.at[1],
            device_id=place(seam, first + worker),
            device_id_type=MESH,
        )

    def down_forward_weights(source):
        return pltpu.make_async_remote_copy(
            src_ref=wdown_ref.at[source],
            dst_ref=wcells_ref.at[pl.ds(0, HALO)],
            send_sem=onward_sem.at[1, lax.rem(source, lags // 2)],
            recv_sem=wrecv_sem.at[0],
            device_id=place(seam, source),
            device_id_type=MESH,
        )

    @pl.when(is_lower)
    def _():
        down_copy(lag).start()

    @pl.when(is_upper)
    def _():
        up_copy().start()

    for step in range(WORKERS):
        worker = order(step)

        @pl.when(worker != mine)
        def _():
            cell_copy(0, worker, lag).start()

    def arrived(kind):
        block = cells_ref.at[
            pl.ds((HALO, 0, HALO + groups)[kind], groups if kind == 0 else HALO)
        ]
        return pltpu.make_async_copy(block, block, recv_sem.at[min(kind, 1)])

    def gram_copies(worker, source):
        where = place(tile, first + worker)
        return (
            pltpu.make_async_remote_copy(
                src_ref=gsend_ref.at[worker],
                dst_ref=gram_ref.at[source],
                send_sem=gsend_sem.at[worker],
                recv_sem=grecv_sem.at[source],
                device_id=where,
                device_id_type=MESH,
            ),
            pltpu.make_async_remote_copy(
                src_ref=rsend_ref.at[worker],
                dst_ref=rhs_ref.at[source],
                send_sem=rsend_sem.at[worker],
                recv_sem=rrecv_sem.at[source],
                device_id=where,
                device_id_type=MESH,
            ),
        )

    @pl.when(jnp.logical_and(is_worker, jnp.logical_not(at_seam)))
    def _():
        weight_sums()

    @pl.when(jnp.logical_not(is_worker))
    def _():
        for load in loads[1:6]:
            load.wait()

    @pl.when(is_worker)
    def _():
        @pl.when(near_below)
        def _():
            weight_copy(1).start()

        @pl.when(near_above)
        def _():
            weight_copy(2).start()

        @pl.when(is_lower)
        def _():
            down_weights(lag).start()

        @pl.when(is_upper)
        def _():
            up_weights().start()

        pltpu.make_async_copy(
            send_ref.at[mine], cells_ref.at[pl.ds(HALO, groups), lag], recv_sem.at[0]
        ).start()

        @pl.when(tile == 0)
        def _():
            cells_ref[0:HALO] = jnp.zeros((HALO, lags, share, cols), bf16)
            wcells_ref[0:HALO] = jnp.zeros((HALO, 8, cols), f32)

        @pl.when(tile == tiles - 1)
        def _():
            cells_ref[HALO + groups :] = jnp.zeros((HALO, lags, share, cols), bf16)
            wcells_ref[HALO + groups :] = jnp.zeros((HALO, 8, cols), f32)

    @pl.when(is_last)
    def _():
        up_copy().wait_recv()
        for step in range(WORKERS):
            up_forward(order(step)).start()

        @pl.when(is_worker)
        def _():
            up_weights().wait_recv()
            up_forward_weights().start()

    def sends_weights(source):
        return jnp.logical_and(source >= first, source < first + WORKERS)

    @pl.when(is_end)
    def _():
        @pl.loop(0, middle)
        def _(n):
            source = end_base + n
            down_copy(source).wait_recv()
            for worker in range(WORKERS):
                down_forward(source, worker).start()

            @pl.when(sends_weights(source))
            def _():
                down_weights(source).wait_recv()
                down_forward_weights(source).start()

    row_major = lax.broadcasted_iota(jnp.int32, (share * rows, share * rows), 0)
    member_major = lax.broadcasted_iota(jnp.int32, (share * rows, share * rows), 1)
    wanted = lax.rem(row_major, share) * rows + row_major // share
    turn_ref[...] = jnp.where(member_major == wanted, 1.0, 0.0).astype(bf16)

    @pl.loop(0, rows)
    def _(r):
        out_ref[r] = jnp.zeros((members, cols), bf16)

    loads[6].wait()

    def lift(m, total):
        for n in range(8):
            total = total + hist_ref[8 * m + n].astype(f32)
        return total

    mean = lax.fori_loop(0, members // 8, lift, jnp.zeros((rows, cols), f32)) / members
    mean_ref[...] = mean

    @pl.loop(0, members // 8)
    def _(m):
        for n in range(8):
            hist_ref[8 * m + n] = (hist_ref[8 * m + n].astype(f32) - mean).astype(bf16)

    @pl.loop(0, members // (2 * share))
    def _(g):
        first = hist_ref[pl.ds(2 * share * g, share)].reshape(share * rows, cols)
        second = hist_ref[pl.ds(2 * share * g + share, share)].reshape(share * rows, cols)
        pair = jnp.concatenate([first, second], axis=1)
        turned = jnp.dot(turn_ref[...], pair, preferred_element_type=f32)
        turned = turned.reshape(rows, share, 2 * cols)
        turned = jnp.concatenate([turned[:, :, :cols], turned[:, :, cols:]], axis=1)
        start = pl.multiple_of(2 * share * g, 2 * share)
        turned_ref[:, pl.ds(start, 2 * share), :] = turned.astype(bf16)


    @pl.when(is_worker)
    def _():
        sub = lax.broadcasted_iota(jnp.int32, (patch_cols, cols), 0)
        lane = lax.broadcasted_iota(jnp.int32, (patch_cols, cols), 1)
        col_offset = (lane - PATCH * sub).astype(f32) - 7.5
        col_square = col_offset * col_offset
        squares = []
        for a in range(2):
            radius = jnp.zeros((patch_cols, cols), f32)
            for b in range(patch_cols):
                value = radius_ref[a * patch_cols + b].astype(f32)
                radius = jnp.where(sub == b, value, radius)
            squares.append(radius * radius)

        acc_ref[...] = jnp.zeros_like(acc_ref)
        accw_ref[...] = jnp.zeros_like(accw_ref)
        half = patch_cols // 2

        def accumulate(begin, count):
            wides, anomalies, scales, weighteds = [], [], [], []
            for n in range(count):
                j = begin + n
                values = cells_ref[j].astype(f32).reshape(members, cols)
                average = jnp.sum(values, axis=0, keepdims=True) / members
                anomaly = (values - average).astype(bf16)
                anomalies.append(anomaly)
                wides.append(anomaly.astype(f32))
                table = wcells_ref[j]
                innovation = table[1:2] - table[2:3] * average
                for a in range(2):
                    row_offset = (WORKERS * j - PATCH * a - 24 + mine).astype(f32) - 7.5
                    taper = 1.0 - (row_offset * row_offset + col_square) / squares[a]
                    taper = jnp.maximum(0.0, taper)
                    taper = taper * taper
                    both = taper[:half] + taper[half:]
                    scales.append(both * table[0:1])
                    weighteds.append(taper * innovation)
            left = jnp.concatenate(anomalies, axis=1)
            for b in range(half):
                near = lane[:1] < PATCH * b + 40
                near, far = (
                    jnp.where(near, 1.0, 0.0).astype(bf16),
                    jnp.where(near, 0.0, 1.0).astype(bf16),
                )
                rights = []
                for n in range(count):
                    column = []
                    for a in range(2):
                        scaled = (wides[n] * scales[2 * n + a][b : b + 1]).astype(bf16)
                        column += [scaled * near, scaled * far]
                    rights.append(jnp.concatenate(column, axis=0))
                right = jnp.concatenate(rights, axis=1)
                acc_ref[b] += lax.dot_general(left, right, NT, preferred_element_type=f32)
            side_left = jnp.concatenate(
                [
                    jnp.concatenate(weighteds[2 * n : 2 * n + 2], axis=0).astype(bf16)
                    for n in range(count)
                ],
                axis=1,
            )
            accw_ref[...] += lax.dot_general(side_left, left, NT, preferred_element_type=f32)

        arrived(0).wait()

        @pl.when(near_below)
        def _():
            halo_copy(1).start()

        @pl.when(near_above)
        def _():
            halo_copy(2).start()

        @pl.loop(0, 2)
        def _(n):
            accumulate(HALO + n * (groups // 2), groups // 2)

        @pl.loop(0, 2)
        def _(turn):
            side = jnp.where(tile < tiles // 2, turn, 1 - turn)

            @pl.when(jnp.logical_and(side == 0, near_above))
            def _():
                halo_copy(1).wait_recv()

            @pl.when(jnp.logical_and(side == 0, is_upper))
            def _():
                arrived(1).wait()

            @pl.when(jnp.logical_and(side == 0, has_above))
            def _():
                weight_copy(1).wait_recv()

            @pl.when(jnp.logical_and(side == 1, near_below))
            def _():
                halo_copy(2).wait_recv()

            @pl.when(jnp.logical_and(side == 1, is_lower))
            def _():
                arrived(2).wait()

            @pl.when(jnp.logical_and(side == 1, has_below))
            def _():
                weight_copy(2).wait_recv()

            accumulate(side * (HALO + groups), HALO)

        for worker in range(WORKERS):
            for a in range(2):
                lanes = slice(2 * a * members, 2 * (a + 1) * members)
                gsend_ref[worker, a] = acc_ref[worker, :, lanes].astype(bf16)
                q = a * patch_cols + worker
                rsend_ref[worker, a : a + 1] = jnp.concatenate(
                    [accw_ref[q : q + 1], accw_ref[q + half : q + half + 1]], axis=1
                )

        for worker in range(WORKERS):

            @pl.when(worker != mine)
            def _():
                for copy in gram_copies(worker, mine):
                    copy.start()

        gram_ref[mine] = gsend_ref[mine]
        rhs_ref[mine] = rsend_ref[mine]

    def transform_copy(target_lag, worker):
        return pltpu.make_async_remote_copy(
            src_ref=tsend_ref,
            dst_ref=trans_ref.at[worker],
            send_sem=tsend_sem.at[target_lag],
            recv_sem=trecv_sem.at[worker],
            device_id=place(tile, target_lag),
            device_id_type=MESH,
        )

    @pl.when(is_worker)
    def _():
        for source in range(WORKERS):

            @pl.when(source != mine)
            def _():
                for copy in gram_copies(0, source):
                    copy.wait_recv()

        row = lax.broadcasted_iota(jnp.int32, (members, 2 * members), 0)
        column = lax.broadcasted_iota(jnp.int32, (members, 2 * members), 1)
        identity = (row == lax.rem(column, members)).astype(f32)
        is_low = column[:1] < members
        low = jnp.where(is_low, 1.0, 0.0).astype(bf16)
        high = jnp.where(is_low, 0.0, 1.0).astype(bf16)

        def pick(values):
            return jnp.where(is_low, values[0], values[1])

        def lane_sums(x):
            return [
                jnp.sum(x[:, n * members : (n + 1) * members], axis=1, keepdims=True)
                for n in range(2)
            ]

        iterates, roots, bounds, rights_ = [], [], [], []
        for a in range(2):
            gram = gram_ref[0, a].astype(f32)
            rhs = rhs_ref[0, a : a + 1]
            for source in range(1, WORKERS):
                gram = gram + gram_ref[source, a].astype(f32)
                rhs = rhs + rhs_ref[source, a : a + 1]
            squares_ = lane_sums(jnp.sum(gram * gram, axis=0, keepdims=True))
            bound = members - 1.0 + jnp.sqrt(pick(squares_))
            bounds.append(bound)
            rights_.append(rhs)
            iterates.append((gram + (members - 1.0) * identity) / bound)
        roots = [1.5 * identity - 0.5 * iterate for iterate in iterates]
        iterates = [product(y, root, low, high) for y, root in zip(iterates, roots)]
        for sweep in range(1, NS_STEPS):
            corrections = [
                1.5 * identity - 0.5 * product(root, y, low, high)
                for root, y in zip(roots, iterates)
            ]
            if sweep < NS_STEPS - 1:
                iterates = [product(y, c, low, high) for y, c in zip(iterates, corrections)]
            roots = [product(c, root, low, high) for c, root in zip(corrections, roots)]
        for a in range(2):
            root, bound = roots[a], bounds[a]
            inner = pick(lane_sums(root * rights_[a]))
            weights = jnp.sum(root * inner, axis=0, keepdims=True) / bound
            factor = jnp.sqrt(jnp.full_like(bound, members - 1.0)) / jnp.sqrt(bound)
            tsend_ref[a] = (factor * root + weights).astype(bf16)

        for target in (0, lags - 1, 1, lags - 2, 2, lags - 3, 3, lags - 4):

            @pl.when(target != lag)
            def _():
                transform_copy(target, mine).start()

        trans_ref[mine] = tsend_ref[...]

    lane_patch = lax.broadcasted_iota(jnp.int32, (members, cols), 1) // PATCH
    half_rows = rows // 2

    @pl.loop(0, WORKERS)
    def _(step):
        near = jnp.where(is_worker, mine, jnp.where(lag < first, 0, WORKERS - 1))
        worker = jnp.where(
            is_worker, lax.rem(near + step, WORKERS), jnp.where(lag < first, step, near - step)
        )

        @pl.when(worker != mine)
        def _():
            transform_copy(lag, worker).wait_recv()

        mine_low = lane_patch == worker
        mine_high = lane_patch == worker + WORKERS
        mask = jnp.logical_or(mine_low, mine_high)
        low = jnp.where(mine_low[:1], 1.0, 0.0).astype(bf16)
        high = jnp.where(mine_high[:1], 1.0, 0.0).astype(bf16)
        for a in range(2):
            block = trans_ref[worker, a]

            @pl.loop(0, half_rows // 2, unroll=8)
            def _(i):
                rights = []
                for n in range(2):
                    state = turned_ref[a * half_rows + 2 * i + n]
                    rights.append(jnp.concatenate([state * low, state * high], axis=0))
                right = jnp.concatenate(rights, axis=1)
                mixed = jnp.dot(block, right, preferred_element_type=f32)
                for n in range(2):
                    r = a * half_rows + 2 * i + n
                    value = mixed[:, n * cols : (n + 1) * cols] + mean_ref[pl.ds(r, 1), :]
                    out_ref[r] = jnp.where(mask, value.astype(bf16), out_ref[r])

    @pl.when(is_lower)
    def _():
        down_copy(lag).wait_send()

        @pl.when(is_worker)
        def _():
            down_weights(lag).wait_send()

    @pl.when(is_upper)
    def _():
        up_copy().wait_send()

        @pl.when(is_worker)
        def _():
            up_weights().wait_send()

    @pl.when(is_last)
    def _():
        pltpu.make_async_copy(relay_ref, relay_ref, forward_sem.at[0]).wait()

        @pl.when(is_worker)
        def _():
            up_forward_weights().wait_send()

    @pl.when(is_end)
    def _():
        @pl.loop(0, middle)
        def _(n):
            source = end_base + n
            pltpu.make_async_copy(
                down_ref.at[source], down_ref.at[source], onward_sem.at[0, n]
            ).wait()

            @pl.when(sends_weights(source))
            def _():
                down_forward_weights(source).wait_send()

    for worker in range(WORKERS):

        @pl.when(worker != mine)
        def _():
            cell_copy(0, worker, lag).wait_send()

    @pl.when(is_worker)
    def _():
        @pl.when(near_above)
        def _():
            weight_copy(2).wait_send()
            halo_copy(2).wait_send()

        @pl.when(near_below)
        def _():
            weight_copy(1).wait_send()
            halo_copy(1).wait_send()

        for worker in range(WORKERS):

            @pl.when(worker != mine)
            def _():
                for copy in gram_copies(worker, mine):
                    copy.wait_send()

        for target in range(lags):

            @pl.when(target != lag)
            def _():
                transform_copy(target, mine).wait_send()


def solution(mesh):
    tiles, lags = mesh.shape["dom"], mesh.shape["lag"]

    def shards(history, forecast, spot, alive, heat, spread, radius):
        share, rows, cols = forecast.shape
        members = share * lags
        groups = rows // WORKERS
        window = groups + 2 * HALO
        f32, bf16, dma = jnp.float32, jnp.bfloat16, pltpu.SemaphoreType.DMA
        result = pl.pallas_call(
            functools.partial(kernel, tiles, lags),
            out_shape=jax.ShapeDtypeStruct((rows, members, cols), history.dtype),
            in_specs=[pl.BlockSpec(memory_space=pltpu.HBM)] * 7,
            out_specs=pl.BlockSpec(memory_space=pltpu.VMEM),
            scratch_shapes=[
                pltpu.VMEM(forecast.shape, bf16),
                pltpu.VMEM(spot.shape, jnp.int32),
                pltpu.VMEM(heat.shape, f32),
                pltpu.VMEM(spread.shape, f32),
                pltpu.SMEM(alive.shape, jnp.int32),
                pltpu.SMEM(radius.shape, jnp.int32),
                pltpu.VMEM((members, rows, cols), bf16),
                pltpu.VMEM((share * rows, share * rows), bf16),
                pltpu.VMEM((rows, cols), f32),
                pltpu.VMEM((rows, members, cols), bf16),
                pltpu.VMEM((share * rows, cols), f32),
                pltpu.VMEM((WORKERS, groups, share, cols), bf16),
                pltpu.VMEM((window, lags, share, cols), bf16),
                pltpu.VMEM((8 * rows, cols), f32),
                pltpu.VMEM((groups, 8, cols), f32),
                pltpu.VMEM((window, 8, cols), f32),
                pltpu.VMEM((WORKERS, members, 4 * members), f32),
                pltpu.VMEM((2 * WORKERS * 2, members), f32),
                pltpu.VMEM((WORKERS, 2, members, 2 * members), bf16),
                pltpu.VMEM((WORKERS, 2, members, 2 * members), bf16),
                pltpu.VMEM((WORKERS, 2, 2 * members), f32),
                pltpu.VMEM((WORKERS, 2, 2 * members), f32),
                pltpu.VMEM((2, members, 2 * members), bf16),
                pltpu.VMEM((WORKERS, 2, members, 2 * members), bf16),
                pltpu.VMEM((WORKERS, HALO, share, cols), bf16),
                pltpu.VMEM((HALO, 8, cols), f32),
                pltpu.VMEM((lags, WORKERS, HALO, share, cols), bf16),
                pltpu.VMEM((lags, HALO, 8, cols), f32),
                dma((7,)),
                dma((WORKERS,)),
                dma((2,)),
                dma((2,)),
                dma((2,)),
                dma((WORKERS,)),
                dma((WORKERS,)),
                dma((WORKERS,)),
                dma((WORKERS,)),
                dma((lags,)),
                dma((WORKERS,)),
                dma((2,)),
                dma((2,)),
                dma((4,)),
                dma((2,)),
                dma((2, lags // 2)),
                dma((2, lags // 2)),
            ],
            compiler_params=pltpu.CompilerParams(
                collective_id=0, has_side_effects=True, vmem_limit_bytes=16 << 20
            ),
            name="smoother",
        )(
            *(
                pltpu.with_memory_space_constraint(x, pltpu.HBM)
                for x in (forecast, spot, heat, spread, alive, radius, history)
            )
        )
        return jnp.transpose(result, (1, 0, 2))[None]

    in_specs = (
        P("lag", None, "dom", None),
        P("lag", "dom", None),
        P("dom", None),
        P("dom"),
        P("dom", None),
        P("dom", None),
        P("dom"),
    )
    out_specs = P("lag", None, "dom", None)
    return jax.shard_map(shards, mesh=mesh, in_specs=in_specs, out_specs=out_specs, check_vma=False)
```

```python
import functools

import jax
import jax.numpy as jnp
from jax import lax
from jax.experimental import pallas as pl
from jax.experimental.pallas import tpu as pltpu
from jax.sharding import PartitionSpec as P

PATCH = 16
NS_STEPS = 4
WORKERS = 4
HALO = 24 // WORKERS
MESH = pl.DeviceIdType.MESH
NT = (((1,), (1,)), ((), ()))


def split2(x):
    high = x.astype(jnp.bfloat16)
    return high, (x - high.astype(jnp.float32)).astype(jnp.bfloat16)


def product(x, y, low, high):
    xh, xl = split2(x)
    yh, yl = split2(y)
    yh = jnp.concatenate([yh * low, yh * high], axis=0)
    yl = jnp.concatenate([yl * low, yl * high], axis=0)
    dot = functools.partial(jnp.dot, preferred_element_type=jnp.float32)
    wide = dot(jnp.concatenate([xh, xl], axis=1), jnp.concatenate([yh, yh], axis=0))
    return wide + dot(xh, yl)


def kernel(
    tiles,
    lags,
    fore_hbm,
    spot_hbm,
    heat_hbm,
    spread_hbm,
    alive_hbm,
    radius_hbm,
    hist_hbm,
    out_ref,
    fore_ref,
    spot_ref,
    heat_ref,
    spread_ref,
    alive_ref,
    radius_ref,
    hist_ref,
    turn_ref,
    mean_ref,
    turned_ref,
    fore32_ref,
    send_ref,
    cells_ref,
    field_ref,
    wsend_ref,
    wcells_ref,
    acc_ref,
    accw_ref,
    gsend_ref,
    gram_ref,
    rsend_ref,
    rhs_ref,
    tsend_ref,
    trans_ref,
    relay_ref,
    wrelay_ref,
    down_ref,
    wdown_ref,
    load_sem,
    send_sem,
    recv_sem,
    wsend_sem,
    wrecv_sem,
    gsend_sem,
    grecv_sem,
    rsend_sem,
    rrecv_sem,
    tsend_sem,
    trecv_sem,
    hsend_sem,
    hrecv_sem,
    relay_sem,
    forward_sem,
    down_sem,
    onward_sem,
):
    tile = lax.axis_index("dom")
    lag = lax.axis_index("lag")
    share, rows, cols = fore_ref.shape
    members = share * lags
    groups = rows // WORKERS
    patch_cols = cols // PATCH
    slots = spot_ref.shape[1]
    first = lags // 2 - WORKERS // 2
    f32, bf16 = jnp.float32, jnp.bfloat16
    has_below = tile < tiles - 1
    has_above = tile > 0
    seam = tiles // 2
    is_lower = tile == seam - 1
    is_upper = tile == seam
    is_last = tile == tiles - 1
    at_seam = jnp.logical_or(is_lower, is_upper)
    sums_early = jnp.logical_or(at_seam, is_last)
    middle = lags // 2
    is_end = jnp.logical_and(is_last, jnp.logical_or(lag == 0, lag == lags - 1))
    end_lag = jnp.where(lag < middle, lags - 1, 0)
    end_base = jnp.where(lag == 0, middle, 0)
    near_below = jnp.logical_and(has_below, tile != seam - 1)
    near_above = jnp.logical_and(has_above, tile != seam)
    mine = lag - first
    is_worker = jnp.logical_and(mine >= 0, mine < WORKERS)

    def place(target_tile, target_lag):
        return {"dom": target_tile, "lag": target_lag}

    loads = [
        pltpu.make_async_copy(source, target, load_sem.at[n])
        for n, (source, target) in enumerate(
            (
                (fore_hbm, fore_ref),
                (alive_hbm, alive_ref),
                (radius_hbm, radius_ref),
                (spot_hbm, spot_ref),
                (spread_hbm, spread_ref),
                (heat_hbm, heat_ref),
                (hist_hbm.at[0], hist_ref),
            )
        )
    ]

    barrier = pltpu.get_barrier_semaphore()

    def greet(target_tile, target_lag):
        pl.semaphore_signal(
            barrier, inc=1, device_id=place(target_tile, target_lag), device_id_type=MESH
        )

    @pl.when(is_worker)
    def _():
        @pl.when(is_lower)
        def _():
            for target in range(lags):
                greet(tiles - 1, target)

        @pl.when(is_upper)
        def _():
            greet(tiles - 1, 0)
            greet(tiles - 1, lags - 1)

        for step in range(1, lags):
            greet(tile, lax.rem(lag + step, lags))

        @pl.when(near_above)
        def _():
            greet(tile - 1, lag)

        @pl.when(near_below)
        def _():
            greet(tile + 1, lag)

    @pl.when(is_last)
    def _():
        greet(seam, lag)

    @pl.when(is_end)
    def _():
        for n in range(middle):
            greet(seam - 1, end_base + n)

    for load in loads:
        load.start()

    loads[0].wait()
    for m in range(share):
        fore32_ref[m * rows : (m + 1) * rows, :] = fore_ref[m].astype(f32)
    for target in range(WORKERS):
        for k in range(groups):
            row = k * WORKERS + target
            send_ref[target, k] = fore32_ref[pl.ds(row, share, stride=rows), :].astype(bf16)

    def weight_sums():
        for load in loads[1:6]:
            load.wait()

        field_ref[...] = jnp.zeros_like(field_ref)
        slot_index = lax.broadcasted_iota(jnp.int32, (1, slots), 1)
        row_iota = lax.broadcasted_iota(jnp.int32, (PATCH, slots), 0)
        col_iota = lax.broadcasted_iota(jnp.int32, (cols, slots), 0)

        @pl.loop(0, rows // PATCH)
        def _(a):
            @pl.loop(0, patch_cols)
            def _(b):
                p = a * patch_cols + b
                spot = spot_ref[pl.ds(p, 1), :]
                live = slot_index < alive_ref[p]
                spread = jnp.where(live, spread_ref[pl.ds(p, 1), :], 0.0)
                weight = spread.astype(bf16).astype(f32)
                level = spread * heat_ref[pl.ds(p, 1), :]
                parts = [weight]
                for value in (level, spread):
                    for _ in range(3):
                        part = value.astype(bf16).astype(f32)
                        parts.append(part)
                        value = value - part
                in_row = row_iota == lax.shift_right_logical(spot, 4)
                in_col = col_iota == (spot & (PATCH - 1)) + b * PATCH
                left = jnp.concatenate([jnp.where(in_row, part, 0.0) for part in parts], axis=0)
                right = jnp.where(in_col, 1.0, 0.0).astype(bf16)
                sums = lax.dot_general(left.astype(bf16), right, NT, preferred_element_type=f32)
                base = pl.multiple_of(a * PATCH, PATCH)
                for q, chosen in enumerate(((0,), (3, 2, 1), (6, 5, 4))):
                    total = field_ref[pl.ds(q * rows + base, PATCH), :]
                    for c in chosen:
                        total = total + sums[c * PATCH : (c + 1) * PATCH]
                    field_ref[pl.ds(q * rows + base, PATCH), :] = total

        for k in range(groups):
            table = field_ref[pl.ds(k * WORKERS + mine, 8, stride=rows), :]
            wsend_ref[k] = table
            wcells_ref[HALO + k] = table

    @pl.when(jnp.logical_and(is_worker, sums_early))
    def _():
        weight_sums()

    pl.semaphore_wait(
        barrier,
        WORKERS
        - jnp.where(is_worker, 1, 0)
        + jnp.where(jnp.logical_and(is_worker, near_above), 1, 0)
        + jnp.where(jnp.logical_and(is_worker, near_below), 1, 0)
        + jnp.where(at_seam, 1, 0)
        + jnp.where(is_last, WORKERS, 0)
        + jnp.where(is_end, WORKERS, 0),
    )

    def cell_copy(kind, worker, source_lag):
        begin = groups - HALO if kind == 1 else 0
        count = groups if kind == 0 else HALO
        start = (HALO, 0, HALO + groups)[kind]
        return pltpu.make_async_remote_copy(
            src_ref=send_ref.at[worker, pl.ds(begin, count)],
            dst_ref=cells_ref.at[pl.ds(start, count), source_lag],
            send_sem=send_sem.at[worker],
            recv_sem=recv_sem.at[min(kind, 1)],
            device_id=place(tile + (0, 1, -1)[kind], first + worker),
            device_id_type=MESH,
        )

    def weight_copy(kind):
        begin = groups - HALO if kind == 1 else 0
        start = (HALO, 0, HALO + groups)[kind]
        return pltpu.make_async_remote_copy(
            src_ref=wsend_ref.at[pl.ds(begin, HALO)],
            dst_ref=wcells_ref.at[pl.ds(start, HALO)],
            send_sem=wsend_sem.at[kind - 1],
            recv_sem=wrecv_sem.at[kind - 1],
            device_id=place(tile + (0, 1, -1)[kind], lag),
            device_id_type=MESH,
        )

    def order(step):
        return jnp.where(lag < lags // 2, WORKERS - 1 - step, step)

    def halo_copy(kind):
        return pltpu.make_async_remote_copy(
            src_ref=cells_ref.at[pl.ds(groups if kind == 1 else HALO, HALO)],
            dst_ref=cells_ref.at[pl.ds(0 if kind == 1 else HALO + groups, HALO)],
            send_sem=hsend_sem.at[kind - 1],
            recv_sem=hrecv_sem.at[kind - 1],
            device_id=place(tile + (0, 1, -1)[kind], lag),
            device_id_type=MESH,
        )

    def up_copy():
        return pltpu.make_async_remote_copy(
            src_ref=send_ref.at[:, pl.ds(0, HALO)],
            dst_ref=relay_ref,
            send_sem=relay_sem.at[0],
            recv_sem=relay_sem.at[1],
            device_id=place(tiles - 1, lag),
            device_id_type=MESH,
        )

    def up_weights():
        return pltpu.make_async_remote_copy(
            src_ref=wsend_ref.at[pl.ds(0, HALO)],
            dst_ref=wrelay_ref,
            send_sem=relay_sem.at[2],
            recv_sem=relay_sem.at[3],
            device_id=place(tiles - 1, lag),
            device_id_type=MESH,
        )

    def up_forward(worker):
        return pltpu.make_async_remote_copy(
            src_ref=relay_ref.at[worker],
            dst_ref=cells_ref.at[pl.ds(HALO + groups, HALO), lag],
            send_sem=forward_sem.at[0],
            recv_sem=recv_sem.at[1],
            device_id=place(seam - 1, first + worker),
            device_id_type=MESH,
        )

    def up_forward_weights():
        return pltpu.make_async_remote_copy(
            src_ref=wrelay_ref,
            dst_ref=wcells_ref.at[pl.ds(HALO + groups, HALO)],
            send_sem=forward_sem.at[1],
            recv_sem=wrecv_sem.at[1],
            device_id=place(seam - 1, lag),
            device_id_type=MESH,
        )

    def down_copy(source):
        return pltpu.make_async_remote_copy(
            src_ref=send_ref.at[:, pl.ds(groups - HALO, HALO)],
            dst_ref=down_ref.at[source],
            send_sem=relay_sem.at[0],
            recv_sem=down_sem.at[0, lax.rem(source, lags // 2)],
            device_id=place(tiles - 1, end_lag),
            device_id_type=MESH,
        )

    def down_weights(source):
        return pltpu.make_async_remote_copy(
            src_ref=wsend_ref.at[pl.ds(groups - HALO, HALO)],
            dst_ref=wdown_ref.at[source],
            send_sem=relay_sem.at[2],
            recv_sem=down_sem.at[1, lax.rem(source, lags // 2)],
            device_id=place(tiles - 1, end_lag),
            device_id_type=MESH,
        )

    def down_forward(source, worker):
        return pltpu.make_async_remote_copy(
            src_ref=down_ref.at[source, worker],
            dst_ref=cells_ref.at[pl.ds(0, HALO), source],
            send_sem=onward_sem.at[0, lax.rem(source, lags // 2)],
            recv_sem=recv_sem.at[1],
            device_id=place(seam, first + worker),
            device_id_type=MESH,
        )

    def down_forward_weights(source):
        return pltpu.make_async_remote_copy(
            src_ref=wdown_ref.at[source],
            dst_ref=wcells_ref.at[pl.ds(0, HALO)],
            send_sem=onward_sem.at[1, lax.rem(source, lags // 2)],
            recv_sem=wrecv_sem.at[0],
            device_id=place(seam, source),
            device_id_type=MESH,
        )

    @pl.when(is_lower)
    def _():
        down_copy(lag).start()

    @pl.when(is_upper)
    def _():
        up_copy().start()

    for step in range(WORKERS):
        worker = order(step)

        @pl.when(worker != mine)
        def _():
            cell_copy(0, worker, lag).start()

    def arrived(kind):
        block = cells_ref.at[
            pl.ds((HALO, 0, HALO + groups)[kind], groups if kind == 0 else HALO)
        ]
        return pltpu.make_async_copy(block, block, recv_sem.at[min(kind, 1)])

    def gram_copies(worker, source):
        where = place(tile, first + worker)
        return (
            pltpu.make_async_remote_copy(
                src_ref=gsend_ref.at[worker],
                dst_ref=gram_ref.at[source],
                send_sem=gsend_sem.at[worker],
                recv_sem=grecv_sem.at[source],
                device_id=where,
                device_id_type=MESH,
            ),
            pltpu.make_async_remote_copy(
                src_ref=rsend_ref.at[worker],
                dst_ref=rhs_ref.at[source],
                send_sem=rsend_sem.at[worker],
                recv_sem=rrecv_sem.at[source],
                device_id=where,
                device_id_type=MESH,
            ),
        )

    @pl.when(jnp.logical_and(is_worker, jnp.logical_not(sums_early)))
    def _():
        weight_sums()

    @pl.when(jnp.logical_not(is_worker))
    def _():
        for load in loads[1:6]:
            load.wait()

    @pl.when(is_worker)
    def _():
        @pl.when(near_below)
        def _():
            weight_copy(1).start()

        @pl.when(near_above)
        def _():
            weight_copy(2).start()

        @pl.when(is_lower)
        def _():
            down_weights(lag).start()

        @pl.when(is_upper)
        def _():
            up_weights().start()

        pltpu.make_async_copy(
            send_ref.at[mine], cells_ref.at[pl.ds(HALO, groups), lag], recv_sem.at[0]
        ).start()

        @pl.when(tile == 0)
        def _():
            cells_ref[0:HALO] = jnp.zeros((HALO, lags, share, cols), bf16)
            wcells_ref[0:HALO] = jnp.zeros((HALO, 8, cols), f32)

        @pl.when(tile == tiles - 1)
        def _():
            cells_ref[HALO + groups :] = jnp.zeros((HALO, lags, share, cols), bf16)
            wcells_ref[HALO + groups :] = jnp.zeros((HALO, 8, cols), f32)

    @pl.when(is_last)
    def _():
        up_copy().wait_recv()
        for step in range(WORKERS):
            up_forward(order(step)).start()

        @pl.when(is_worker)
        def _():
            up_weights().wait_recv()
            up_forward_weights().start()

    def sends_weights(source):
        return jnp.logical_and(source >= first, source < first + WORKERS)

    @pl.when(is_end)
    def _():
        @pl.loop(0, middle)
        def _(n):
            source = end_base + n
            down_copy(source).wait_recv()
            for worker in range(WORKERS):
                down_forward(source, worker).start()

            @pl.when(sends_weights(source))
            def _():
                down_weights(source).wait_recv()
                down_forward_weights(source).start()

    row_major = lax.broadcasted_iota(jnp.int32, (share * rows, share * rows), 0)
    member_major = lax.broadcasted_iota(jnp.int32, (share * rows, share * rows), 1)
    wanted = lax.rem(row_major, share) * rows + row_major // share
    turn_ref[...] = jnp.where(member_major == wanted, 1.0, 0.0).astype(bf16)

    @pl.loop(0, rows)
    def _(r):
        out_ref[r] = jnp.zeros((members, cols), bf16)

    loads[6].wait()

    def lift(m, total):
        for n in range(8):
            total = total + hist_ref[8 * m + n].astype(f32)
        return total

    mean = lax.fori_loop(0, members // 8, lift, jnp.zeros((rows, cols), f32)) / members
    mean_ref[...] = mean

    @pl.loop(0, members // 8)
    def _(m):
        for n in range(8):
            hist_ref[8 * m + n] = (hist_ref[8 * m + n].astype(f32) - mean).astype(bf16)

    @pl.loop(0, members // (2 * share))
    def _(g):
        first = hist_ref[pl.ds(2 * share * g, share)].reshape(share * rows, cols)
        second = hist_ref[pl.ds(2 * share * g + share, share)].reshape(share * rows, cols)
        pair = jnp.concatenate([first, second], axis=1)
        turned = jnp.dot(turn_ref[...], pair, preferred_element_type=f32)
        turned = turned.reshape(rows, share, 2 * cols)
        turned = jnp.concatenate([turned[:, :, :cols], turned[:, :, cols:]], axis=1)
        start = pl.multiple_of(2 * share * g, 2 * share)
        turned_ref[:, pl.ds(start, 2 * share), :] = turned.astype(bf16)


    @pl.when(is_worker)
    def _():
        sub = lax.broadcasted_iota(jnp.int32, (patch_cols, cols), 0)
        lane = lax.broadcasted_iota(jnp.int32, (patch_cols, cols), 1)
        col_offset = (lane - PATCH * sub).astype(f32) - 7.5
        col_square = col_offset * col_offset
        squares = []
        for a in range(2):
            radius = jnp.zeros((patch_cols, cols), f32)
            for b in range(patch_cols):
                value = radius_ref[a * patch_cols + b].astype(f32)
                radius = jnp.where(sub == b, value, radius)
            squares.append(radius * radius)

        acc_ref[...] = jnp.zeros_like(acc_ref)
        accw_ref[...] = jnp.zeros_like(accw_ref)
        half = patch_cols // 2

        def accumulate(begin, count):
            wides, anomalies, scales, weighteds = [], [], [], []
            for n in range(count):
                j = begin + n
                values = cells_ref[j].astype(f32).reshape(members, cols)
                average = jnp.sum(values, axis=0, keepdims=True) / members
                anomaly = (values - average).astype(bf16)
                anomalies.append(anomaly)
                wides.append(anomaly.astype(f32))
                table = wcells_ref[j]
                innovation = table[1:2] - table[2:3] * average
                for a in range(2):
                    row_offset = (WORKERS * j - PATCH * a - 24 + mine).astype(f32) - 7.5
                    taper = 1.0 - (row_offset * row_offset + col_square) / squares[a]
                    taper = jnp.maximum(0.0, taper)
                    taper = taper * taper
                    both = taper[:half] + taper[half:]
                    scales.append(both * table[0:1])
                    weighteds.append(taper * innovation)
            left = jnp.concatenate(anomalies, axis=1)
            for b in range(half):
                near = lane[:1] < PATCH * b + 40
                near, far = (
                    jnp.where(near, 1.0, 0.0).astype(bf16),
                    jnp.where(near, 0.0, 1.0).astype(bf16),
                )
                rights = []
                for n in range(count):
                    column = []
                    for a in range(2):
                        scaled = (wides[n] * scales[2 * n + a][b : b + 1]).astype(bf16)
                        column += [scaled * near, scaled * far]
                    rights.append(jnp.concatenate(column, axis=0))
                right = jnp.concatenate(rights, axis=1)
                acc_ref[b] += lax.dot_general(left, right, NT, preferred_element_type=f32)
            side_left = jnp.concatenate(
                [
                    jnp.concatenate(weighteds[2 * n : 2 * n + 2], axis=0).astype(bf16)
                    for n in range(count)
                ],
                axis=1,
            )
            accw_ref[...] += lax.dot_general(side_left, left, NT, preferred_element_type=f32)

        arrived(0).wait()

        @pl.when(near_below)
        def _():
            halo_copy(1).start()

        @pl.when(near_above)
        def _():
            halo_copy(2).start()

        @pl.loop(0, 2)
        def _(n):
            accumulate(HALO + n * (groups // 2), groups // 2)

        @pl.loop(0, 2)
        def _(turn):
            side = jnp.where(tile < tiles // 2, turn, 1 - turn)

            @pl.when(jnp.logical_and(side == 0, near_above))
            def _():
                halo_copy(1).wait_recv()

            @pl.when(jnp.logical_and(side == 0, is_upper))
            def _():
                arrived(1).wait()

            @pl.when(jnp.logical_and(side == 0, has_above))
            def _():
                weight_copy(1).wait_recv()

            @pl.when(jnp.logical_and(side == 1, near_below))
            def _():
                halo_copy(2).wait_recv()

            @pl.when(jnp.logical_and(side == 1, is_lower))
            def _():
                arrived(2).wait()

            @pl.when(jnp.logical_and(side == 1, has_below))
            def _():
                weight_copy(2).wait_recv()

            accumulate(side * (HALO + groups), HALO)

        for worker in range(WORKERS):
            for a in range(2):
                lanes = slice(2 * a * members, 2 * (a + 1) * members)
                gsend_ref[worker, a] = acc_ref[worker, :, lanes].astype(bf16)
                q = a * patch_cols + worker
                rsend_ref[worker, a : a + 1] = jnp.concatenate(
                    [accw_ref[q : q + 1], accw_ref[q + half : q + half + 1]], axis=1
                )

        for worker in range(WORKERS):

            @pl.when(worker != mine)
            def _():
                for copy in gram_copies(worker, mine):
                    copy.start()

        gram_ref[mine] = gsend_ref[mine]
        rhs_ref[mine] = rsend_ref[mine]

    def transform_copy(target_lag, worker):
        return pltpu.make_async_remote_copy(
            src_ref=tsend_ref,
            dst_ref=trans_ref.at[worker],
            send_sem=tsend_sem.at[target_lag],
            recv_sem=trecv_sem.at[worker],
            device_id=place(tile, target_lag),
            device_id_type=MESH,
        )

    @pl.when(is_worker)
    def _():
        for source in range(WORKERS):

            @pl.when(source != mine)
            def _():
                for copy in gram_copies(0, source):
                    copy.wait_recv()

        row = lax.broadcasted_iota(jnp.int32, (members, 2 * members), 0)
        column = lax.broadcasted_iota(jnp.int32, (members, 2 * members), 1)
        identity = (row == lax.rem(column, members)).astype(f32)
        is_low = column[:1] < members
        low = jnp.where(is_low, 1.0, 0.0).astype(bf16)
        high = jnp.where(is_low, 0.0, 1.0).astype(bf16)

        def pick(values):
            return jnp.where(is_low, values[0], values[1])

        def lane_sums(x):
            return [
                jnp.sum(x[:, n * members : (n + 1) * members], axis=1, keepdims=True)
                for n in range(2)
            ]

        iterates, roots, bounds, rights_ = [], [], [], []
        for a in range(2):
            gram = gram_ref[0, a].astype(f32)
            rhs = rhs_ref[0, a : a + 1]
            for source in range(1, WORKERS):
                gram = gram + gram_ref[source, a].astype(f32)
                rhs = rhs + rhs_ref[source, a : a + 1]
            squares_ = lane_sums(jnp.sum(gram * gram, axis=0, keepdims=True))
            bound = members - 1.0 + jnp.sqrt(pick(squares_))
            bounds.append(bound)
            rights_.append(rhs)
            iterates.append((gram + (members - 1.0) * identity) / bound)
        roots = [1.5 * identity - 0.5 * iterate for iterate in iterates]
        iterates = [product(y, root, low, high) for y, root in zip(iterates, roots)]
        for sweep in range(1, NS_STEPS):
            corrections = [
                1.5 * identity - 0.5 * product(root, y, low, high)
                for root, y in zip(roots, iterates)
            ]
            if sweep < NS_STEPS - 1:
                iterates = [product(y, c, low, high) for y, c in zip(iterates, corrections)]
            roots = [product(c, root, low, high) for c, root in zip(corrections, roots)]
        for a in range(2):
            root, bound = roots[a], bounds[a]
            inner = pick(lane_sums(root * rights_[a]))
            weights = jnp.sum(root * inner, axis=0, keepdims=True) / bound
            factor = jnp.sqrt(jnp.full_like(bound, members - 1.0)) / jnp.sqrt(bound)
            tsend_ref[a] = (factor * root + weights).astype(bf16)

        for target in (0, lags - 1, 1, lags - 2, 2, lags - 3, 3, lags - 4):

            @pl.when(target != lag)
            def _():
                transform_copy(target, mine).start()

        trans_ref[mine] = tsend_ref[...]

    lane_patch = lax.broadcasted_iota(jnp.int32, (members, cols), 1) // PATCH
    half_rows = rows // 2

    @pl.loop(0, WORKERS)
    def _(step):
        near = jnp.where(is_worker, mine, jnp.where(lag < first, 0, WORKERS - 1))
        worker = jnp.where(
            is_worker, lax.rem(near + step, WORKERS), jnp.where(lag < first, step, near - step)
        )

        @pl.when(worker != mine)
        def _():
            transform_copy(lag, worker).wait_recv()

        mine_low = lane_patch == worker
        mine_high = lane_patch == worker + WORKERS
        mask = jnp.logical_or(mine_low, mine_high)
        low = jnp.where(mine_low[:1], 1.0, 0.0).astype(bf16)
        high = jnp.where(mine_high[:1], 1.0, 0.0).astype(bf16)
        for a in range(2):
            block = trans_ref[worker, a]

            @pl.loop(0, half_rows // 2, unroll=8)
            def _(i):
                rights = []
                for n in range(2):
                    state = turned_ref[a * half_rows + 2 * i + n]
                    rights.append(jnp.concatenate([state * low, state * high], axis=0))
                right = jnp.concatenate(rights, axis=1)
                mixed = jnp.dot(block, right, preferred_element_type=f32)
                for n in range(2):
                    r = a * half_rows + 2 * i + n
                    value = mixed[:, n * cols : (n + 1) * cols] + mean_ref[pl.ds(r, 1), :]
                    out_ref[r] = jnp.where(mask, value.astype(bf16), out_ref[r])

    @pl.when(is_lower)
    def _():
        down_copy(lag).wait_send()

        @pl.when(is_worker)
        def _():
            down_weights(lag).wait_send()

    @pl.when(is_upper)
    def _():
        up_copy().wait_send()

        @pl.when(is_worker)
        def _():
            up_weights().wait_send()

    @pl.when(is_last)
    def _():
        pltpu.make_async_copy(relay_ref, relay_ref, forward_sem.at[0]).wait()

        @pl.when(is_worker)
        def _():
            up_forward_weights().wait_send()

    @pl.when(is_end)
    def _():
        @pl.loop(0, middle)
        def _(n):
            source = end_base + n
            pltpu.make_async_copy(
                down_ref.at[source], down_ref.at[source], onward_sem.at[0, n]
            ).wait()

            @pl.when(sends_weights(source))
            def _():
                down_forward_weights(source).wait_send()

    for worker in range(WORKERS):

        @pl.when(worker != mine)
        def _():
            cell_copy(0, worker, lag).wait_send()

    @pl.when(is_worker)
    def _():
        @pl.when(near_above)
        def _():
            weight_copy(2).wait_send()
            halo_copy(2).wait_send()

        @pl.when(near_below)
        def _():
            weight_copy(1).wait_send()
            halo_copy(1).wait_send()

        for worker in range(WORKERS):

            @pl.when(worker != mine)
            def _():
                for copy in gram_copies(worker, mine):
                    copy.wait_send()

        for target in range(lags):

            @pl.when(target != lag)
            def _():
                transform_copy(target, mine).wait_send()


def solution(mesh):
    tiles, lags = mesh.shape["dom"], mesh.shape["lag"]

    def shards(history, forecast, spot, alive, heat, spread, radius):
        share, rows, cols = forecast.shape
        members = share * lags
        groups = rows // WORKERS
        window = groups + 2 * HALO
        f32, bf16, dma = jnp.float32, jnp.bfloat16, pltpu.SemaphoreType.DMA
        result = pl.pallas_call(
            functools.partial(kernel, tiles, lags),
            out_shape=jax.ShapeDtypeStruct((rows, members, cols), history.dtype),
            in_specs=[pl.BlockSpec(memory_space=pltpu.HBM)] * 7,
            out_specs=pl.BlockSpec(memory_space=pltpu.VMEM),
            scratch_shapes=[
                pltpu.VMEM(forecast.shape, bf16),
                pltpu.VMEM(spot.shape, jnp.int32),
                pltpu.VMEM(heat.shape, f32),
                pltpu.VMEM(spread.shape, f32),
                pltpu.SMEM(alive.shape, jnp.int32),
                pltpu.SMEM(radius.shape, jnp.int32),
                pltpu.VMEM((members, rows, cols), bf16),
                pltpu.VMEM((share * rows, share * rows), bf16),
                pltpu.VMEM((rows, cols), f32),
                pltpu.VMEM((rows, members, cols), bf16),
                pltpu.VMEM((share * rows, cols), f32),
                pltpu.VMEM((WORKERS, groups, share, cols), bf16),
                pltpu.VMEM((window, lags, share, cols), bf16),
                pltpu.VMEM((8 * rows, cols), f32),
                pltpu.VMEM((groups, 8, cols), f32),
                pltpu.VMEM((window, 8, cols), f32),
                pltpu.VMEM((WORKERS, members, 4 * members), f32),
                pltpu.VMEM((2 * WORKERS * 2, members), f32),
                pltpu.VMEM((WORKERS, 2, members, 2 * members), bf16),
                pltpu.VMEM((WORKERS, 2, members, 2 * members), bf16),
                pltpu.VMEM((WORKERS, 2, 2 * members), f32),
                pltpu.VMEM((WORKERS, 2, 2 * members), f32),
                pltpu.VMEM((2, members, 2 * members), bf16),
                pltpu.VMEM((WORKERS, 2, members, 2 * members), bf16),
                pltpu.VMEM((WORKERS, HALO, share, cols), bf16),
                pltpu.VMEM((HALO, 8, cols), f32),
                pltpu.VMEM((lags, WORKERS, HALO, share, cols), bf16),
                pltpu.VMEM((lags, HALO, 8, cols), f32),
                dma((7,)),
                dma((WORKERS,)),
                dma((2,)),
                dma((2,)),
                dma((2,)),
                dma((WORKERS,)),
                dma((WORKERS,)),
                dma((WORKERS,)),
                dma((WORKERS,)),
                dma((lags,)),
                dma((WORKERS,)),
                dma((2,)),
                dma((2,)),
                dma((4,)),
                dma((2,)),
                dma((2, lags // 2)),
                dma((2, lags // 2)),
            ],
            compiler_params=pltpu.CompilerParams(
                collective_id=0, has_side_effects=True, vmem_limit_bytes=16 << 20
            ),
            name="smoother",
        )(
            *(
                pltpu.with_memory_space_constraint(x, pltpu.HBM)
                for x in (forecast, spot, heat, spread, alive, radius, history)
            )
        )
        return jnp.transpose(result, (1, 0, 2))[None]

    in_specs = (
        P("lag", None, "dom", None),
        P("lag", "dom", None),
        P("dom", None),
        P("dom"),
        P("dom", None),
        P("dom", None),
        P("dom"),
    )
    out_specs = P("lag", None, "dom", None)
    return jax.shard_map(shards, mesh=mesh, in_specs=in_specs, out_specs=out_specs, check_vma=False)
```

```python
import functools

import jax
import jax.numpy as jnp
from jax import lax
from jax.experimental import pallas as pl
from jax.experimental.pallas import tpu as pltpu
from jax.sharding import PartitionSpec as P

PATCH = 16
NS_STEPS = 4
WORKERS = 4
HALO = 24 // WORKERS
MESH = pl.DeviceIdType.MESH
NT = (((1,), (1,)), ((), ()))


def split2(x):
    high = x.astype(jnp.bfloat16)
    return high, (x - high.astype(jnp.float32)).astype(jnp.bfloat16)


def product(x, y, low, high):
    xh, xl = split2(x)
    yh, yl = split2(y)
    yh = jnp.concatenate([yh * low, yh * high], axis=0)
    yl = jnp.concatenate([yl * low, yl * high], axis=0)
    dot = functools.partial(jnp.dot, preferred_element_type=jnp.float32)
    wide = dot(jnp.concatenate([xh, xl], axis=1), jnp.concatenate([yh, yh], axis=0))
    return wide + dot(xh, yl)


def kernel(
    tiles,
    lags,
    fore_hbm,
    spot_hbm,
    heat_hbm,
    spread_hbm,
    alive_hbm,
    radius_hbm,
    hist_hbm,
    out_ref,
    fore_ref,
    spot_ref,
    heat_ref,
    spread_ref,
    alive_ref,
    radius_ref,
    hist_ref,
    turn_ref,
    mean_ref,
    turned_ref,
    fore32_ref,
    send_ref,
    cells_ref,
    field_ref,
    wsend_ref,
    wcells_ref,
    acc_ref,
    accw_ref,
    gsend_ref,
    gram_ref,
    rsend_ref,
    rhs_ref,
    tsend_ref,
    trans_ref,
    relay_ref,
    wrelay_ref,
    down_ref,
    wdown_ref,
    load_sem,
    send_sem,
    recv_sem,
    wsend_sem,
    wrecv_sem,
    gsend_sem,
    grecv_sem,
    rsend_sem,
    rrecv_sem,
    tsend_sem,
    trecv_sem,
    hsend_sem,
    hrecv_sem,
    relay_sem,
    forward_sem,
    down_sem,
    onward_sem,
):
    tile = lax.axis_index("dom")
    lag = lax.axis_index("lag")
    share, rows, cols = fore_ref.shape
    members = share * lags
    groups = rows // WORKERS
    patch_cols = cols // PATCH
    slots = spot_ref.shape[1]
    first = lags // 2 - WORKERS // 2
    f32, bf16 = jnp.float32, jnp.bfloat16
    has_below = tile < tiles - 1
    has_above = tile > 0
    seam = tiles // 2
    is_lower = tile == seam - 1
    is_upper = tile == seam
    is_last = tile == tiles - 1
    at_seam = jnp.logical_or(is_lower, is_upper)
    sums_early = jnp.logical_or(at_seam, is_last)
    middle = lags // 2
    is_end = jnp.logical_and(is_last, jnp.logical_or(lag == 0, lag == lags - 1))
    end_lag = jnp.where(lag < middle, lags - 1, 0)
    end_base = jnp.where(lag == 0, middle, 0)
    near_below = jnp.logical_and(has_below, tile != seam - 1)
    near_above = jnp.logical_and(has_above, tile != seam)
    mine = lag - first
    is_worker = jnp.logical_and(mine >= 0, mine < WORKERS)

    def place(target_tile, target_lag):
        return {"dom": target_tile, "lag": target_lag}

    loads = [
        pltpu.make_async_copy(source, target, load_sem.at[n])
        for n, (source, target) in enumerate(
            (
                (fore_hbm, fore_ref),
                (alive_hbm, alive_ref),
                (radius_hbm, radius_ref),
                (spot_hbm, spot_ref),
                (spread_hbm, spread_ref),
                (heat_hbm, heat_ref),
                (hist_hbm.at[0], hist_ref),
            )
        )
    ]

    barrier = pltpu.get_barrier_semaphore()

    def greet(target_tile, target_lag):
        pl.semaphore_signal(
            barrier, inc=1, device_id=place(target_tile, target_lag), device_id_type=MESH
        )

    @pl.when(is_worker)
    def _():
        @pl.when(is_lower)
        def _():
            for target in range(lags):
                greet(tiles - 1, target)

        @pl.when(is_upper)
        def _():
            greet(tiles - 1, 0)
            greet(tiles - 1, lags - 1)

        for step in range(1, lags):
            greet(tile, lax.rem(lag + step, lags))

        @pl.when(near_above)
        def _():
            greet(tile - 1, lag)

        @pl.when(near_below)
        def _():
            greet(tile + 1, lag)

    @pl.when(is_last)
    def _():
        greet(seam, lag)

    @pl.when(is_end)
    def _():
        for n in range(middle):
            greet(seam - 1, end_base + n)

    for load in loads:
        load.start()

    loads[0].wait()
    for m in range(share):
        fore32_ref[m * rows : (m + 1) * rows, :] = fore_ref[m].astype(f32)
    for target in range(WORKERS):
        for k in range(groups):
            row = k * WORKERS + target
            send_ref[target, k] = fore32_ref[pl.ds(row, share, stride=rows), :].astype(bf16)

    def weight_sums():
        for load in loads[1:6]:
            load.wait()

        field_ref[...] = jnp.zeros_like(field_ref)
        slot_index = lax.broadcasted_iota(jnp.int32, (1, slots), 1)
        row_iota = lax.broadcasted_iota(jnp.int32, (PATCH, slots), 0)
        col_iota = lax.broadcasted_iota(jnp.int32, (cols, slots), 0)

        @pl.loop(0, rows // PATCH)
        def _(a):
            @pl.loop(0, patch_cols)
            def _(b):
                p = a * patch_cols + b
                spot = spot_ref[pl.ds(p, 1), :]
                live = slot_index < alive_ref[p]
                spread = jnp.where(live, spread_ref[pl.ds(p, 1), :], 0.0)
                weight = spread.astype(bf16).astype(f32)
                level = spread * heat_ref[pl.ds(p, 1), :]
                parts = [weight]
                for value in (level, spread):
                    for _ in range(3):
                        part = value.astype(bf16).astype(f32)
                        parts.append(part)
                        value = value - part
                in_row = row_iota == lax.shift_right_logical(spot, 4)
                in_col = col_iota == (spot & (PATCH - 1)) + b * PATCH
                left = jnp.concatenate([jnp.where(in_row, part, 0.0) for part in parts], axis=0)
                right = jnp.where(in_col, 1.0, 0.0).astype(bf16)
                sums = lax.dot_general(left.astype(bf16), right, NT, preferred_element_type=f32)
                base = pl.multiple_of(a * PATCH, PATCH)
                for q, chosen in enumerate(((0,), (3, 2, 1), (6, 5, 4))):
                    total = field_ref[pl.ds(q * rows + base, PATCH), :]
                    for c in chosen:
                        total = total + sums[c * PATCH : (c + 1) * PATCH]
                    field_ref[pl.ds(q * rows + base, PATCH), :] = total

        for k in range(groups):
            table = field_ref[pl.ds(k * WORKERS + mine, 8, stride=rows), :]
            wsend_ref[k] = table
            wcells_ref[HALO + k] = table

    @pl.when(jnp.logical_and(is_worker, sums_early))
    def _():
        weight_sums()

    pl.semaphore_wait(
        barrier,
        WORKERS
        - jnp.where(is_worker, 1, 0)
        + jnp.where(jnp.logical_and(is_worker, near_above), 1, 0)
        + jnp.where(jnp.logical_and(is_worker, near_below), 1, 0)
        + jnp.where(at_seam, 1, 0)
        + jnp.where(is_last, WORKERS, 0)
        + jnp.where(is_end, WORKERS, 0),
    )

    def cell_copy(kind, worker, source_lag):
        begin = groups - HALO if kind == 1 else 0
        count = groups if kind == 0 else HALO
        start = (HALO, 0, HALO + groups)[kind]
        return pltpu.make_async_remote_copy(
            src_ref=send_ref.at[worker, pl.ds(begin, count)],
            dst_ref=cells_ref.at[pl.ds(start, count), source_lag],
            send_sem=send_sem.at[worker],
            recv_sem=recv_sem.at[min(kind, 1)],
            device_id=place(tile + (0, 1, -1)[kind], first + worker),
            device_id_type=MESH,
        )

    def weight_copy(kind):
        begin = groups - HALO if kind == 1 else 0
        start = (HALO, 0, HALO + groups)[kind]
        return pltpu.make_async_remote_copy(
            src_ref=wsend_ref.at[pl.ds(begin, HALO)],
            dst_ref=wcells_ref.at[pl.ds(start, HALO)],
            send_sem=wsend_sem.at[kind - 1],
            recv_sem=wrecv_sem.at[kind - 1],
            device_id=place(tile + (0, 1, -1)[kind], lag),
            device_id_type=MESH,
        )

    def order(step):
        return jnp.where(lag < lags // 2, WORKERS - 1 - step, step)

    def halo_copy(kind):
        return pltpu.make_async_remote_copy(
            src_ref=cells_ref.at[pl.ds(groups if kind == 1 else HALO, HALO)],
            dst_ref=cells_ref.at[pl.ds(0 if kind == 1 else HALO + groups, HALO)],
            send_sem=hsend_sem.at[kind - 1],
            recv_sem=hrecv_sem.at[kind - 1],
            device_id=place(tile + (0, 1, -1)[kind], lag),
            device_id_type=MESH,
        )

    def up_copy():
        return pltpu.make_async_remote_copy(
            src_ref=send_ref.at[:, pl.ds(0, HALO)],
            dst_ref=relay_ref,
            send_sem=relay_sem.at[0],
            recv_sem=relay_sem.at[1],
            device_id=place(tiles - 1, lag),
            device_id_type=MESH,
        )

    def up_weights():
        return pltpu.make_async_remote_copy(
            src_ref=wsend_ref.at[pl.ds(0, HALO)],
            dst_ref=wrelay_ref,
            send_sem=relay_sem.at[2],
            recv_sem=relay_sem.at[3],
            device_id=place(tiles - 1, lag),
            device_id_type=MESH,
        )

    def up_forward(worker):
        return pltpu.make_async_remote_copy(
            src_ref=relay_ref.at[worker],
            dst_ref=cells_ref.at[pl.ds(HALO + groups, HALO), lag],
            send_sem=forward_sem.at[0],
            recv_sem=recv_sem.at[1],
            device_id=place(seam - 1, first + worker),
            device_id_type=MESH,
        )

    def up_forward_weights():
        return pltpu.make_async_remote_copy(
            src_ref=wrelay_ref,
            dst_ref=wcells_ref.at[pl.ds(HALO + groups, HALO)],
            send_sem=forward_sem.at[1],
            recv_sem=wrecv_sem.at[1],
            device_id=place(seam - 1, lag),
            device_id_type=MESH,
        )

    def down_copy(source):
        return pltpu.make_async_remote_copy(
            src_ref=send_ref.at[:, pl.ds(groups - HALO, HALO)],
            dst_ref=down_ref.at[source],
            send_sem=relay_sem.at[0],
            recv_sem=down_sem.at[0, lax.rem(source, lags // 2)],
            device_id=place(tiles - 1, end_lag),
            device_id_type=MESH,
        )

    def down_weights(source):
        return pltpu.make_async_remote_copy(
            src_ref=wsend_ref.at[pl.ds(groups - HALO, HALO)],
            dst_ref=wdown_ref.at[source],
            send_sem=relay_sem.at[2],
            recv_sem=down_sem.at[1, lax.rem(source, lags // 2)],
            device_id=place(tiles - 1, end_lag),
            device_id_type=MESH,
        )

    def down_forward(source, worker):
        return pltpu.make_async_remote_copy(
            src_ref=down_ref.at[source, worker],
            dst_ref=cells_ref.at[pl.ds(0, HALO), source],
            send_sem=onward_sem.at[0, lax.rem(source, lags // 2)],
            recv_sem=recv_sem.at[1],
            device_id=place(seam, first + worker),
            device_id_type=MESH,
        )

    def down_forward_weights(source):
        return pltpu.make_async_remote_copy(
            src_ref=wdown_ref.at[source],
            dst_ref=wcells_ref.at[pl.ds(0, HALO)],
            send_sem=onward_sem.at[1, lax.rem(source, lags // 2)],
            recv_sem=wrecv_sem.at[0],
            device_id=place(seam, source),
            device_id_type=MESH,
        )

    @pl.when(is_lower)
    def _():
        down_copy(lag).start()

    @pl.when(is_upper)
    def _():
        up_copy().start()

    for step in range(WORKERS):
        worker = order(step)

        @pl.when(worker != mine)
        def _():
            cell_copy(0, worker, lag).start()

    def arrived(kind):
        block = cells_ref.at[
            pl.ds((HALO, 0, HALO + groups)[kind], groups if kind == 0 else HALO)
        ]
        return pltpu.make_async_copy(block, block, recv_sem.at[min(kind, 1)])

    def gram_copies(worker, source):
        where = place(tile, first + worker)
        return (
            pltpu.make_async_remote_copy(
                src_ref=gsend_ref.at[worker],
                dst_ref=gram_ref.at[source],
                send_sem=gsend_sem.at[worker],
                recv_sem=grecv_sem.at[source],
                device_id=where,
                device_id_type=MESH,
            ),
            pltpu.make_async_remote_copy(
                src_ref=rsend_ref.at[worker],
                dst_ref=rhs_ref.at[source],
                send_sem=rsend_sem.at[worker],
                recv_sem=rrecv_sem.at[source],
                device_id=where,
                device_id_type=MESH,
            ),
        )

    @pl.when(jnp.logical_and(is_worker, jnp.logical_not(sums_early)))
    def _():
        weight_sums()

    @pl.when(jnp.logical_not(is_worker))
    def _():
        for load in loads[1:6]:
            load.wait()

    @pl.when(is_worker)
    def _():
        @pl.when(near_below)
        def _():
            weight_copy(1).start()

        @pl.when(near_above)
        def _():
            weight_copy(2).start()

        @pl.when(is_lower)
        def _():
            down_weights(lag).start()

        @pl.when(is_upper)
        def _():
            up_weights().start()

        pltpu.make_async_copy(
            send_ref.at[mine], cells_ref.at[pl.ds(HALO, groups), lag], recv_sem.at[0]
        ).start()

        @pl.when(tile == 0)
        def _():
            cells_ref[0:HALO] = jnp.zeros((HALO, lags, share, cols), bf16)
            wcells_ref[0:HALO] = jnp.zeros((HALO, 8, cols), f32)

        @pl.when(tile == tiles - 1)
        def _():
            cells_ref[HALO + groups :] = jnp.zeros((HALO, lags, share, cols), bf16)
            wcells_ref[HALO + groups :] = jnp.zeros((HALO, 8, cols), f32)

    @pl.when(is_last)
    def _():
        up_copy().wait_recv()
        for step in range(WORKERS):
            up_forward(order(step)).start()

        @pl.when(is_worker)
        def _():
            up_weights().wait_recv()
            up_forward_weights().start()

    def sends_weights(source):
        return jnp.logical_and(source >= first, source < first + WORKERS)

    @pl.when(is_end)
    def _():
        @pl.loop(0, middle)
        def _(n):
            source = end_base + n
            down_copy(source).wait_recv()
            for worker in range(WORKERS):
                down_forward(source, worker).start()

        @pl.loop(0, middle)
        def _(n):
            source = end_base + n

            @pl.when(sends_weights(source))
            def _():
                down_weights(source).wait_recv()
                down_forward_weights(source).start()

    row_major = lax.broadcasted_iota(jnp.int32, (share * rows, share * rows), 0)
    member_major = lax.broadcasted_iota(jnp.int32, (share * rows, share * rows), 1)
    wanted = lax.rem(row_major, share) * rows + row_major // share
    turn_ref[...] = jnp.where(member_major == wanted, 1.0, 0.0).astype(bf16)

    @pl.loop(0, rows)
    def _(r):
        out_ref[r] = jnp.zeros((members, cols), bf16)

    loads[6].wait()

    def lift(m, total):
        for n in range(8):
            total = total + hist_ref[8 * m + n].astype(f32)
        return total

    mean = lax.fori_loop(0, members // 8, lift, jnp.zeros((rows, cols), f32)) / members
    mean_ref[...] = mean

    @pl.loop(0, members // 8)
    def _(m):
        for n in range(8):
            hist_ref[8 * m + n] = (hist_ref[8 * m + n].astype(f32) - mean).astype(bf16)

    @pl.loop(0, members // (2 * share))
    def _(g):
        first = hist_ref[pl.ds(2 * share * g, share)].reshape(share * rows, cols)
        second = hist_ref[pl.ds(2 * share * g + share, share)].reshape(share * rows, cols)
        pair = jnp.concatenate([first, second], axis=1)
        turned = jnp.dot(turn_ref[...], pair, preferred_element_type=f32)
        turned = turned.reshape(rows, share, 2 * cols)
        turned = jnp.concatenate([turned[:, :, :cols], turned[:, :, cols:]], axis=1)
        start = pl.multiple_of(2 * share * g, 2 * share)
        turned_ref[:, pl.ds(start, 2 * share), :] = turned.astype(bf16)


    @pl.when(is_worker)
    def _():
        sub = lax.broadcasted_iota(jnp.int32, (patch_cols, cols), 0)
        lane = lax.broadcasted_iota(jnp.int32, (patch_cols, cols), 1)
        col_offset = (lane - PATCH * sub).astype(f32) - 7.5
        col_square = col_offset * col_offset
        squares = []
        for a in range(2):
            radius = jnp.zeros((patch_cols, cols), f32)
            for b in range(patch_cols):
                value = radius_ref[a * patch_cols + b].astype(f32)
                radius = jnp.where(sub == b, value, radius)
            squares.append(radius * radius)

        acc_ref[...] = jnp.zeros_like(acc_ref)
        accw_ref[...] = jnp.zeros_like(accw_ref)
        half = patch_cols // 2

        def accumulate(begin, count):
            wides, anomalies, scales, weighteds = [], [], [], []
            for n in range(count):
                j = begin + n
                values = cells_ref[j].astype(f32).reshape(members, cols)
                average = jnp.sum(values, axis=0, keepdims=True) / members
                anomaly = (values - average).astype(bf16)
                anomalies.append(anomaly)
                wides.append(anomaly.astype(f32))
                table = wcells_ref[j]
                innovation = table[1:2] - table[2:3] * average
                for a in range(2):
                    row_offset = (WORKERS * j - PATCH * a - 24 + mine).astype(f32) - 7.5
                    taper = 1.0 - (row_offset * row_offset + col_square) / squares[a]
                    taper = jnp.maximum(0.0, taper)
                    taper = taper * taper
                    both = taper[:half] + taper[half:]
                    scales.append(both * table[0:1])
                    weighteds.append(taper * innovation)
            left = jnp.concatenate(anomalies, axis=1)
            for b in range(half):
                near = lane[:1] < PATCH * b + 40
                near, far = (
                    jnp.where(near, 1.0, 0.0).astype(bf16),
                    jnp.where(near, 0.0, 1.0).astype(bf16),
                )
                rights = []
                for n in range(count):
                    column = []
                    for a in range(2):
                        scaled = (wides[n] * scales[2 * n + a][b : b + 1]).astype(bf16)
                        column += [scaled * near, scaled * far]
                    rights.append(jnp.concatenate(column, axis=0))
                right = jnp.concatenate(rights, axis=1)
                acc_ref[b] += lax.dot_general(left, right, NT, preferred_element_type=f32)
            side_left = jnp.concatenate(
                [
                    jnp.concatenate(weighteds[2 * n : 2 * n + 2], axis=0).astype(bf16)
                    for n in range(count)
                ],
                axis=1,
            )
            accw_ref[...] += lax.dot_general(side_left, left, NT, preferred_element_type=f32)

        arrived(0).wait()

        @pl.when(near_below)
        def _():
            halo_copy(1).start()

        @pl.when(near_above)
        def _():
            halo_copy(2).start()

        @pl.loop(0, 2)
        def _(n):
            accumulate(HALO + n * (groups // 2), groups // 2)

        @pl.loop(0, 2)
        def _(turn):
            side = jnp.where(tile < tiles // 2, turn, 1 - turn)

            @pl.when(jnp.logical_and(side == 0, near_above))
            def _():
                halo_copy(1).wait_recv()

            @pl.when(jnp.logical_and(side == 0, is_upper))
            def _():
                arrived(1).wait()

            @pl.when(jnp.logical_and(side == 0, has_above))
            def _():
                weight_copy(1).wait_recv()

            @pl.when(jnp.logical_and(side == 1, near_below))
            def _():
                halo_copy(2).wait_recv()

            @pl.when(jnp.logical_and(side == 1, is_lower))
            def _():
                arrived(2).wait()

            @pl.when(jnp.logical_and(side == 1, has_below))
            def _():
                weight_copy(2).wait_recv()

            accumulate(side * (HALO + groups), HALO)

        for worker in range(WORKERS):
            for a in range(2):
                lanes = slice(2 * a * members, 2 * (a + 1) * members)
                gsend_ref[worker, a] = acc_ref[worker, :, lanes].astype(bf16)
                q = a * patch_cols + worker
                rsend_ref[worker, a : a + 1] = jnp.concatenate(
                    [accw_ref[q : q + 1], accw_ref[q + half : q + half + 1]], axis=1
                )

        for worker in range(WORKERS):

            @pl.when(worker != mine)
            def _():
                for copy in gram_copies(worker, mine):
                    copy.start()

        gram_ref[mine] = gsend_ref[mine]
        rhs_ref[mine] = rsend_ref[mine]

    def transform_copy(target_lag, worker):
        return pltpu.make_async_remote_copy(
            src_ref=tsend_ref,
            dst_ref=trans_ref.at[worker],
            send_sem=tsend_sem.at[target_lag],
            recv_sem=trecv_sem.at[worker],
            device_id=place(tile, target_lag),
            device_id_type=MESH,
        )

    @pl.when(is_worker)
    def _():
        for source in range(WORKERS):

            @pl.when(source != mine)
            def _():
                for copy in gram_copies(0, source):
                    copy.wait_recv()

        row = lax.broadcasted_iota(jnp.int32, (members, 2 * members), 0)
        column = lax.broadcasted_iota(jnp.int32, (members, 2 * members), 1)
        identity = (row == lax.rem(column, members)).astype(f32)
        is_low = column[:1] < members
        low = jnp.where(is_low, 1.0, 0.0).astype(bf16)
        high = jnp.where(is_low, 0.0, 1.0).astype(bf16)

        def pick(values):
            return jnp.where(is_low, values[0], values[1])

        def lane_sums(x):
            return [
                jnp.sum(x[:, n * members : (n + 1) * members], axis=1, keepdims=True)
                for n in range(2)
            ]

        iterates, roots, bounds, rights_ = [], [], [], []
        for a in range(2):
            gram = gram_ref[0, a].astype(f32)
            rhs = rhs_ref[0, a : a + 1]
            for source in range(1, WORKERS):
                gram = gram + gram_ref[source, a].astype(f32)
                rhs = rhs + rhs_ref[source, a : a + 1]
            squares_ = lane_sums(jnp.sum(gram * gram, axis=0, keepdims=True))
            bound = members - 1.0 + jnp.sqrt(pick(squares_))
            bounds.append(bound)
            rights_.append(rhs)
            iterates.append((gram + (members - 1.0) * identity) / bound)
        roots = [1.5 * identity - 0.5 * iterate for iterate in iterates]
        iterates = [product(y, root, low, high) for y, root in zip(iterates, roots)]
        for sweep in range(1, NS_STEPS):
            corrections = [
                1.5 * identity - 0.5 * product(root, y, low, high)
                for root, y in zip(roots, iterates)
            ]
            if sweep < NS_STEPS - 1:
                iterates = [product(y, c, low, high) for y, c in zip(iterates, corrections)]
            roots = [product(c, root, low, high) for c, root in zip(corrections, roots)]
        for a in range(2):
            root, bound = roots[a], bounds[a]
            inner = pick(lane_sums(root * rights_[a]))
            weights = jnp.sum(root * inner, axis=0, keepdims=True) / bound
            factor = jnp.sqrt(jnp.full_like(bound, members - 1.0)) / jnp.sqrt(bound)
            tsend_ref[a] = (factor * root + weights).astype(bf16)

        for target in (0, lags - 1, 1, lags - 2, 2, lags - 3, 3, lags - 4):

            @pl.when(target != lag)
            def _():
                transform_copy(target, mine).start()

        trans_ref[mine] = tsend_ref[...]

    lane_patch = lax.broadcasted_iota(jnp.int32, (members, cols), 1) // PATCH
    half_rows = rows // 2

    @pl.loop(0, WORKERS)
    def _(step):
        near = jnp.where(is_worker, mine, jnp.where(lag < first, 0, WORKERS - 1))
        worker = jnp.where(
            is_worker, lax.rem(near + step, WORKERS), jnp.where(lag < first, step, near - step)
        )

        @pl.when(worker != mine)
        def _():
            transform_copy(lag, worker).wait_recv()

        mine_low = lane_patch == worker
        mine_high = lane_patch == worker + WORKERS
        mask = jnp.logical_or(mine_low, mine_high)
        low = jnp.where(mine_low[:1], 1.0, 0.0).astype(bf16)
        high = jnp.where(mine_high[:1], 1.0, 0.0).astype(bf16)
        for a in range(2):
            block = trans_ref[worker, a]

            @pl.loop(0, half_rows // 2, unroll=8)
            def _(i):
                rights = []
                for n in range(2):
                    state = turned_ref[a * half_rows + 2 * i + n]
                    rights.append(jnp.concatenate([state * low, state * high], axis=0))
                right = jnp.concatenate(rights, axis=1)
                mixed = jnp.dot(block, right, preferred_element_type=f32)
                for n in range(2):
                    r = a * half_rows + 2 * i + n
                    value = mixed[:, n * cols : (n + 1) * cols] + mean_ref[pl.ds(r, 1), :]
                    out_ref[r] = jnp.where(mask, value.astype(bf16), out_ref[r])

    @pl.when(is_lower)
    def _():
        down_copy(lag).wait_send()

        @pl.when(is_worker)
        def _():
            down_weights(lag).wait_send()

    @pl.when(is_upper)
    def _():
        up_copy().wait_send()

        @pl.when(is_worker)
        def _():
            up_weights().wait_send()

    @pl.when(is_last)
    def _():
        pltpu.make_async_copy(relay_ref, relay_ref, forward_sem.at[0]).wait()

        @pl.when(is_worker)
        def _():
            up_forward_weights().wait_send()

    @pl.when(is_end)
    def _():
        @pl.loop(0, middle)
        def _(n):
            source = end_base + n
            pltpu.make_async_copy(
                down_ref.at[source], down_ref.at[source], onward_sem.at[0, n]
            ).wait()

            @pl.when(sends_weights(source))
            def _():
                down_forward_weights(source).wait_send()

    for worker in range(WORKERS):

        @pl.when(worker != mine)
        def _():
            cell_copy(0, worker, lag).wait_send()

    @pl.when(is_worker)
    def _():
        @pl.when(near_above)
        def _():
            weight_copy(2).wait_send()
            halo_copy(2).wait_send()

        @pl.when(near_below)
        def _():
            weight_copy(1).wait_send()
            halo_copy(1).wait_send()

        for worker in range(WORKERS):

            @pl.when(worker != mine)
            def _():
                for copy in gram_copies(worker, mine):
                    copy.wait_send()

        for target in range(lags):

            @pl.when(target != lag)
            def _():
                transform_copy(target, mine).wait_send()


def solution(mesh):
    tiles, lags = mesh.shape["dom"], mesh.shape["lag"]

    def shards(history, forecast, spot, alive, heat, spread, radius):
        share, rows, cols = forecast.shape
        members = share * lags
        groups = rows // WORKERS
        window = groups + 2 * HALO
        f32, bf16, dma = jnp.float32, jnp.bfloat16, pltpu.SemaphoreType.DMA
        result = pl.pallas_call(
            functools.partial(kernel, tiles, lags),
            out_shape=jax.ShapeDtypeStruct((rows, members, cols), history.dtype),
            in_specs=[pl.BlockSpec(memory_space=pltpu.HBM)] * 7,
            out_specs=pl.BlockSpec(memory_space=pltpu.VMEM),
            scratch_shapes=[
                pltpu.VMEM(forecast.shape, bf16),
                pltpu.VMEM(spot.shape, jnp.int32),
                pltpu.VMEM(heat.shape, f32),
                pltpu.VMEM(spread.shape, f32),
                pltpu.SMEM(alive.shape, jnp.int32),
                pltpu.SMEM(radius.shape, jnp.int32),
                pltpu.VMEM((members, rows, cols), bf16),
                pltpu.VMEM((share * rows, share * rows), bf16),
                pltpu.VMEM((rows, cols), f32),
                pltpu.VMEM((rows, members, cols), bf16),
                pltpu.VMEM((share * rows, cols), f32),
                pltpu.VMEM((WORKERS, groups, share, cols), bf16),
                pltpu.VMEM((window, lags, share, cols), bf16),
                pltpu.VMEM((8 * rows, cols), f32),
                pltpu.VMEM((groups, 8, cols), f32),
                pltpu.VMEM((window, 8, cols), f32),
                pltpu.VMEM((WORKERS, members, 4 * members), f32),
                pltpu.VMEM((2 * WORKERS * 2, members), f32),
                pltpu.VMEM((WORKERS, 2, members, 2 * members), bf16),
                pltpu.VMEM((WORKERS, 2, members, 2 * members), bf16),
                pltpu.VMEM((WORKERS, 2, 2 * members), f32),
                pltpu.VMEM((WORKERS, 2, 2 * members), f32),
                pltpu.VMEM((2, members, 2 * members), bf16),
                pltpu.VMEM((WORKERS, 2, members, 2 * members), bf16),
                pltpu.VMEM((WORKERS, HALO, share, cols), bf16),
                pltpu.VMEM((HALO, 8, cols), f32),
                pltpu.VMEM((lags, WORKERS, HALO, share, cols), bf16),
                pltpu.VMEM((lags, HALO, 8, cols), f32),
                dma((7,)),
                dma((WORKERS,)),
                dma((2,)),
                dma((2,)),
                dma((2,)),
                dma((WORKERS,)),
                dma((WORKERS,)),
                dma((WORKERS,)),
                dma((WORKERS,)),
                dma((lags,)),
                dma((WORKERS,)),
                dma((2,)),
                dma((2,)),
                dma((4,)),
                dma((2,)),
                dma((2, lags // 2)),
                dma((2, lags // 2)),
            ],
            compiler_params=pltpu.CompilerParams(
                collective_id=0, has_side_effects=True, vmem_limit_bytes=16 << 20
            ),
            name="smoother",
        )(
            *(
                pltpu.with_memory_space_constraint(x, pltpu.HBM)
                for x in (forecast, spot, heat, spread, alive, radius, history)
            )
        )
        return jnp.transpose(result, (1, 0, 2))[None]

    in_specs = (
        P("lag", None, "dom", None),
        P("lag", "dom", None),
        P("dom", None),
        P("dom"),
        P("dom", None),
        P("dom", None),
        P("dom"),
    )
    out_specs = P("lag", None, "dom", None)
    return jax.shard_map(shards, mesh=mesh, in_specs=in_specs, out_specs=out_specs, check_vma=False)
```
